32 devices in a mesh: gx: 4 (over z), gy: 2 (over y), gz: 4 (over x, core).
Axes of the slice: x: 2, y: 2, z: 4, core: 2. Of those that a mesh axis runs over, the one named last changes fastest.
Arguments:
- features: bfloat16 [32, 16, 8, 512], P(None, 'gx', 'gy', 'gz'), may hold values from -6 to 6
- cotangent: bfloat16 [32, 16, 8, 512], P(None, 'gx', 'gy', 'gz'), may hold values from -6 to 6
- w_fine_in: bfloat16 [27, 32, 32], replicated, may hold values from -0.21875 to 0.21875
- w_coarse_in: bfloat16 [27, 32, 128], replicated, may hold values from -0.21875 to 0.21875
- w_coarse_mid: bfloat16 [27, 128, 128], replicated, may hold values from -0.109375 to 0.109375
- w_lift: bfloat16 [128, 32], replicated, may hold values from -0.5 to 0.5
- w_fine_out: bfloat16 [27, 32, 32], replicated, may hold values from -0.21875 to 0.21875
Outputs:
- output: bfloat16 [32, 16, 8, 512], P(None, 'gx', 'gy', 'gz')
- grad_input: bfloat16 [32, 16, 8, 512], P(None, 'gx', 'gy', 'gz')
- grad_fine_in: float32 [27, 32, 32], P(None, 'gx', ('gy', 'gz'))
- grad_coarse_in: float32 [27, 32, 128], P(None, 'gx', ('gy', 'gz'))
- grad_coarse_mid: float32 [27, 128, 128], P(None, 'gx', ('gy', 'gz'))
- grad_lift: float32 [128, 32], P('gx', ('gy', 'gz'))
- grad_fine_out: float32 [27, 32, 32], P(None, 'gx', ('gy', 'gz'))
The draws below stay inside these ranges and needn't reach their ends.
All inputs are finite; a program needn't handle non-finite values.
Results may differ from the reference program's by a relative error of at most 0.02.
Values may be sent and summed in bfloat16 or wider, within the bound.
A program may use at most 128 MiB of HBM per device.

```python
import math
import jax
import jax.numpy as jnp
from jax import lax

C = 32
CC = 128
NX = 16
NY = 8
NZ = 512


def levels(rng, dims, shards, least, top_value):
    loudness = 1.0
    for axis_at, shards_of in shards:
        heights = jax.random.uniform(jax.random.fold_in(jax.random.fold_in(rng, 6), axis_at), (shards_of,), jnp.float32, least / len(shards), top_value / len(shards))
        loudness = loudness * jnp.repeat(jnp.exp(heights), dims[axis_at] // shards_of).reshape((-1,) + (1,) * (len(dims) - 1 - axis_at))
    return loudness


def scatter_about(rng, shape, scale, reach, pieces=(), kind=jnp.bfloat16):
    values = jax.random.normal(rng, shape, jnp.float32) * scale
    if len(pieces) > 0:
        values = levels(rng, shape, pieces, -0.22, 0.18) * values
    return jnp.clip(values, min=-reach, max=reach).astype(kind)


def setup_inputs(seed: int = 0) -> dict:
    key_of = jax.random.split(jax.random.key(seed), 8)
    return {
        "features": scatter_about(key_of[0], (C, NX, NY, NZ), 1.0, 6.0, ((1, 4), (2, 2), (3, 4))),
        "cotangent": scatter_about(key_of[1], (C, NX, NY, NZ), 1.0, 6.0, ((1, 4), (2, 2), (3, 4))),
        "w_fine_in": scatter_about(key_of[2], (27, C, C), (27 * C) ** -0.5, 0.21875),
        "w_coarse_in": scatter_about(key_of[3], (27, C, CC), (27 * C) ** -0.5, 0.21875),
        "w_coarse_mid": scatter_about(key_of[4], (27, CC, CC), (27 * CC) ** -0.5, 0.109375),
        "w_lift": scatter_about(key_of[5], (CC, C), CC ** -0.5, 0.5),
        "w_fine_out": scatter_about(key_of[6], (27, C, C), (27 * C) ** -0.5, 0.21875),
    }


def conv_full(field, weight):
    cin = weight.shape[1]
    cout = weight.shape[2]
    kernel = weight.astype(jnp.float32).reshape(3, 3, 3, cin, cout).transpose(4, 3, 0, 1, 2)
    result = lax.conv_general_dilated(field.astype(jnp.float32)[None], kernel, (1, 1, 1), [(1, 1), (1, 1), (1, 1)], dimension_numbers=('NCDHW', 'OIDHW', 'NCDHW'), precision=lax.Precision.HIGHEST)
    return result[0]

def conv_back(grad, weight):
    return conv_full(grad, jnp.flip(weight, 0).transpose(0, 2, 1))

def weight_grad(field, grad):
    cin = field.shape[0]
    cout = grad.shape[0]
    depth, height, length = (field.shape[1], field.shape[2], field.shape[3])
    padded = jnp.pad(field.astype(jnp.float32), ((0, 0), (1, 1), (1, 1), (1, 1)))
    flat_grad = grad.astype(jnp.float32).reshape(cout, -1)
    blocks = []
    for tap in range(27):
        shift_x, shift_y, shift_z = (tap // 9, tap // 3 % 3, tap % 3)
        window = padded[:, shift_x:shift_x + depth, shift_y:shift_y + height, shift_z:shift_z + length].reshape(cin, -1)
        blocks.append(lax.dot_general(window, flat_grad, (((1,), (1,)), ((), ())), precision=lax.Precision.HIGHEST))
    return jnp.stack(blocks)

def pool_blocks(field):
    chans, depth, height, length = field.shape
    grouped = field.astype(jnp.float32).reshape(chans, depth // 4, 4, height // 4, 4, length // 4, 4)
    return grouped.sum(axis=(2, 4, 6))

def spread_up(field):
    chans, depth, height, length = field.shape
    grown = jnp.broadcast_to(field[:, :, None, :, None, :, None], (chans, depth, 4, height, 4, length, 4))
    return grown.reshape(chans, depth * 4, height * 4, length * 4)

def silu_slope(values):
    sigma = jax.nn.sigmoid(values)
    return sigma * (1.0 + values * (1.0 - sigma))

def reference(features, cotangent, w_fine_in, w_coarse_in, w_coarse_mid, w_lift, w_fine_out):
    scale = 1.0 / math.sqrt(NX * NY * NZ)
    z_first = conv_full(features, w_fine_in)
    act_first = jax.nn.silu(z_first).astype(jnp.bfloat16)
    pooled = (pool_blocks(act_first) / 64.0).astype(jnp.bfloat16)
    z_second = conv_full(pooled, w_coarse_in)
    act_second = jax.nn.silu(z_second).astype(jnp.bfloat16)
    z_third = conv_full(act_second, w_coarse_mid)
    act_third = jax.nn.silu(z_third).astype(jnp.bfloat16)
    lift_f = w_lift.astype(jnp.float32)
    third_f = act_third.astype(jnp.float32)
    lifted = jnp.tensordot(lift_f, third_f, axes=((0,), (0,)), precision=lax.Precision.HIGHEST)
    joined = (act_first.astype(jnp.float32) + spread_up(lifted)).astype(jnp.bfloat16)
    output = conv_full(joined, w_fine_out).astype(jnp.bfloat16)
    grad_fine_out = weight_grad(joined, cotangent) * scale
    d_joined = conv_back(cotangent, w_fine_out)
    d_lift = pool_blocks(d_joined)
    grad_lift = jnp.tensordot(third_f, d_lift, axes=((1, 2, 3), (1, 2, 3)), precision=lax.Precision.HIGHEST) * scale
    d_third = jnp.tensordot(lift_f, d_lift, axes=((1,), (0,)), precision=lax.Precision.HIGHEST)
    dz_third = (d_third * silu_slope(z_third)).astype(jnp.bfloat16)
    grad_coarse_mid = weight_grad(act_second, dz_third) * scale
    dz_second = (conv_back(dz_third, w_coarse_mid) * silu_slope(z_second)).astype(jnp.bfloat16)
    grad_coarse_in = weight_grad(pooled, dz_second) * scale
    d_pool = conv_back(dz_second, w_coarse_in)
    dz_first = ((d_joined + spread_up(d_pool) / 64.0) * silu_slope(z_first)).astype(jnp.bfloat16)
    grad_fine_in = weight_grad(features, dz_first) * scale
    grad_input = conv_back(dz_first, w_fine_in).astype(jnp.bfloat16)
    return (output, grad_input, grad_fine_in, grad_coarse_in, grad_coarse_mid, grad_lift, grad_fine_out)
```

```python
import math

import jax
import jax.numpy as jnp
from jax import lax
from jax.experimental import pallas as pl
from jax.experimental.pallas import tpu as pltpu
from jax.sharding import PartitionSpec as P

AXES = ("gx", "gy", "gz")
MESH = pl.DeviceIdType.MESH
DIRECT = 64


def place(flat, counts):
    nx, ny, nz = counts
    return (flat // (ny * nz), (flat // nz) % ny, flat % nz)


def meet(counts, total, me):
    barrier = pltpu.get_barrier_semaphore()

    def greet(k, carry):
        pl.semaphore_signal(
            barrier, inc=1, device_id=place((me + k) % total, counts), device_id_type=MESH
        )
        return carry

    lax.fori_loop(1, total, greet, 0)
    pl.semaphore_wait(barrier, total - 1)


def spread_kernel(counts, each, x_ref, o_ref, local_sem, send_sem, recv_sem, during):
    total = counts[0] * counts[1] * counts[2]
    me = (lax.axis_index("gx") * counts[1] + lax.axis_index("gy")) * counts[2] + lax.axis_index(
        "gz"
    )
    def copy(k):
        peer = (me + k) % total
        return pltpu.make_async_remote_copy(
            src_ref=x_ref.at[peer] if each else x_ref,
            dst_ref=o_ref.at[me],
            send_sem=send_sem.at[k],
            recv_sem=recv_sem.at[k],
            device_id=place(peer, counts),
            device_id_type=MESH,
        )

    def begin(k, carry):
        copy(k).start()
        return carry

    def finish(k, carry):
        copy(k).wait()
        return carry

    lax.fori_loop(1, total, begin, 0)
    own = pltpu.make_async_copy(x_ref.at[me] if each else x_ref, o_ref.at[me], local_sem)
    own.start()
    during()
    own.wait()
    lax.fori_loop(1, total, finish, 0)


def gather_kernel(counts, x_ref, w_mid, w_in, o_ref, mid_back, in_back, *sems):
    wide, narrow = w_mid.shape[2], in_back.shape[2]

    def turn():
        def body(ab, carry):
            for c in range(3):
                rows = slice(c * wide, c * wide + wide)
                mid_back[ab, rows, :] = w_mid[8 - ab, (2 - c) * wide : (3 - c) * wide, :].T
                in_back[ab, rows, :] = w_in[8 - ab, (2 - c) * narrow : (3 - c) * narrow, :].T
            return carry

        lax.fori_loop(0, 9, body, 0)

    spread_kernel(counts, False, x_ref, o_ref, *sems, turn)


def sum_kernel(counts, scale, x_ref, o_ref, landed, *sems):
    spread_kernel(counts, True, x_ref, landed, *sems, lambda: None)
    o_ref[...] = landed[...].astype(jnp.float32).sum(0) * scale


def extended(cells, sides, width):
    for axis, dim in sides:
        count = lax.axis_size(axis)
        ends = count - 1
        head = lax.slice_in_dim(cells, 0, width, axis=dim)
        tail = lax.slice_in_dim(cells, cells.shape[dim] - width, cells.shape[dim], axis=dim)
        cells = jnp.concatenate(
            [
                lax.ppermute(tail, axis, [(i, (i + 1) % count) for i in range(ends)]),
                cells,
                lax.ppermute(head, axis, [((i + 1) % count, i) for i in range(ends)]),
            ],
            axis=dim,
        )
    return cells


def silu_slope(values):
    sigma = jax.nn.sigmoid(values)
    return sigma * (1.0 + values * (1.0 - sigma))


def conv_valid(padded, weight, form="NCDHW"):
    kernel = weight.reshape(3, 3, 3, weight.shape[1], weight.shape[2])
    result = lax.conv_general_dilated(
        padded[None],
        kernel,
        (1, 1, 1),
        "VALID",
        dimension_numbers=(form, "DHWIO", form),
        preferred_element_type=jnp.float32,
    )
    return result[0]


def flipped(weight):
    return jnp.flip(weight, 0).transpose(0, 2, 1)


def pool_blocks(field):
    chans, depth, height, length = field.shape
    grouped = field.astype(jnp.float32).reshape(
        chans, depth // 4, 4, height // 4, 4, length // 4, 4
    )
    return grouped.sum(axis=(2, 4, 6))


def spread_up(field):
    chans, depth, height, length = field.shape
    grown = jnp.broadcast_to(
        field[:, :, None, :, None, :, None], (chans, depth, 4, height, 4, length, 4)
    )
    return grown.reshape(chans, depth * 4, height * 4, length * 4)


def tap_grad_direct(padded, grad):
    depth = padded.shape[1] - 2
    height = padded.shape[2] - 2
    length = padded.shape[3] - 2
    flat_grad = grad.reshape(grad.shape[0], -1)
    blocks = []
    for tap in range(27):
        shift_x, shift_y, shift_z = (tap // 9, tap // 3 % 3, tap % 3)
        window = padded[
            :, shift_x : shift_x + depth, shift_y : shift_y + height, shift_z : shift_z + length
        ].reshape(padded.shape[0], -1)
        blocks.append(
            lax.dot_general(
                window, flat_grad, (((1,), (1,)), ((), ())), preferred_element_type=jnp.float32
            )
        )
    return jnp.stack(blocks)


def fine_rim(field):
    return extended(field, (("gx", 1), ("gy", 2), ("gz", 3)), 1)


def coarse_rim(field):
    return extended(field, (("gx", 1), ("gy", 2), ("gz", 3)), 1)


def reduce_grad(partial_value):
    first = lax.psum_scatter(partial_value, "gx", scatter_dimension=1, tiled=True)
    return lax.psum_scatter(first, ("gy", "gz"), scatter_dimension=2, tiled=True)


def input_share(field):
    parts = lax.all_to_all(field[None], "gx", split_axis=1, concat_axis=0, tiled=True)
    moved = jnp.moveaxis(parts, 0, 1)
    moved = moved.reshape(moved.shape[0], -1, moved.shape[3], moved.shape[4])
    moved = lax.all_gather(moved, "gy", axis=2, tiled=True)
    return lax.all_gather(moved, "gz", axis=3, tiled=True)


def output_share(field):
    parts = lax.all_to_all(field[None], ("gy", "gz"), split_axis=1, concat_axis=0, tiled=True)
    count_y = lax.axis_size("gy")
    count_z = lax.axis_size("gz")
    chans = parts.shape[1]
    depth, height, length = (parts.shape[2], parts.shape[3], parts.shape[4])
    grid = parts.reshape(count_y, count_z, chans, depth, height, length).transpose(2, 3, 0, 4, 1, 5)
    grid = grid.reshape(chans, depth, count_y * height, count_z * length)
    return lax.all_gather(grid, "gx", axis=1, tiled=True)


def shards_layered(features, cotangent, w_fine_in, w_coarse_in, w_coarse_mid, w_lift, w_fine_out):
    depth, height, length = (features.shape[1], features.shape[2], features.shape[3])
    whole_cells = (
        depth * lax.axis_size("gx") * height * lax.axis_size("gy") * length * lax.axis_size("gz")
    )
    scale = 1.0 / math.sqrt(whole_cells)
    padded_in = fine_rim(features)
    z_first = conv_valid(padded_in, w_fine_in)
    act_first = jax.nn.silu(z_first).astype(jnp.bfloat16)
    pooled = (pool_blocks(act_first) / 64.0).astype(jnp.bfloat16)
    pooled_pad = coarse_rim(pooled)
    z_second = conv_valid(pooled_pad, w_coarse_in)
    act_second = jax.nn.silu(z_second).astype(jnp.bfloat16)
    second_pad = coarse_rim(act_second)
    z_third = conv_valid(second_pad, w_coarse_mid)
    act_third = jax.nn.silu(z_third).astype(jnp.bfloat16)
    lifted = lax.dot_general(
        w_lift, act_third, (((0,), (0,)), ((), ())), preferred_element_type=jnp.float32
    )
    joined = (act_first.astype(jnp.float32) + spread_up(lifted)).astype(jnp.bfloat16)
    padded_joined = fine_rim(joined)
    output = conv_valid(padded_joined, w_fine_out).astype(jnp.bfloat16)
    part_fine_out = tap_grad_direct(padded_joined, cotangent) * scale
    d_joined = conv_valid(fine_rim(cotangent), flipped(w_fine_out))
    d_lift = pool_blocks(d_joined)
    lift_partial = (
        lax.dot_general(
            act_third.astype(jnp.float32),
            d_lift,
            (((1, 2, 3), (1, 2, 3)), ((), ())),
            precision=lax.Precision.HIGHEST,
        )
        * scale
    )
    d_third = lax.dot_general(
        w_lift.astype(jnp.float32),
        d_lift,
        (((1,), (0,)), ((), ())),
        precision=lax.Precision.HIGHEST,
    )
    dz_third = (d_third * silu_slope(z_third)).astype(jnp.bfloat16)
    dz_third_pad = coarse_rim(dz_third)
    grad_coarse_mid = None
    sources = input_share(act_second)
    sources_pad = jnp.pad(sources, ((0, 0), (1, 1), (1, 1), (1, 1)))
    targets = output_share(dz_third)
    grad_coarse_mid = tap_grad_direct(sources_pad, targets) * scale
    dz_second = (conv_valid(dz_third_pad, flipped(w_coarse_mid)) * silu_slope(z_second)).astype(
        jnp.bfloat16
    )
    dz_second_pad = coarse_rim(dz_second)
    part_coarse_in = tap_grad_direct(pooled_pad, dz_second) * scale
    d_pool = conv_valid(dz_second_pad, flipped(w_coarse_in))
    dz_first = ((d_joined + spread_up(d_pool) / 64.0) * silu_slope(z_first)).astype(jnp.bfloat16)
    part_fine_in = tap_grad_direct(padded_in, dz_first) * scale
    grad_input = conv_valid(fine_rim(dz_first), flipped(w_fine_in)).astype(jnp.bfloat16)
    pending = [part_fine_out, lift_partial[None], part_coarse_in, part_fine_in]
    reduced = [reduce_grad(partial_value) for partial_value in pending]
    grad_fine_out = reduced[0]
    grad_lift = reduced[1][0]
    grad_coarse_in = reduced[2]
    grad_fine_in = reduced[3]
    return (
        output,
        grad_input,
        grad_fine_in,
        grad_coarse_in,
        grad_coarse_mid,
        grad_lift,
        grad_fine_out,
    )


def halo_kernel(counts, x_ref, o_ref, rows, packed, from_low, from_high, sends, recvs):
    nx, ny, nz = counts
    gx, gy, gz = (lax.axis_index(axis) for axis in AXES)
    sides = [(i, j, 0) for i in (-1, 0, 1) for j in (-1, 0, 1) if (i, j) != (0, 0)]
    sides += [(0, 0, -1), (0, 0, 1)]

    def there(side, sign):
        x, y, z = gx + sign * side[0], gy + sign * side[1], gz + sign * side[2]
        real = (x >= 0) & (x < nx) & (y >= 0) & (y < ny) & (z >= 0) & (z < nz)
        return (x, y, z), real

    d, h = x_ref.shape[:2]
    take = {-1: lambda n: pl.ds(0, 2), 0: lambda n: pl.ds(0, n), 1: lambda n: pl.ds(n - 2, 2)}
    land = {-1: lambda n: pl.ds(n + 2, 2), 0: lambda n: pl.ds(2, n), 1: lambda n: pl.ds(0, 2)}

    def transfer(k, side):
        if k < 8:
            source = x_ref.at[take[side[0]](d), take[side[1]](h)]
            target = rows.at[land[side[0]](d), land[side[1]](h)]
        else:
            source, target = packed, (from_high if side[2] < 0 else from_low)
        return pltpu.make_async_remote_copy(
            src_ref=source,
            dst_ref=target,
            send_sem=sends.at[k],
            recv_sem=recvs.at[k],
            device_id=there(side, 1)[0],
            device_id_type=MESH,
        )

    def run(first, last):
        for k in range(first, last):

            @pl.when(there(sides[k], 1)[1])
            def _():
                transfer(k, sides[k]).start()

    def settle(first, last):
        for k in range(first, last):

            @pl.when(there(sides[k], -1)[1])
            def _():
                transfer(k, sides[k]).wait_recv()

            @pl.when(there(sides[k], 1)[1])
            def _():
                transfer(k, sides[k]).wait_send()

    run(0, 8)
    settle(0, 8)
    rows[2 : 2 + d, 2 : 2 + h] = x_ref[...]
    lane = lax.broadcasted_iota(jnp.int32, (x_ref.shape[2], 128), 1)
    spots = [(x, y) for x in range(d + 4) for y in range(h + 4)]
    for part in range(2):
        group = jnp.zeros(lane.shape, jnp.float32)
        for r in range(32):
            x, y = spots[part * 32 + r]
            turned = pltpu.roll(rows[x, y].astype(jnp.float32), (2 + 4 * r) % 128, 1)
            group = jnp.where(lane // 4 == r, turned, group)
        packed[:, part * 128 : part * 128 + 128] = group.astype(jnp.bfloat16)
    run(8, 10)
    for x, y in spots:
        o_ref[x, y, :, 0:128] = rows[x, y]
    settle(8, 10)
    for part in range(2):
        span = slice(part * 128, part * 128 + 128)
        group = jnp.where(
            lane % 4 >= 2,
            from_high[:, span].astype(jnp.float32),
            from_low[:, span].astype(jnp.float32),
        )
        for r in range(32):
            x, y = spots[part * 32 + r]
            o_ref[x, y, :, 128:256] = pltpu.roll(group, 126 - 4 * r if r < 32 else 0, 1).astype(
                jnp.bfloat16
            )


def vmem(count):
    return [pl.BlockSpec(memory_space=pltpu.VMEM)] * count


ROOMY = 60 * 1024 * 1024


def stacked(value):
    size = value.shape[1]
    return jnp.concatenate(
        [pltpu.roll(value, 1, 1), value, pltpu.roll(value, size - 1, 1)]
    ).astype(jnp.bfloat16)


def around(ref, x, y, rows, lanes):
    return jnp.concatenate(
        [ref[x + a, y + b, rows, lanes] for a in range(3) for b in range(3)]
    )


def dot(a, b):
    return jnp.dot(a, b, preferred_element_type=jnp.float32)


def dot_over(a, b, dims, precision=None):
    return lax.dot_general(
        a, b, ((dims[:1], dims[1:]), ((), ())), precision=precision, preferred_element_type=jnp.float32
    )


def ahead(weight):
    return weight[...].reshape(27 * weight.shape[1], weight.shape[2]).T


def back(weight):
    return jnp.concatenate([weight[26 - t] for t in range(27)], axis=1)


def grouped(count, size, body):
    def several(g, carry):
        for i in range(size):
            body(g * size + i, carry)
        return carry

    lax.fori_loop(0, count // size, several, 0)


def fine_kernel(ext, w_in, w_out, z_ref, d_ref, mine, taps, total, ws):
    ws[0], ws[1] = ahead(w_in), back(w_out)

    def fill(r, carry):
        x, y = r // 8, r % 8
        for f in range(2):
            value = ext[x, y, f * 32 : f * 32 + 32, :].astype(jnp.float32)
            taps[x, y, f * 96 : f * 96 + 96, :] = stacked(value)
        return carry

    grouped(64, 4, fill)
    total[...] = jnp.zeros_like(total)

    def body(r, carry):
        x, y = r // 6, r % 6
        z = dot(ws[0], around(taps, x, y, slice(0, 96), slice(None)))
        d = dot(ws[1], around(taps, x, y, slice(96, 192), slice(None)))
        z_ref[x, y] = z
        d_ref[x, y] = d
        act = jax.nn.silu(z[:, :128]).astype(jnp.bfloat16).astype(jnp.float32)
        own = jnp.where((x >= 1) & (x <= 4) & (y >= 1) & (y <= 4), 1.0, 0.0)
        total[...] += own * jnp.concatenate([act, d[:, :128]])
        return carry

    grouped(36, 6, body)
    row = lax.broadcasted_iota(jnp.int32, (32, 128), 0)
    lane = lax.broadcasted_iota(jnp.int32, (32, 128), 1)
    pick = jnp.where(lane // 4 == row, 1.0, 0.0)
    sums = dot_over(pick, total[...], (1, 1), lax.Precision.HIGHEST)
    both = jnp.concatenate([sums[:, :32] * (1.0 / 64.0), sums[:, 32:]], axis=1)
    mine[...] = jnp.concatenate([both[:16], both[16:]], axis=1).astype(jnp.bfloat16)


def coarse_kernel(
    counts, scale, full, w_in, w_mid, w_lift, w_mid_back, w_in_back,
    grown, g_mid, g_in, g_lift,
    pad_in, pad_mid, pad_smid, pad_sin, table,
):
    nx, ny, nz = counts
    cells = nx * ny * 128
    gx, gy, gz = (lax.axis_index(axis) for axis in AXES)
    for pad in (pad_in, pad_mid, pad_smid, pad_sin):
        pad[...] = jnp.zeros_like(pad)

    def pick(size, parts, index):
        each = size // parts
        row = lax.broadcasted_iota(jnp.int32, (size, each), 0)
        column = lax.broadcasted_iota(jnp.int32, (size, each), 1)
        return jnp.where(row == index * each + column, 1.0, 0.0).astype(jnp.bfloat16)

    at_o = gy * nz + gz
    pick_mid, pick_in = pick(128, nx, gx), pick(32, nx, gx)
    pick_o, pick_lift = pick(128, ny * nz, at_o), pick(32, ny * nz, at_o)

    def fill(pad, value):
        at = lax.broadcasted_iota(jnp.int32, value.shape, 0) % 128
        low = jnp.where(at == 0, 0.0, pltpu.roll(value, 1, 0))
        high = jnp.where(at == 127, 0.0, pltpu.roll(value, cells - 1, 0))
        wide = jnp.concatenate([low, value, high], axis=1).astype(jnp.bfloat16)
        pad[1 : nx + 1, 1 : ny + 1] = wide.reshape(nx, ny, 128, wide.shape[1])

    def window(pad, ab):
        a, b = ab // 3, ab % 3
        return pad[a : a + nx, b : b + ny].reshape(cells, pad.shape[3])

    def conv(pad, weight):
        result = dot(window(pad, 0), weight[0])
        for ab in range(1, 9):
            result = result + dot(window(pad, ab), weight[ab])
        return result

    def slope(v):
        sigma = jax.nn.sigmoid(v)
        return sigma * (1.0 + v * (1.0 - sigma))

    pieces = []
    for k in range(nx * ny):
        for z in range(nz):
            block = full[k * nz + z]
            pieces += [block[:, :64], block[:, 64:]]
    both = jnp.concatenate(pieces)
    pooled, d_lift = both[:, :32], both[:, 32:]
    fill(pad_in, pooled.astype(jnp.float32))
    z_second = conv(pad_in, w_in)
    act_second = jax.nn.silu(z_second)
    fill(pad_mid, act_second)
    z_third = conv(pad_mid, w_mid)
    act_third = jax.nn.silu(z_third).astype(jnp.bfloat16)
    lifted = dot(act_third, w_lift[...])
    dz_third = (dot_over(d_lift, w_lift[...], (1, 1)) * slope(z_third)).astype(jnp.bfloat16)
    fill(pad_mid, dz_third.astype(jnp.float32))
    dz_second = (conv(pad_mid, w_mid_back) * slope(z_second)).astype(jnp.bfloat16)
    fill(pad_mid, dz_second.astype(jnp.float32))
    d_pool = conv(pad_mid, w_in_back)

    table[...] = (
        jnp.concatenate([lifted, d_pool * (1.0 / 64.0)], axis=1)
        .astype(jnp.bfloat16)
        .reshape(nx, ny, 128, 64)
    )
    row = lax.broadcasted_iota(jnp.int32, (128, 256), 0)
    lane = lax.broadcasted_iota(jnp.int32, (128, 256), 1)
    cell = jnp.where(lane < 192, lane // 4, -1) + gz * 32
    grow = jnp.where(row == cell, 1.0, 0.0).astype(jnp.bfloat16)
    for i in range(3):
        for j in range(3):
            x = jnp.clip(gx + i - 1, 0, nx - 1)
            y = jnp.clip(gy + j - 1, 0, ny - 1)
            grown[i, j] = dot_over(table[x, y], grow, (0, 0))

    third_o = dot(dz_third, pick_o).T.astype(jnp.bfloat16)
    second_o = dot(dz_second, pick_o).T.astype(jnp.bfloat16)
    fill(pad_smid, dot(act_second.astype(jnp.bfloat16), pick_mid))
    fill(pad_sin, dot(pooled, pick_in))
    for ab in range(9):
        g_mid[ab] = dot(third_o, window(pad_smid, ab)) * scale
        g_in[ab] = dot(second_o, window(pad_sin, ab)) * scale
    third_i = dot(act_third, pick_mid).astype(jnp.bfloat16)
    lift_o = dot(d_lift, pick_lift).T.astype(jnp.bfloat16)
    g_lift[...] = dot(lift_o, third_i) * scale


def last_kernel(
    counts, ext, z_ref, d_ref, grown, w_out, w_in, out, g_input, parts, tj, td, tf, sums, ws
):
    ws[0], ws[1] = ahead(w_out), back(w_in)
    nx, ny, nz = counts
    gx, gy, gz = (lax.axis_index(axis) for axis in AXES)
    lane = lax.broadcasted_iota(jnp.int32, (32, 256), 1)
    at_z = gz * 128 + jnp.where(lane < 192, lane, lane - 256)
    keep_z = jnp.where((at_z >= 0) & (at_z < nz * 128), 1.0, 0.0)

    def fill(r, carry):
        x, y = r // 6, r % 6
        at_x, at_y = gx * 4 + x - 1, gy * 4 + y - 1
        real = (at_x >= 0) & (at_x < nx * 4) & (at_y >= 0) & (at_y < ny * 4)
        keep = keep_z * jnp.where(real, 1.0, 0.0)
        up = grown[(x + 3) // 4, (y + 3) // 4]
        z = z_ref[x, y]
        sigma = jax.nn.sigmoid(z)
        act = (z * sigma).astype(jnp.bfloat16).astype(jnp.float32)
        joined = (act + up[:32]).astype(jnp.bfloat16).astype(jnp.float32) * keep
        dz = (d_ref[x, y] + up[32:]) * (sigma * (1.0 + z * (1.0 - sigma))) * keep
        dz = dz.astype(jnp.bfloat16).astype(jnp.float32)
        tj[x, y] = stacked(joined)[:, :128]
        td[x, y] = stacked(dz)[:, :128]
        tf[x, y] = stacked(ext[x + 1, y + 1, 0:32, :].astype(jnp.float32))[:, :128]
        return carry

    grouped(36, 3, fill)
    sums[...] = jnp.zeros_like(sums)

    def body(r, carry):
        x, y = r // 2, (r % 2) * 2
        whole = slice(None)

        def pair(ref):
            return jnp.concatenate(
                [around(ref, x, y, whole, whole), around(ref, x, y + 1, whole, whole)], axis=1
            )

        near = pair(tj)
        result = dot(ws[0], near).astype(jnp.bfloat16)
        out[x, y], out[x, y + 1] = result[:, :128], result[:, 128:]
        cot = jnp.concatenate(
            [ext[x + 2, y + 2, 32:64, 0:128], ext[x + 2, y + 3, 32:64, 0:128]], axis=1
        )
        sums[0] += dot_over(near, cot, (1, 1))
        result = dot(ws[1], pair(td)).astype(jnp.bfloat16)
        g_input[x, y], g_input[x, y + 1] = result[:, :128], result[:, 128:]
        grad = jnp.concatenate(
            [td[x + 1, y + 1, 32:64, :], td[x + 1, y + 2, 32:64, :]], axis=1
        )
        sums[1] += dot_over(pair(tf), grad, (1, 1))
        return carry

    grouped(8, 2, body)
    ci, co = 32 // nx, 32 // (ny * nz)
    for f in range(2):
        value = sums[f].reshape(27, nx, ci, 32)
        for i in range(nx):
            block = value[:, i].reshape(27 * ci, 32).T
            for j in range(ny * nz):
                parts[i * ny * nz + j, f * co : f * co + co, 0 : 27 * ci] = block[
                    j * co : j * co + co
                ].astype(jnp.bfloat16)


def whole_kernel(
    counts, scale, x_ref, w_in, w_out, w_in9, w_mid9, w_lift,
    out, g_input, g_mid, g_in, g_lift, sums_out,
    ext, rows, packed, from_low, from_high, halo_sends, halo_recvs,
    z_ref, d_ref, mine, taps, total_ref, ws,
    full, mid_back, in_back, gather_local, gather_sends, gather_recvs,
    grown, pad_in, pad_mid, pad_smid, pad_sin, table,
    tj, td, tf, sums, parts, landed, sum_local, sum_sends, sum_recvs,
):
    total = counts[0] * counts[1] * counts[2]
    me = (lax.axis_index("gx") * counts[1] + lax.axis_index("gy")) * counts[2] + lax.axis_index(
        "gz"
    )
    for ref in (rows, from_low, from_high):
        ref[...] = jnp.zeros_like(ref)
    meet(counts, total, me)
    halo_kernel(counts, x_ref, ext, rows, packed, from_low, from_high, halo_sends, halo_recvs)
    fine_kernel(ext, w_in, w_out, z_ref, d_ref, mine, taps, total_ref, ws)
    gather_kernel(
        counts, mine, w_mid9, w_in9, full, mid_back, in_back,
        gather_local, gather_sends, gather_recvs,
    )
    coarse_kernel(
        counts, scale, full, w_in9, w_mid9, w_lift, mid_back, in_back,
        grown, g_mid, g_in, g_lift, pad_in, pad_mid, pad_smid, pad_sin, table,
    )
    last_kernel(
        counts, ext, z_ref, d_ref, grown, w_out, w_in, out, g_input, parts, tj, td, tf, sums, ws
    )
    sum_kernel(counts, scale, parts, sums_out, landed, sum_local, sum_sends, sum_recvs)


def shards(features, cotangent, w_fine_in, w_coarse_in, w_coarse_mid, w_lift, w_fine_out):
    counts = tuple(lax.axis_size(axis) for axis in AXES)
    nx, ny, nz = counts
    total = nx * ny * nz
    chans, depth, height, length = features.shape
    wide = w_lift.shape[0]
    scale = 1.0 / math.sqrt(total * depth * height * length)
    f32, bf16 = jnp.float32, jnp.bfloat16
    shape = jax.ShapeDtypeStruct
    rows = jnp.concatenate([features, cotangent]).transpose(1, 2, 0, 3)
    co, cw = wide // (ny * nz), wide // nx
    ci = chans // nx
    pads = [3 * chans, 3 * wide, 3 * cw, 3 * ci]
    block = (2 * chans // (ny * nz), 27 * ci)
    edge = pltpu.VMEM((2 * chans, 256), bf16)
    near = pltpu.VMEM((6, 6, 3 * chans, 128), bf16)
    field = pltpu.VMEM((6, 6, chans, 256), f32)
    one, many = pltpu.SemaphoreType.DMA, pltpu.SemaphoreType.DMA((total,))
    output, grad_input, g_mid, g_in, g_lift, sums = pl.pallas_call(
        lambda *refs: whole_kernel(counts, scale, *refs),
        out_shape=(
            shape((4, 4, chans, 128), bf16),
            shape((4, 4, chans, 128), bf16),
            shape((9, co, 3 * cw), f32),
            shape((9, co, 3 * ci), f32),
            shape((chans // (ny * nz), cw), f32),
            shape(block, f32),
        ),
        in_specs=vmem(6),
        out_specs=vmem(6),
        scratch_shapes=[
            pltpu.VMEM((8, 8, 2 * chans, 256), bf16),
            pltpu.VMEM((8, 8, 2 * chans, 128), bf16),
            edge, edge, edge,
            pltpu.SemaphoreType.DMA((10,)),
            pltpu.SemaphoreType.DMA((10,)),
            field, field,
            pltpu.VMEM((16, 128), bf16),
            pltpu.VMEM((8, 8, 192, 256), bf16),
            pltpu.VMEM((64, 128), f32),
            pltpu.VMEM((2, chans, 27 * chans), bf16),
            pltpu.VMEM((total, 16, 128), bf16),
            pltpu.VMEM((9, 3 * wide, wide), bf16),
            pltpu.VMEM((9, 3 * wide, chans), bf16),
            one, many, many,
            pltpu.VMEM((3, 3, 2 * chans, 256), f32),
        ]
        + [pltpu.VMEM((nx + 2, ny + 2, 128, k), bf16) for k in pads]
        + [
            pltpu.VMEM((nx, ny, 128, 2 * chans), bf16),
            near, near, near,
            pltpu.VMEM((2, 27 * chans, chans), f32),
            pltpu.VMEM((total,) + block, bf16),
            pltpu.VMEM((total,) + block, bf16),
            one, many, many,
        ],
        compiler_params=pltpu.CompilerParams(
            collective_id=0, has_side_effects=True, vmem_limit_bytes=ROOMY
        ),
        name="whole",
    )(
        rows, w_fine_in, w_fine_out,
        w_coarse_in.reshape(9, 3 * chans, wide), w_coarse_mid.reshape(9, 3 * wide, wide), w_lift,
    )
    sums = sums.reshape(2, -1, 27, ci).transpose(0, 2, 3, 1)

    def owned(grad):
        return grad.reshape(9, grad.shape[1], 3, -1).transpose(0, 2, 3, 1).reshape(
            27, -1, grad.shape[1]
        )

    return (
        output.transpose(2, 0, 1, 3),
        grad_input.transpose(2, 0, 1, 3),
        sums[1],
        owned(g_in),
        owned(g_mid),
        g_lift.T,
        sums[0],
    )


def choose(features, *rest):
    nx, ny, nz = (lax.axis_size(axis) for axis in AXES)
    total = nx * ny * nz
    wide = rest[4].shape[0]
    fits = features.shape == (32, 4, 4, 128) and nz == 4 and total <= DIRECT
    fits = fits and 32 % (ny * nz) == 0 and 32 % nx == 0 and 32 // nx == 8 and wide == 128
    return (shards if fits else shards_layered)(features, *rest)


def solution(mesh):
    whole = P(None, "gx", "gy", "gz")
    split = P(None, "gx", ("gy", "gz"))
    return jax.shard_map(
        choose,
        mesh=mesh,
        in_specs=(whole, whole, P(), P(), P(), P(), P()),
        out_specs=(whole, whole, split, split, split, P("gx", ("gy", "gz")), split),
        check_vma=False,
    )
```

```python
import math

import jax
import jax.numpy as jnp
from jax import lax
from jax.experimental import pallas as pl
from jax.experimental.pallas import tpu as pltpu
from jax.sharding import PartitionSpec as P

AXES = ("gx", "gy", "gz")
MESH = pl.DeviceIdType.MESH
DIRECT = 64


def place(flat, counts):
    nx, ny, nz = counts
    return (flat // (ny * nz), (flat // nz) % ny, flat % nz)


def extended(cells, sides, width):
    for axis, dim in sides:
        count = lax.axis_size(axis)
        ends = count - 1
        head = lax.slice_in_dim(cells, 0, width, axis=dim)
        tail = lax.slice_in_dim(cells, cells.shape[dim] - width, cells.shape[dim], axis=dim)
        cells = jnp.concatenate(
            [
                lax.ppermute(tail, axis, [(i, (i + 1) % count) for i in range(ends)]),
                cells,
                lax.ppermute(head, axis, [((i + 1) % count, i) for i in range(ends)]),
            ],
            axis=dim,
        )
    return cells


def silu_slope(values):
    sigma = jax.nn.sigmoid(values)
    return sigma * (1.0 + values * (1.0 - sigma))


def conv_valid(padded, weight, form="NCDHW"):
    kernel = weight.reshape(3, 3, 3, weight.shape[1], weight.shape[2])
    result = lax.conv_general_dilated(
        padded[None],
        kernel,
        (1, 1, 1),
        "VALID",
        dimension_numbers=(form, "DHWIO", form),
        preferred_element_type=jnp.float32,
    )
    return result[0]


def flipped(weight):
    return jnp.flip(weight, 0).transpose(0, 2, 1)


def pool_blocks(field):
    chans, depth, height, length = field.shape
    grouped = field.astype(jnp.float32).reshape(
        chans, depth // 4, 4, height // 4, 4, length // 4, 4
    )
    return grouped.sum(axis=(2, 4, 6))


def spread_up(field):
    chans, depth, height, length = field.shape
    grown = jnp.broadcast_to(
        field[:, :, None, :, None, :, None], (chans, depth, 4, height, 4, length, 4)
    )
    return grown.reshape(chans, depth * 4, height * 4, length * 4)


def tap_grad_direct(padded, grad):
    depth = padded.shape[1] - 2
    height = padded.shape[2] - 2
    length = padded.shape[3] - 2
    flat_grad = grad.reshape(grad.shape[0], -1)
    blocks = []
    for tap in range(27):
        shift_x, shift_y, shift_z = (tap // 9, tap // 3 % 3, tap % 3)
        window = padded[
            :, shift_x : shift_x + depth, shift_y : shift_y + height, shift_z : shift_z + length
        ].reshape(padded.shape[0], -1)
        blocks.append(
            lax.dot_general(
                window, flat_grad, (((1,), (1,)), ((), ())), preferred_element_type=jnp.float32
            )
        )
    return jnp.stack(blocks)


def fine_rim(field):
    return extended(field, (("gx", 1), ("gy", 2), ("gz", 3)), 1)


def coarse_rim(field):
    return extended(field, (("gx", 1), ("gy", 2), ("gz", 3)), 1)


def reduce_grad(partial_value):
    first = lax.psum_scatter(partial_value, "gx", scatter_dimension=1, tiled=True)
    return lax.psum_scatter(first, ("gy", "gz"), scatter_dimension=2, tiled=True)


def input_share(field):
    parts = lax.all_to_all(field[None], "gx", split_axis=1, concat_axis=0, tiled=True)
    moved = jnp.moveaxis(parts, 0, 1)
    moved = moved.reshape(moved.shape[0], -1, moved.shape[3], moved.shape[4])
    moved = lax.all_gather(moved, "gy", axis=2, tiled=True)
    return lax.all_gather(moved, "gz", axis=3, tiled=True)


def output_share(field):
    parts = lax.all_to_all(field[None], ("gy", "gz"), split_axis=1, concat_axis=0, tiled=True)
    count_y = lax.axis_size("gy")
    count_z = lax.axis_size("gz")
    chans = parts.shape[1]
    depth, height, length = (parts.shape[2], parts.shape[3], parts.shape[4])
    grid = parts.reshape(count_y, count_z, chans, depth, height, length).transpose(2, 3, 0, 4, 1, 5)
    grid = grid.reshape(chans, depth, count_y * height, count_z * length)
    return lax.all_gather(grid, "gx", axis=1, tiled=True)


def shards_layered(features, cotangent, w_fine_in, w_coarse_in, w_coarse_mid, w_lift, w_fine_out):
    depth, height, length = (features.shape[1], features.shape[2], features.shape[3])
    whole_cells = (
        depth * lax.axis_size("gx") * height * lax.axis_size("gy") * length * lax.axis_size("gz")
    )
    scale = 1.0 / math.sqrt(whole_cells)
    padded_in = fine_rim(features)
    z_first = conv_valid(padded_in, w_fine_in)
    act_first = jax.nn.silu(z_first).astype(jnp.bfloat16)
    pooled = (pool_blocks(act_first) / 64.0).astype(jnp.bfloat16)
    pooled_pad = coarse_rim(pooled)
    z_second = conv_valid(pooled_pad, w_coarse_in)
    act_second = jax.nn.silu(z_second).astype(jnp.bfloat16)
    second_pad = coarse_rim(act_second)
    z_third = conv_valid(second_pad, w_coarse_mid)
    act_third = jax.nn.silu(z_third).astype(jnp.bfloat16)
    lifted = lax.dot_general(
        w_lift, act_third, (((0,), (0,)), ((), ())), preferred_element_type=jnp.float32
    )
    joined = (act_first.astype(jnp.float32) + spread_up(lifted)).astype(jnp.bfloat16)
    padded_joined = fine_rim(joined)
    output = conv_valid(padded_joined, w_fine_out).astype(jnp.bfloat16)
    part_fine_out = tap_grad_direct(padded_joined, cotangent) * scale
    d_joined = conv_valid(fine_rim(cotangent), flipped(w_fine_out))
    d_lift = pool_blocks(d_joined)
    lift_partial = (
        lax.dot_general(
            act_third.astype(jnp.float32),
            d_lift,
            (((1, 2, 3), (1, 2, 3)), ((), ())),
            precision=lax.Precision.HIGHEST,
        )
        * scale
    )
    d_third = lax.dot_general(
        w_lift.astype(jnp.float32),
        d_lift,
        (((1,), (0,)), ((), ())),
        precision=lax.Precision.HIGHEST,
    )
    dz_third = (d_third * silu_slope(z_third)).astype(jnp.bfloat16)
    dz_third_pad = coarse_rim(dz_third)
    grad_coarse_mid = None
    sources = input_share(act_second)
    sources_pad = jnp.pad(sources, ((0, 0), (1, 1), (1, 1), (1, 1)))
    targets = output_share(dz_third)
    grad_coarse_mid = tap_grad_direct(sources_pad, targets) * scale
    dz_second = (conv_valid(dz_third_pad, flipped(w_coarse_mid)) * silu_slope(z_second)).astype(
        jnp.bfloat16
    )
    dz_second_pad = coarse_rim(dz_second)
    part_coarse_in = tap_grad_direct(pooled_pad, dz_second) * scale
    d_pool = conv_valid(dz_second_pad, flipped(w_coarse_in))
    dz_first = ((d_joined + spread_up(d_pool) / 64.0) * silu_slope(z_first)).astype(jnp.bfloat16)
    part_fine_in = tap_grad_direct(padded_in, dz_first) * scale
    grad_input = conv_valid(fine_rim(dz_first), flipped(w_fine_in)).astype(jnp.bfloat16)
    pending = [part_fine_out, lift_partial[None], part_coarse_in, part_fine_in]
    reduced = [reduce_grad(partial_value) for partial_value in pending]
    grad_fine_out = reduced[0]
    grad_lift = reduced[1][0]
    grad_coarse_in = reduced[2]
    grad_fine_in = reduced[3]
    return (
        output,
        grad_input,
        grad_fine_in,
        grad_coarse_in,
        grad_coarse_mid,
        grad_lift,
        grad_fine_out,
    )


SIDES = [(i, j, 0) for i in (-1, 0, 1) for j in (-1, 0, 1) if (i, j) != (0, 0)]
SIDES += [(i, j, k) for i in (-1, 0, 1) for j in (-1, 0, 1) for k in (-1, 1)]
ROOMY = 60 * 1024 * 1024


def vmem(count):
    return [pl.BlockSpec(memory_space=pltpu.VMEM)] * count


def slot(i, j, k):
    return ((i + 1) * 3 + j + 1) * 2 + (1 if k > 0 else 0)


def there(counts, side, sign):
    place_of = [lax.axis_index(axis) + sign * step for axis, step in zip(AXES, side)]
    real = True
    for at, count, step in zip(place_of, counts, side):
        if step != 0:
            real = real & (at >= 0) & (at < count)
    return tuple(place_of), real


def swap_copy(counts, n, rows, packed, got, sends, recvs):
    i, j, k = SIDES[n]
    take = {-1: pl.ds(1, 1), 0: pl.ds(1, 4), 1: pl.ds(4, 1)}
    land = {-1: pl.ds(5, 1), 0: pl.ds(1, 4), 1: pl.ds(0, 1)}
    if k == 0:
        source, target = rows.at[take[i], take[j]], rows.at[land[i], land[j]]
    else:
        source, target = packed, got.at[slot(-i, -j, -k)]
    return pltpu.make_async_remote_copy(
        src_ref=source,
        dst_ref=target,
        send_sem=sends.at[n],
        recv_sem=recvs.at[n],
        device_id=there(counts, SIDES[n], 1)[0],
        device_id_type=MESH,
    )


def swap_start(counts, *refs):
    for n in range(len(SIDES)):

        @pl.when(there(counts, SIDES[n], 1)[1])
        def _():
            swap_copy(counts, n, *refs).start()


def swap_finish(counts, *refs):
    for n in range(len(SIDES)):

        @pl.when(there(counts, SIDES[n], -1)[1])
        def _():
            swap_copy(counts, n, *refs).wait_recv()

        @pl.when(there(counts, SIDES[n], 1)[1])
        def _():
            swap_copy(counts, n, *refs).wait_send()


def spot(x, y):
    return (x + 1) * 6 + y + 1


def lanes_of(rows, width=128):
    return lax.broadcasted_iota(jnp.int32, (rows, width), 1)


def clear_rim(rows, got):
    rows[0] = jnp.zeros(rows.shape[1:], rows.dtype)
    rows[5] = jnp.zeros(rows.shape[1:], rows.dtype)
    for x in range(1, 5):
        rows[x, 0] = jnp.zeros(rows.shape[2:], rows.dtype)
        rows[x, 5] = jnp.zeros(rows.shape[2:], rows.dtype)
    got[...] = jnp.zeros_like(got)


def edges(values, x, y, group):
    lane = lanes_of(32)
    place_of = spot(x, y)
    for f, value in enumerate(values):
        turned = pltpu.roll(value, (2 * place_of + 1 + 64 * f) % 128, 1)
        group = jnp.where(lane // 2 == place_of + 32 * f, turned, group)
    return group


def columns(got, f):
    lane = lanes_of(32)
    low = lane % 2 == 1
    at_x, at_y = lane // 12, lane // 2 % 6
    result = jnp.zeros((32, 128), jnp.float32)
    for i in (-1, 0, 1):
        for j in (-1, 0, 1):
            mine = (lane < 72) & (at_x == 0 if i < 0 else at_x == 5 if i > 0 else (at_x > 0) & (at_x < 5))
            mine = mine & (at_y == 0 if j < 0 else at_y == 5 if j > 0 else (at_y > 0) & (at_y < 5))
            for k in (-1, 1):
                turn = (48 * i + 8 * j - 64 * f - k) % 128
                block = pltpu.roll(got[slot(i, j, k)].astype(jnp.float32), turn, 1)
                result = jnp.where(mine & (low if k < 0 else ~low), block, result)
    return result


def column_window(value):
    return jnp.concatenate(
        [
            pltpu.roll(value, (-12 * (a - 1) - 2 * (b - 1)) % 128, 1)
            for a in range(3)
            for b in range(3)
        ]
    ).astype(jnp.bfloat16)


def dot(a, b):
    return jnp.dot(a, b, preferred_element_type=jnp.float32)


def dot_over(a, b, dims, precision=None):
    return lax.dot_general(
        a, b, ((dims[:1], dims[1:]), ((), ())), precision=precision, preferred_element_type=jnp.float32
    )


def ahead(weight):
    size = weight.shape[1]
    taps = weight[...].reshape(9, 3, size, weight.shape[2])
    return jnp.concatenate([taps[:, c].reshape(9 * size, weight.shape[2]).T for c in range(3)])


def back(weight):
    return jnp.concatenate(
        [
            jnp.concatenate([weight[26 - 3 * ab - c] for ab in range(9)], axis=1)
            for c in range(3)
        ]
    )


def near(ref, x, chans):
    return jnp.concatenate(
        [
            jnp.concatenate([ref[x + a, y + b, chans, :] for y in range(4)], axis=1)
            for a in range(3)
            for b in range(3)
        ]
    )


def settle(taps, rim, x):
    lane = lanes_of(32)
    rows = []
    for y in range(4):
        part = taps[:, y * 128 : y * 128 + 128]
        edge = pltpu.roll(rim, (127 - 2 * spot(x, y)) % 128, 1)
        low = jnp.where(lane == 0, edge, pltpu.roll(part[:32], 1, 1))
        high = jnp.where(lane == 127, edge, pltpu.roll(part[64:], 127, 1))
        rows.append(low + part[32:64] + high)
    return rows


def rim_of(weight, window):
    taps = dot(weight, window)
    return jnp.where(lanes_of(32) % 2 == 1, taps[:32], taps[64:])


def thrice(value):
    lane = lax.broadcasted_iota(jnp.int32, value.shape, 1) % 128
    size = value.shape[1]
    value = value.astype(jnp.float32)
    parts = []
    for at in range(0, size, 128):
        part = value[:, at : at + 128]
        spare = lane[:, :128]
        parts.append(
            jnp.concatenate(
                [
                    jnp.where(spare == 127, 0.0, pltpu.roll(part, 127, 1)),
                    part,
                    jnp.where(spare == 0, 0.0, pltpu.roll(part, 1, 1)),
                ]
            )
        )
    return jnp.concatenate(parts, axis=1).astype(jnp.bfloat16)


def thrice_rim(edge):
    low = lanes_of(32) % 2 == 1
    return jnp.concatenate(
        [jnp.where(low, edge, 0.0), jnp.zeros_like(edge), jnp.where(low, 0.0, edge)]
    ).astype(jnp.bfloat16)


def silu_parts(z):
    sigma = jax.nn.sigmoid(z)
    act = (z * sigma).astype(jnp.bfloat16).astype(jnp.float32)
    return act, sigma * (1.0 + z * (1.0 - sigma))


def spread(value, chooser):
    high = value.astype(jnp.bfloat16)
    rest = value - high.astype(jnp.float32)
    middle = rest.astype(jnp.bfloat16)
    low = (rest - middle.astype(jnp.float32)).astype(jnp.bfloat16)
    count = value.shape[0]
    chosen = dot(jnp.concatenate([high, middle, low]), chooser)
    return chosen[:count] + chosen[count : 2 * count] + chosen[2 * count :]


def chooser_of(blocks, step, inner):
    row = lax.broadcasted_iota(jnp.int32, (27 * blocks, 128 * blocks), 0)
    lane = lax.broadcasted_iota(jnp.int32, (27 * blocks, 128 * blocks), 1)
    tap = lane % 128
    ab, c = tap // 3, tap % 3
    source = ab * step + c * inner + lane // 128
    return jnp.where((row == source) & (tap < 27), 1.0, 0.0).astype(jnp.bfloat16)


def whole_kernel(
    counts, scale, fea, cot, w_in, w_out, w_in9, w_mid9, w_lift,
    out, g_input, g_fine_in, g_in, g_mid, g_lift, g_fine_out,
    one, two, got_one, got_two, pack_one, pack_two, sends_one, recvs_one, sends_two, recvs_two,
    tmp, ws, near_rim, rim_sums, total_ref, mine, full, mid_back, in_back, weight_sems,
    w9, wm9, gather_local, gather_sends, gather_recvs,
    grown, grown_rim, pad_in, pad_mid, pad_smid, pad_sin, table, thirds,
    jd, dz_edges, sums, parts, landed, sum_local, sum_sends, sum_recvs,
):
    nx, ny, nz = counts
    total = nx * ny * nz
    gx, gy, gz = (lax.axis_index(axis) for axis in AXES)
    me = (gx * ny + gy) * nz + gz
    f32, bf16 = jnp.float32, jnp.bfloat16
    fetches = [
        pltpu.make_async_copy(w_in9, w9, weight_sems.at[0]),
        pltpu.make_async_copy(w_mid9, wm9, weight_sems.at[1]),
    ]
    for fetch in fetches:
        fetch.start()
    clear_rim(one, got_one)
    clear_rim(two, got_two)
    barrier = pltpu.get_barrier_semaphore()

    def greet(k, carry):
        pl.semaphore_signal(
            barrier, inc=1, device_id=place((me + k) % total, counts), device_id_type=MESH
        )
        return carry

    lax.fori_loop(1, total, greet, 0)

    group = jnp.zeros((32, 128), f32)
    for x in range(4):
        tmp[0] = fea[:, x].astype(f32).reshape(128, 128)
        tmp[1] = cot[:, x].astype(f32).reshape(128, 128)
        for y in range(4):
            values = [tmp[f, pl.ds(y, 32, stride=4), :] for f in range(2)]
            one[x + 1, y + 1] = jnp.concatenate(values).astype(bf16)
            group = edges(values, x, y, group)
    pack_one[...] = group.astype(bf16)
    ws[0], ws[1], ws[2], ws[3] = ahead(w_in), back(w_out), ahead(w_out), back(w_in)
    pl.semaphore_wait(barrier, total - 1)
    first = (counts, one, pack_one, got_one, sends_one, recvs_one)
    swap_start(*first)
    swap_finish(*first)

    for f in range(2):
        window = column_window(columns(got_one, f))
        if f == 0:
            near_rim[0] = window
        rim_sums[f] = rim_of(ws[f], window)
    total_ref[...] = jnp.zeros_like(total_ref)
    pack_two[...] = jnp.zeros_like(pack_two)

    def fine(x, carry):
        z = settle(dot(ws[0], near(one, x, slice(0, 32))), rim_sums[0], x)
        d = settle(dot(ws[1], near(one, x, slice(32, 64))), rim_sums[1], x)
        group = pack_two[...].astype(f32)
        acts = jnp.zeros((32, 128), f32)
        for y in range(4):
            two[x + 1, y + 1] = jnp.concatenate([z[y], d[y]]).astype(bf16)
            group = edges([z[y], d[y]], x, y, group)
            acts = acts + silu_parts(z[y])[0]
        pack_two[...] = group.astype(bf16)
        total_ref[...] += jnp.concatenate([acts, d[0] + d[1] + d[2] + d[3]])
        return carry

    lax.fori_loop(0, 4, fine, 0)
    row = lax.broadcasted_iota(jnp.int32, (32, 128), 0)
    pick_cell = jnp.where(lanes_of(32) // 4 == row, 1.0, 0.0)
    means = dot_over(pick_cell, total_ref[...], (1, 1), lax.Precision.HIGHEST)
    both = jnp.concatenate([means[:, :32] * (1.0 / 64.0), means[:, 32:]], axis=1)
    mine[...] = jnp.concatenate([both[:16], both[16:]], axis=1).astype(bf16)

    def spread_copy(k, source, target, local_sems):
        peer = (me + k) % total
        return pltpu.make_async_remote_copy(
            src_ref=source(peer),
            dst_ref=target.at[me],
            send_sem=local_sems[0].at[k],
            recv_sem=local_sems[1].at[k],
            device_id=place(peer, counts),
            device_id_type=MESH,
        )

    def gather_copy(k):
        return spread_copy(k, lambda peer: mine, full, (gather_sends, gather_recvs))

    def sum_copy(k):
        return spread_copy(k, lambda peer: parts.at[peer], landed, (sum_sends, sum_recvs))

    def each_peer(act):
        def step(k, carry):
            act(k)
            return carry

        lax.fori_loop(1, total, step, 0)

    each_peer(lambda k: gather_copy(k).start())
    own = pltpu.make_async_copy(mine, full.at[me], gather_local)
    own.start()
    second = (counts, two, pack_two, got_two, sends_two, recvs_two)
    swap_start(*second)

    for fetch in fetches:
        fetch.wait()
    wide, narrow = w9.shape[2], in_back.shape[2]

    def turn(ab, carry):
        for c in range(3):
            rows = slice(c * wide, c * wide + wide)
            mid_back[ab, rows, :] = wm9[8 - ab, (2 - c) * wide : (3 - c) * wide, :].T
            in_back[ab, rows, :] = w9[8 - ab, (2 - c) * narrow : (3 - c) * narrow, :].T
        return carry

    lax.fori_loop(0, 9, turn, 0)
    for pad in (pad_in, pad_mid, pad_smid, pad_sin):
        pad[...] = jnp.zeros_like(pad)
    own.wait()
    each_peer(lambda k: gather_copy(k).wait())

    cells = nx * ny * 128

    def pick(size, pieces, index):
        each = size // pieces
        row = lax.broadcasted_iota(jnp.int32, (size, each), 0)
        column = lax.broadcasted_iota(jnp.int32, (size, each), 1)
        return jnp.where(row == index * each + column, 1.0, 0.0).astype(bf16)

    at_o = gy * nz + gz
    pick_mid, pick_in = pick(128, nx, gx), pick(32, nx, gx)
    pick_o, pick_lift = pick(128, ny * nz, at_o), pick(32, ny * nz, at_o)

    def fill(pad, value):
        at = lax.broadcasted_iota(jnp.int32, value.shape, 0) % 128
        low = jnp.where(at == 0, 0.0, pltpu.roll(value, 1, 0))
        high = jnp.where(at == 127, 0.0, pltpu.roll(value, cells - 1, 0))
        wide = jnp.concatenate([low, value, high], axis=1).astype(bf16)
        pad[1 : nx + 1, 1 : ny + 1] = wide.reshape(nx, ny, 128, wide.shape[1])

    def window(pad, ab):
        a, b = ab // 3, ab % 3
        return pad[a : a + nx, b : b + ny].reshape(cells, pad.shape[3])

    def conv(pad, weight):
        result = dot(window(pad, 0), weight[0])
        for ab in range(1, 9):
            result = result + dot(window(pad, ab), weight[ab])
        return result

    def slope(v):
        sigma = jax.nn.sigmoid(v)
        return sigma * (1.0 + v * (1.0 - sigma))

    pieces = []
    for k in range(nx * ny):
        for z in range(nz):
            block = full[k * nz + z]
            pieces += [block[:, :64], block[:, 64:]]
    both = jnp.concatenate(pieces)
    pooled, d_lift = both[:, :32], both[:, 32:]
    fill(pad_in, pooled.astype(f32))
    z_second = conv(pad_in, w9)
    act_second = jax.nn.silu(z_second)
    fill(pad_mid, act_second)
    z_third = conv(pad_mid, wm9)
    act_third = jax.nn.silu(z_third).astype(bf16)
    lifted = dot(act_third, w_lift[...].T)
    dz_third = (dot(d_lift, w_lift[...]) * slope(z_third)).astype(bf16)
    fill(pad_mid, dz_third.astype(f32))
    dz_second = (conv(pad_mid, mid_back) * slope(z_second)).astype(bf16)
    fill(pad_mid, dz_second.astype(f32))
    d_pool = conv(pad_mid, in_back)
    table[...] = (
        jnp.concatenate([lifted, d_pool * (1.0 / 64.0)], axis=1)
        .astype(bf16)
        .reshape(nx, ny, 128, 64)
    )
    thirds[0] = dot(dz_third, pick_o).T.astype(bf16)
    thirds[1] = dot(dz_second, pick_o).T.astype(bf16)
    fill(pad_smid, dot(act_second.astype(bf16), pick_mid))
    fill(pad_sin, dot(pooled, pick_in))
    third_i = dot(act_third, pick_mid).astype(bf16)
    lift_o = dot(d_lift, pick_lift).T.astype(bf16)
    g_lift[...] = dot(lift_o, third_i) * scale

    row = lax.broadcasted_iota(jnp.int32, (128, 128), 0)
    lane = lanes_of(128)
    grow = jnp.where(row == lane // 4 + gz * 32, 1.0, 0.0).astype(bf16)
    past = gz * 32 + jnp.where(lane % 2 == 1, -1, 32)
    at_x, at_y = lane // 12, lane // 2 % 6
    rim = jnp.zeros((64, 128), f32)
    for i in range(3):
        for j in range(3):
            x = jnp.clip(gx + i - 1, 0, nx - 1)
            y = jnp.clip(gy + j - 1, 0, ny - 1)
            grown[i, j] = dot_over(table[x, y], grow, (0, 0))
            mine_too = ((at_x + 3) // 4 == i) & ((at_y + 3) // 4 == j) & (lane < 72)
            far = jnp.where((row == past) & mine_too, 1.0, 0.0).astype(bf16)
            rim = rim + dot_over(table[x, y], far, (0, 0))
    swap_finish(*second)

    lane = lanes_of(32)
    at_x, at_y = gx * 4 + lane // 12 - 1, gy * 4 + lane // 2 % 6 - 1
    real = (at_x >= 0) & (at_x < nx * 4) & (at_y >= 0) & (at_y < ny * 4) & (lane < 72)
    reach = gz + jnp.where(lane % 2 == 1, -1, 1)
    real = real & (reach >= 0) & (reach < nz)
    act, bend = silu_parts(columns(got_two, 0))
    near_rim[1] = column_window(jnp.where(real, act + rim[:32], 0.0))
    near_rim[2] = column_window(jnp.where(real, (columns(got_two, 1) + rim[32:]) * bend, 0.0))
    rim_sums[0] = rim_of(ws[2], near_rim[1])
    rim_sums[1] = rim_of(ws[3], near_rim[2])
    dz_edges[...] = jnp.zeros_like(dz_edges)

    def join(r, carry):
        x, y = r // 6, r % 6
        at_x, at_y = gx * 4 + x - 1, gy * 4 + y - 1
        real = (at_x >= 0) & (at_x < nx * 4) & (at_y >= 0) & (at_y < ny * 4)
        keep = jnp.where(real, 1.0, 0.0)
        up = grown[(x + 3) // 4, (y + 3) // 4]
        both = two[x, y].astype(f32)
        act, bend = silu_parts(both[:32])
        joined = (act + up[:32]) * keep
        dz = (both[32:] + up[32:]) * bend * keep
        jd[x, y] = jnp.concatenate([joined, dz]).astype(bf16)
        here = jnp.where((x >= 1) & (x <= 4) & (y >= 1) & (y <= 4), r, -1)
        turned = pltpu.roll(dz, (2 * r + 1) % 128, 1)
        dz_edges[...] = jnp.where(lanes_of(32) // 2 == here, turned, dz_edges[...])
        return carry

    lax.fori_loop(0, 36, join, 0)
    ends = pltpu.roll(pack_one[...].astype(f32), 64, 1)
    ends = jnp.where(lanes_of(32) < 64, ends, 0.0)
    sums[0] = dot_over(near_rim[1], thrice_rim(ends), (1, 1))
    sums[1] = dot_over(near_rim[0], thrice_rim(dz_edges[...]), (1, 1))

    def last(x, carry):
        joined = near(jd, x, slice(0, 32))
        rows = settle(dot(ws[2], joined), rim_sums[0], x)
        for y in range(4):
            tmp[0, pl.ds(y, 32, stride=4), :] = rows[y]
        out[:, x] = tmp[0].reshape(32, 4, 128).astype(bf16)
        given = [one[x + 1, y + 1, 32:64, :] for y in range(4)]
        sums[0] += dot_over(joined, thrice(jnp.concatenate(given, axis=1)), (1, 1))
        rows = settle(dot(ws[3], near(jd, x, slice(32, 64))), rim_sums[1], x)
        for y in range(4):
            tmp[1, pl.ds(y, 32, stride=4), :] = rows[y]
        g_input[:, x] = tmp[1].reshape(32, 4, 128).astype(bf16)
        given = [jd[x + 1, y + 1, 32:64, :] for y in range(4)]
        sums[1] += dot_over(
            near(one, x, slice(0, 32)), thrice(jnp.concatenate(given, axis=1)), (1, 1)
        )
        return carry

    lax.fori_loop(0, 4, last, 0)
    ci, co = 32 // nx, 32 // (ny * nz)
    for f in range(2):
        value = sums[f].reshape(9, nx, ci, 96)
        for i in range(nx):
            turned = value[:, i].reshape(9 * ci, 96).T
            block = jnp.concatenate([turned[:32], turned[32:64], turned[64:]], axis=1)
            for j in range(ny * nz):
                parts[i * ny * nz + j, f * co : f * co + co, :] = block[
                    j * co : j * co + co
                ].astype(bf16)
    each_peer(lambda k: sum_copy(k).start())
    own = pltpu.make_async_copy(parts.at[me], landed.at[me], sum_local)
    own.start()

    taken = []
    for ab in range(9):
        grad = dot(thirds[0], window(pad_smid, ab)) * scale
        share = grad.shape[1] // 3
        for c in range(3):
            g_mid[3 * ab + c] = grad[:, c * share : c * share + share]
        taken.append(dot(thirds[1], window(pad_sin, ab)) * scale)
    chosen = spread(jnp.concatenate(taken, axis=1), chooser_of(ci, 3 * ci, ci))
    for i in range(ci):
        g_in[i] = chosen[:, i * 128 : i * 128 + 27]
    chooser = chooser_of(ci, ci, 9 * ci)
    own.wait()
    each_peer(lambda k: sum_copy(k).wait())
    chosen = spread(landed[...].astype(f32).sum(0) * scale, chooser)
    for i in range(ci):
        g_fine_out[i] = chosen[:co, i * 128 : i * 128 + 27]
        g_fine_in[i] = chosen[co:, i * 128 : i * 128 + 27]


def shards(features, cotangent, w_fine_in, w_coarse_in, w_coarse_mid, w_lift, w_fine_out):
    counts = tuple(lax.axis_size(axis) for axis in AXES)
    nx, ny, nz = counts
    total = nx * ny * nz
    chans, depth, height, length = features.shape
    wide = w_lift.shape[0]
    scale = 1.0 / math.sqrt(total * depth * height * length)
    f32, bf16 = jnp.float32, jnp.bfloat16
    shape = jax.ShapeDtypeStruct
    co, cw = wide // (ny * nz), wide // nx
    ci, fo = chans // nx, chans // (ny * nz)
    pads = [3 * chans, 3 * wide, 3 * cw, 3 * ci]
    block = (2 * fo, 27 * ci)
    rows = pltpu.VMEM((6, 6, 2 * chans, 128), bf16)
    got = pltpu.VMEM((18, chans, 128), bf16)
    packed = pltpu.VMEM((chans, 128), bf16)
    swaps = pltpu.SemaphoreType.DMA((len(SIDES),))
    one, many = pltpu.SemaphoreType.DMA, pltpu.SemaphoreType.DMA((total,))
    anywhere = pl.BlockSpec(memory_space=pl.ANY)
    output, grad_input, g_fine_in, g_in, g_mid, g_lift, g_fine_out = pl.pallas_call(
        lambda *refs: whole_kernel(counts, scale, *refs),
        out_shape=(
            shape(features.shape, bf16),
            shape(features.shape, bf16),
            shape((ci, fo, 27), f32),
            shape((ci, co, 27), f32),
            shape((27, co, cw), f32),
            shape((fo, cw), f32),
            shape((ci, fo, 27), f32),
        ),
        in_specs=vmem(4) + [anywhere] * 2 + vmem(1),
        out_specs=vmem(7),
        scratch_shapes=[
            rows, rows, got, got, packed, packed, swaps, swaps, swaps, swaps,
            pltpu.VMEM((2, 128, 128), f32),
            pltpu.VMEM((4, 3 * chans, 9 * chans), bf16),
            pltpu.VMEM((3, 9 * chans, 128), bf16),
            pltpu.VMEM((2, chans, 128), f32),
            pltpu.VMEM((2 * chans, 128), f32),
            pltpu.VMEM((16, 128), bf16),
            pltpu.VMEM((total, 16, 128), bf16),
            pltpu.VMEM((9, 3 * wide, wide), bf16),
            pltpu.VMEM((9, 3 * wide, chans), bf16),
            pltpu.SemaphoreType.DMA((2,)),
            pltpu.VMEM((9, 3 * chans, wide), bf16),
            pltpu.VMEM((9, 3 * wide, wide), bf16),
            one, many, many,
            pltpu.VMEM((3, 3, 2 * chans, 128), f32),
            pltpu.VMEM((2 * chans, 128), f32),
        ]
        + [pltpu.VMEM((nx + 2, ny + 2, 128, k), bf16) for k in pads]
        + [
            pltpu.VMEM((nx, ny, 128, 2 * chans), bf16),
            pltpu.VMEM((2, co, nx * ny * 128), bf16),
            rows,
            pltpu.VMEM((chans, 128), f32),
            pltpu.VMEM((2, 9 * chans, 3 * chans), f32),
            pltpu.VMEM((total,) + block, bf16),
            pltpu.VMEM((total,) + block, bf16),
            one, many, many,
        ],
        compiler_params=pltpu.CompilerParams(
            collective_id=0, has_side_effects=True, vmem_limit_bytes=ROOMY
        ),
        name="whole",
    )(
        features, cotangent, w_fine_in, w_fine_out,
        w_coarse_in.reshape(9, 3 * chans, wide), w_coarse_mid.reshape(9, 3 * wide, wide), w_lift.T,
    )
    return (
        output,
        grad_input,
        g_fine_in.transpose(2, 0, 1),
        g_in.transpose(2, 0, 1),
        g_mid.transpose(0, 2, 1),
        g_lift.T,
        g_fine_out.transpose(2, 0, 1),
    )


def choose(features, *rest):
    nx, ny, nz = (lax.axis_size(axis) for axis in AXES)
    total = nx * ny * nz
    wide = rest[4].shape[0]
    fits = features.shape == (32, 4, 4, 128) and nz == 4 and total <= DIRECT
    fits = fits and 32 % (ny * nz) == 0 and 32 % nx == 0 and 32 // nx == 8 and wide == 128
    return (shards if fits else shards_layered)(features, *rest)


def solution(mesh):
    whole = P(None, "gx", "gy", "gz")
    split = P(None, "gx", ("gy", "gz"))
    return jax.shard_map(
        choose,
        mesh=mesh,
        in_specs=(whole, whole, P(), P(), P(), P(), P()),
        out_specs=(whole, whole, split, split, split, P("gx", ("gy", "gz")), split),
        check_vma=False,
    )
```

```python
import math

import jax
import jax.numpy as jnp
from jax import lax
from jax.experimental import pallas as pl
from jax.experimental.pallas import tpu as pltpu
from jax.sharding import PartitionSpec as P

AXES = ("gx", "gy", "gz")
MESH = pl.DeviceIdType.MESH
DIRECT = 64


def place(flat, counts):
    nx, ny, nz = counts
    return (flat // (ny * nz), (flat // nz) % ny, flat % nz)


def extended(cells, sides, width):
    for axis, dim in sides:
        count = lax.axis_size(axis)
        ends = count - 1
        head = lax.slice_in_dim(cells, 0, width, axis=dim)
        tail = lax.slice_in_dim(cells, cells.shape[dim] - width, cells.shape[dim], axis=dim)
        cells = jnp.concatenate(
            [
                lax.ppermute(tail, axis, [(i, (i + 1) % count) for i in range(ends)]),
                cells,
                lax.ppermute(head, axis, [((i + 1) % count, i) for i in range(ends)]),
            ],
            axis=dim,
        )
    return cells


def silu_slope(values):
    sigma = jax.nn.sigmoid(values)
    return sigma * (1.0 + values * (1.0 - sigma))


def conv_valid(padded, weight, form="NCDHW"):
    kernel = weight.reshape(3, 3, 3, weight.shape[1], weight.shape[2])
    result = lax.conv_general_dilated(
        padded[None],
        kernel,
        (1, 1, 1),
        "VALID",
        dimension_numbers=(form, "DHWIO", form),
        preferred_element_type=jnp.float32,
    )
    return result[0]


def flipped(weight):
    return jnp.flip(weight, 0).transpose(0, 2, 1)


def pool_blocks(field):
    chans, depth, height, length = field.shape
    grouped = field.astype(jnp.float32).reshape(
        chans, depth // 4, 4, height // 4, 4, length // 4, 4
    )
    return grouped.sum(axis=(2, 4, 6))


def spread_up(field):
    chans, depth, height, length = field.shape
    grown = jnp.broadcast_to(
        field[:, :, None, :, None, :, None], (chans, depth, 4, height, 4, length, 4)
    )
    return grown.reshape(chans, depth * 4, height * 4, length * 4)


def tap_grad_direct(padded, grad):
    depth = padded.shape[1] - 2
    height = padded.shape[2] - 2
    length = padded.shape[3] - 2
    flat_grad = grad.reshape(grad.shape[0], -1)
    blocks = []
    for tap in range(27):
        shift_x, shift_y, shift_z = (tap // 9, tap // 3 % 3, tap % 3)
        window = padded[
            :, shift_x : shift_x + depth, shift_y : shift_y + height, shift_z : shift_z + length
        ].reshape(padded.shape[0], -1)
        blocks.append(
            lax.dot_general(
                window, flat_grad, (((1,), (1,)), ((), ())), preferred_element_type=jnp.float32
            )
        )
    return jnp.stack(blocks)


def fine_rim(field):
    return extended(field, (("gx", 1), ("gy", 2), ("gz", 3)), 1)


def coarse_rim(field):
    return extended(field, (("gx", 1), ("gy", 2), ("gz", 3)), 1)


def reduce_grad(partial_value):
    first = lax.psum_scatter(partial_value, "gx", scatter_dimension=1, tiled=True)
    return lax.psum_scatter(first, ("gy", "gz"), scatter_dimension=2, tiled=True)


def input_share(field):
    parts = lax.all_to_all(field[None], "gx", split_axis=1, concat_axis=0, tiled=True)
    moved = jnp.moveaxis(parts, 0, 1)
    moved = moved.reshape(moved.shape[0], -1, moved.shape[3], moved.shape[4])
    moved = lax.all_gather(moved, "gy", axis=2, tiled=True)
    return lax.all_gather(moved, "gz", axis=3, tiled=True)


def output_share(field):
    parts = lax.all_to_all(field[None], ("gy", "gz"), split_axis=1, concat_axis=0, tiled=True)
    count_y = lax.axis_size("gy")
    count_z = lax.axis_size("gz")
    chans = parts.shape[1]
    depth, height, length = (parts.shape[2], parts.shape[3], parts.shape[4])
    grid = parts.reshape(count_y, count_z, chans, depth, height, length).transpose(2, 3, 0, 4, 1, 5)
    grid = grid.reshape(chans, depth, count_y * height, count_z * length)
    return lax.all_gather(grid, "gx", axis=1, tiled=True)


def shards_layered(features, cotangent, w_fine_in, w_coarse_in, w_coarse_mid, w_lift, w_fine_out):
    depth, height, length = (features.shape[1], features.shape[2], features.shape[3])
    whole_cells = (
        depth * lax.axis_size("gx") * height * lax.axis_size("gy") * length * lax.axis_size("gz")
    )
    scale = 1.0 / math.sqrt(whole_cells)
    padded_in = fine_rim(features)
    z_first = conv_valid(padded_in, w_fine_in)
    act_first = jax.nn.silu(z_first).astype(jnp.bfloat16)
    pooled = (pool_blocks(act_first) / 64.0).astype(jnp.bfloat16)
    pooled_pad = coarse_rim(pooled)
    z_second = conv_valid(pooled_pad, w_coarse_in)
    act_second = jax.nn.silu(z_second).astype(jnp.bfloat16)
    second_pad = coarse_rim(act_second)
    z_third = conv_valid(second_pad, w_coarse_mid)
    act_third = jax.nn.silu(z_third).astype(jnp.bfloat16)
    lifted = lax.dot_general(
        w_lift, act_third, (((0,), (0,)), ((), ())), preferred_element_type=jnp.float32
    )
    joined = (act_first.astype(jnp.float32) + spread_up(lifted)).astype(jnp.bfloat16)
    padded_joined = fine_rim(joined)
    output = conv_valid(padded_joined, w_fine_out).astype(jnp.bfloat16)
    part_fine_out = tap_grad_direct(padded_joined, cotangent) * scale
    d_joined = conv_valid(fine_rim(cotangent), flipped(w_fine_out))
    d_lift = pool_blocks(d_joined)
    lift_partial = (
        lax.dot_general(
            act_third.astype(jnp.float32),
            d_lift,
            (((1, 2, 3), (1, 2, 3)), ((), ())),
            precision=lax.Precision.HIGHEST,
        )
        * scale
    )
    d_third = lax.dot_general(
        w_lift.astype(jnp.float32),
        d_lift,
        (((1,), (0,)), ((), ())),
        precision=lax.Precision.HIGHEST,
    )
    dz_third = (d_third * silu_slope(z_third)).astype(jnp.bfloat16)
    dz_third_pad = coarse_rim(dz_third)
    grad_coarse_mid = None
    sources = input_share(act_second)
    sources_pad = jnp.pad(sources, ((0, 0), (1, 1), (1, 1), (1, 1)))
    targets = output_share(dz_third)
    grad_coarse_mid = tap_grad_direct(sources_pad, targets) * scale
    dz_second = (conv_valid(dz_third_pad, flipped(w_coarse_mid)) * silu_slope(z_second)).astype(
        jnp.bfloat16
    )
    dz_second_pad = coarse_rim(dz_second)
    part_coarse_in = tap_grad_direct(pooled_pad, dz_second) * scale
    d_pool = conv_valid(dz_second_pad, flipped(w_coarse_in))
    dz_first = ((d_joined + spread_up(d_pool) / 64.0) * silu_slope(z_first)).astype(jnp.bfloat16)
    part_fine_in = tap_grad_direct(padded_in, dz_first) * scale
    grad_input = conv_valid(fine_rim(dz_first), flipped(w_fine_in)).astype(jnp.bfloat16)
    pending = [part_fine_out, lift_partial[None], part_coarse_in, part_fine_in]
    reduced = [reduce_grad(partial_value) for partial_value in pending]
    grad_fine_out = reduced[0]
    grad_lift = reduced[1][0]
    grad_coarse_in = reduced[2]
    grad_fine_in = reduced[3]
    return (
        output,
        grad_input,
        grad_fine_in,
        grad_coarse_in,
        grad_coarse_mid,
        grad_lift,
        grad_fine_out,
    )


SIDES = [(i, j, 0) for i in (-1, 0, 1) for j in (-1, 0, 1) if (i, j) != (0, 0)]
SIDES += [(i, j, k) for i in (-1, 0, 1) for j in (-1, 0, 1) for k in (-1, 1)]
ROOMY = 32 * 1024 * 1024
HANDED = 4 * 1024 * 1024


def vmem(count):
    return [pl.BlockSpec(memory_space=pltpu.VMEM)] * count


def slot(i, j, k):
    return ((i + 1) * 3 + j + 1) * 2 + (1 if k > 0 else 0)


def there(counts, side, sign):
    place_of = [lax.axis_index(axis) + sign * step for axis, step in zip(AXES, side)]
    real = True
    for at, count, step in zip(place_of, counts, side):
        if step != 0:
            real = real & (at >= 0) & (at < count)
    return tuple(place_of), real


def swap_copy(counts, n, rows, packed, got, sends, recvs):
    i, j, k = SIDES[n]
    take = {-1: pl.ds(1, 1), 0: pl.ds(1, 4), 1: pl.ds(4, 1)}
    land = {-1: pl.ds(5, 1), 0: pl.ds(1, 4), 1: pl.ds(0, 1)}
    if k == 0:
        source, target = rows.at[take[i], take[j]], rows.at[land[i], land[j]]
    else:
        source, target = packed, got.at[slot(-i, -j, -k)]
    return pltpu.make_async_remote_copy(
        src_ref=source,
        dst_ref=target,
        send_sem=sends.at[n],
        recv_sem=recvs.at[n],
        device_id=there(counts, SIDES[n], 1)[0],
        device_id_type=MESH,
    )


def swap_start(counts, *refs):
    for n in range(len(SIDES)):

        @pl.when(there(counts, SIDES[n], 1)[1])
        def _():
            swap_copy(counts, n, *refs).start()


def swap_finish(counts, *refs):
    for n in range(len(SIDES)):

        @pl.when(there(counts, SIDES[n], -1)[1])
        def _():
            swap_copy(counts, n, *refs).wait_recv()

        @pl.when(there(counts, SIDES[n], 1)[1])
        def _():
            swap_copy(counts, n, *refs).wait_send()


def spot(x, y):
    return (x + 1) * 6 + y + 1


def lanes_of(rows, width=128):
    return lax.broadcasted_iota(jnp.int32, (rows, width), 1)


def clear_rim(rows, got):
    rows[0] = jnp.zeros(rows.shape[1:], rows.dtype)
    rows[5] = jnp.zeros(rows.shape[1:], rows.dtype)
    for x in range(1, 5):
        rows[x, 0] = jnp.zeros(rows.shape[2:], rows.dtype)
        rows[x, 5] = jnp.zeros(rows.shape[2:], rows.dtype)
    got[...] = jnp.zeros_like(got)


def edges(values, x, y, group):
    lane = lanes_of(32)
    place_of = spot(x, y)
    for f, value in enumerate(values):
        turned = pltpu.roll(value, (2 * place_of + 1 + 64 * f) % 128, 1)
        group = jnp.where(lane // 2 == place_of + 32 * f, turned, group)
    return group


def columns(got, f):
    lane = lanes_of(32)
    low = lane % 2 == 1
    at_x, at_y = lane // 12, lane // 2 % 6
    result = jnp.zeros((32, 128), jnp.float32)
    for i in (-1, 0, 1):
        for j in (-1, 0, 1):
            mine = (lane < 72) & (at_x == 0 if i < 0 else at_x == 5 if i > 0 else (at_x > 0) & (at_x < 5))
            mine = mine & (at_y == 0 if j < 0 else at_y == 5 if j > 0 else (at_y > 0) & (at_y < 5))
            for k in (-1, 1):
                turn = (48 * i + 8 * j - 64 * f - k) % 128
                block = pltpu.roll(got[slot(i, j, k)].astype(jnp.float32), turn, 1)
                result = jnp.where(mine & (low if k < 0 else ~low), block, result)
    return result


def column_window(value):
    return jnp.concatenate(
        [
            pltpu.roll(value, (-12 * (a - 1) - 2 * (b - 1)) % 128, 1)
            for a in range(3)
            for b in range(3)
        ]
    ).astype(jnp.bfloat16)


def dot(a, b):
    return jnp.dot(a, b, preferred_element_type=jnp.float32)


def dot_over(a, b, dims, precision=None):
    return lax.dot_general(
        a, b, ((dims[:1], dims[1:]), ((), ())), precision=precision, preferred_element_type=jnp.float32
    )


def ahead(weight):
    size = weight.shape[1]
    taps = weight[...].reshape(9, 3, size, weight.shape[2])
    return jnp.concatenate([taps[:, c].reshape(9 * size, weight.shape[2]).T for c in range(3)])


def back(weight):
    return jnp.concatenate(
        [
            jnp.concatenate([weight[26 - 3 * ab - c] for ab in range(9)], axis=1)
            for c in range(3)
        ]
    )


def near(ref, x, chans):
    return jnp.concatenate(
        [
            jnp.concatenate([ref[x + a, y + b, chans, :] for y in range(4)], axis=1)
            for a in range(3)
            for b in range(3)
        ]
    )


def settle(taps, rim, x):
    lane = lanes_of(32)
    rows = []
    for y in range(4):
        part = taps[:, y * 128 : y * 128 + 128]
        edge = pltpu.roll(rim, (127 - 2 * spot(x, y)) % 128, 1)
        low = jnp.where(lane == 0, edge, pltpu.roll(part[:32], 1, 1))
        high = jnp.where(lane == 127, edge, pltpu.roll(part[64:], 127, 1))
        rows.append(low + part[32:64] + high)
    return rows


def rim_of(weight, window):
    taps = dot(weight, window)
    return jnp.where(lanes_of(32) % 2 == 1, taps[:32], taps[64:])


def thrice(value):
    lane = lax.broadcasted_iota(jnp.int32, value.shape, 1) % 128
    size = value.shape[1]
    value = value.astype(jnp.float32)
    parts = []
    for at in range(0, size, 128):
        part = value[:, at : at + 128]
        spare = lane[:, :128]
        parts.append(
            jnp.concatenate(
                [
                    jnp.where(spare == 127, 0.0, pltpu.roll(part, 127, 1)),
                    part,
                    jnp.where(spare == 0, 0.0, pltpu.roll(part, 1, 1)),
                ]
            )
        )
    return jnp.concatenate(parts, axis=1).astype(jnp.bfloat16)


def thrice_rim(edge):
    low = lanes_of(32) % 2 == 1
    return jnp.concatenate(
        [jnp.where(low, edge, 0.0), jnp.zeros_like(edge), jnp.where(low, 0.0, edge)]
    ).astype(jnp.bfloat16)


def silu_parts(z):
    sigma = jax.nn.sigmoid(z)
    act = (z * sigma).astype(jnp.bfloat16).astype(jnp.float32)
    return act, sigma * (1.0 + z * (1.0 - sigma))


def spread(value, chooser):
    high = value.astype(jnp.bfloat16)
    rest = value - high.astype(jnp.float32)
    middle = rest.astype(jnp.bfloat16)
    low = (rest - middle.astype(jnp.float32)).astype(jnp.bfloat16)
    count = value.shape[0]
    chosen = dot(jnp.concatenate([high, middle, low]), chooser)
    return chosen[:count] + chosen[count : 2 * count] + chosen[2 * count :]


def chooser_of(blocks, step, inner):
    row = lax.broadcasted_iota(jnp.int32, (27 * blocks, 128 * blocks), 0)
    lane = lax.broadcasted_iota(jnp.int32, (27 * blocks, 128 * blocks), 1)
    tap = lane % 128
    ab, c = tap // 3, tap % 3
    source = ab * step + c * inner + lane // 128
    return jnp.where((row == source) & (tap < 27), 1.0, 0.0).astype(jnp.bfloat16)


def whole_kernel(
    counts, scale, fea_far, cot_far, w_in_far, w_out_far, w_in9, w_mid9, w_lift_far,
    out, g_input, g_fine_in, g_in, g_mid, g_lift, g_fine_out,
    one, two, got_one, got_two, pack_one, pack_two, sends_one, recvs_one, sends_two, recvs_two,
    tmp, ws, near_rim, rim_sums, total_ref, mine, full, mid_back, in_back, weight_sems,
    w9, wm9, gather_local, gather_sends, gather_recvs,
    grown, grown_rim, pad_in, pad_mid, pad_smid, pad_sin, table, thirds,
    jd, dz_edges, sums, parts, landed, sum_local, sum_sends, sum_recvs,
    fea, cot, w_in, w_out, w_lift, ready,
):
    nx, ny, nz = counts
    total = nx * ny * nz
    gx, gy, gz = (lax.axis_index(axis) for axis in AXES)
    me = (gx * ny + gy) * nz + gz
    f32, bf16 = jnp.float32, jnp.bfloat16
    pairs = [(fea_far, fea), (cot_far, cot), (w_in_far, w_in), (w_out_far, w_out)]
    pairs += [(w_in9, w9), (w_mid9, wm9), (w_lift_far, w_lift)]
    fetches = [
        pltpu.make_async_copy(source, target, weight_sems.at[n])
        for n, (source, target) in enumerate(pairs)
    ]
    for fetch in fetches:
        fetch.start()
    clear_rim(one, got_one)
    clear_rim(two, got_two)
    barrier = pltpu.get_barrier_semaphore()

    def tell(semaphore):
        told = 0
        for side in SIDES:
            peer, real = there(counts, side, 1)
            told = told + jnp.where(real, 1, 0)

            @pl.when(real)
            def _():
                pl.semaphore_signal(semaphore, inc=1, device_id=peer, device_id_type=MESH)

        return told

    told = tell(barrier)
    fetches[0].wait()
    fetches[1].wait()
    group = jnp.zeros((32, 128), f32)
    for x in range(4):
        tmp[0] = fea[:, x].astype(f32).reshape(128, 128)
        tmp[1] = cot[:, x].astype(f32).reshape(128, 128)
        for y in range(4):
            values = [tmp[f, pl.ds(y, 32, stride=4), :] for f in range(2)]
            one[x + 1, y + 1] = jnp.concatenate(values).astype(bf16)
            group = edges(values, x, y, group)
    pack_one[...] = group.astype(bf16)
    fetches[2].wait()
    fetches[3].wait()
    ws[0], ws[1], ws[2], ws[3] = ahead(w_in), back(w_out), ahead(w_out), back(w_in)
    pl.semaphore_wait(barrier, told)
    first = (counts, one, pack_one, got_one, sends_one, recvs_one)
    swap_start(*first)
    swap_finish(*first)
    tell(ready)

    for f in range(2):
        window = column_window(columns(got_one, f))
        if f == 0:
            near_rim[0] = window
        rim_sums[f] = rim_of(ws[f], window)
    total_ref[...] = jnp.zeros_like(total_ref)
    pack_two[...] = jnp.zeros_like(pack_two)

    def fine(x, carry):
        z = settle(dot(ws[0], near(one, x, slice(0, 32))), rim_sums[0], x)
        d = settle(dot(ws[1], near(one, x, slice(32, 64))), rim_sums[1], x)
        group = pack_two[...].astype(f32)
        acts = jnp.zeros((32, 128), f32)
        for y in range(4):
            two[x + 1, y + 1] = jnp.concatenate([z[y], d[y]]).astype(bf16)
            group = edges([z[y], d[y]], x, y, group)
            acts = acts + silu_parts(z[y])[0]
        pack_two[...] = group.astype(bf16)
        total_ref[...] += jnp.concatenate([acts, d[0] + d[1] + d[2] + d[3]])
        return carry

    lax.fori_loop(0, 4, fine, 0)
    row = lax.broadcasted_iota(jnp.int32, (32, 128), 0)
    pick_cell = jnp.where(lanes_of(32) // 4 == row, 1.0, 0.0)
    means = dot_over(pick_cell, total_ref[...], (1, 1), lax.Precision.HIGHEST)
    both = jnp.concatenate([means[:, :32] * (1.0 / 64.0), means[:, 32:]], axis=1)
    mine[...] = jnp.concatenate([both[:16], both[16:]], axis=1).astype(bf16)

    def spread_copy(k, source, target, local_sems):
        peer = (me + k) % total
        return pltpu.make_async_remote_copy(
            src_ref=source(peer),
            dst_ref=target.at[me],
            send_sem=local_sems[0].at[k],
            recv_sem=local_sems[1].at[k],
            device_id=place(peer, counts),
            device_id_type=MESH,
        )

    def gather_copy(k):
        return spread_copy(k, lambda peer: mine, full, (gather_sends, gather_recvs))

    def sum_copy(k):
        return spread_copy(k, lambda peer: parts.at[peer], landed, (sum_sends, sum_recvs))

    def each_peer(act):
        def step(k, carry):
            act(k)
            return carry

        lax.fori_loop(1, total, step, 0)

    pl.semaphore_wait(ready, told)
    each_peer(lambda k: gather_copy(k).start())
    own = pltpu.make_async_copy(mine, full.at[me], gather_local)
    own.start()
    second = (counts, two, pack_two, got_two, sends_two, recvs_two)
    swap_start(*second)

    for fetch in fetches[4:]:
        fetch.wait()
    wide, narrow = w9.shape[2], in_back.shape[2]

    def turn(ab, carry):
        for c in range(3):
            rows = slice(c * wide, c * wide + wide)
            mid_back[ab, rows, :] = wm9[8 - ab, (2 - c) * wide : (3 - c) * wide, :].T
            in_back[ab, rows, :] = w9[8 - ab, (2 - c) * narrow : (3 - c) * narrow, :].T
        return carry

    lax.fori_loop(0, 9, turn, 0)
    for pad in (pad_in, pad_mid, pad_smid, pad_sin):
        pad[...] = jnp.zeros_like(pad)
    own.wait()
    each_peer(lambda k: gather_copy(k).wait())

    cells = nx * ny * 128

    def pick(size, pieces, index):
        each = size // pieces
        row = lax.broadcasted_iota(jnp.int32, (size, each), 0)
        column = lax.broadcasted_iota(jnp.int32, (size, each), 1)
        return jnp.where(row == index * each + column, 1.0, 0.0).astype(bf16)

    at_o = gy * nz + gz
    pick_mid, pick_in = pick(128, nx, gx), pick(32, nx, gx)
    pick_o, pick_lift = pick(128, ny * nz, at_o), pick(32, ny * nz, at_o)

    def fill(pad, value):
        at = lax.broadcasted_iota(jnp.int32, value.shape, 0) % 128
        low = jnp.where(at == 0, 0.0, pltpu.roll(value, 1, 0))
        high = jnp.where(at == 127, 0.0, pltpu.roll(value, cells - 1, 0))
        wide = jnp.concatenate([low, value, high], axis=1).astype(bf16)
        pad[1 : nx + 1, 1 : ny + 1] = wide.reshape(nx, ny, 128, wide.shape[1])

    def window(pad, ab):
        a, b = ab // 3, ab % 3
        return pad[a : a + nx, b : b + ny].reshape(cells, pad.shape[3])

    def conv(pad, weight):
        result = dot(window(pad, 0), weight[0])
        for ab in range(1, 9):
            result = result + dot(window(pad, ab), weight[ab])
        return result

    def slope(v):
        sigma = jax.nn.sigmoid(v)
        return sigma * (1.0 + v * (1.0 - sigma))

    pieces = []
    for k in range(nx * ny):
        for z in range(nz):
            block = full[k * nz + z]
            pieces += [block[:, :64], block[:, 64:]]
    both = jnp.concatenate(pieces)
    pooled, d_lift = both[:, :32], both[:, 32:]
    fill(pad_in, pooled.astype(f32))
    z_second = conv(pad_in, w9)
    act_second = jax.nn.silu(z_second)
    fill(pad_mid, act_second)
    z_third = conv(pad_mid, wm9)
    act_third = jax.nn.silu(z_third).astype(bf16)
    lifted = dot(act_third, w_lift[...].T)
    dz_third = (dot(d_lift, w_lift[...]) * slope(z_third)).astype(bf16)
    fill(pad_mid, dz_third.astype(f32))
    dz_second = (conv(pad_mid, mid_back) * slope(z_second)).astype(bf16)
    fill(pad_mid, dz_second.astype(f32))
    d_pool = conv(pad_mid, in_back)
    table[...] = (
        jnp.concatenate([lifted, d_pool * (1.0 / 64.0)], axis=1)
        .astype(bf16)
        .reshape(nx, ny, 128, 64)
    )
    thirds[0] = dot(dz_third, pick_o).T.astype(bf16)
    thirds[1] = dot(dz_second, pick_o).T.astype(bf16)
    fill(pad_smid, dot(act_second.astype(bf16), pick_mid))
    fill(pad_sin, dot(pooled, pick_in))
    third_i = dot(act_third, pick_mid).astype(bf16)
    lift_o = dot(d_lift, pick_lift).T.astype(bf16)
    g_lift[...] = dot(lift_o, third_i) * scale

    row = lax.broadcasted_iota(jnp.int32, (128, 128), 0)
    lane = lanes_of(128)
    grow = jnp.where(row == lane // 4 + gz * 32, 1.0, 0.0).astype(bf16)
    past = gz * 32 + jnp.where(lane % 2 == 1, -1, 32)
    at_x, at_y = lane // 12, lane // 2 % 6
    rim = jnp.zeros((64, 128), f32)
    for i in range(3):
        for j in range(3):
            x = jnp.clip(gx + i - 1, 0, nx - 1)
            y = jnp.clip(gy + j - 1, 0, ny - 1)
            grown[i, j] = dot_over(table[x, y], grow, (0, 0))
            mine_too = ((at_x + 3) // 4 == i) & ((at_y + 3) // 4 == j) & (lane < 72)
            far = jnp.where((row == past) & mine_too, 1.0, 0.0).astype(bf16)
            rim = rim + dot_over(table[x, y], far, (0, 0))
    swap_finish(*second)

    lane = lanes_of(32)
    at_x, at_y = gx * 4 + lane // 12 - 1, gy * 4 + lane // 2 % 6 - 1
    real = (at_x >= 0) & (at_x < nx * 4) & (at_y >= 0) & (at_y < ny * 4) & (lane < 72)
    reach = gz + jnp.where(lane % 2 == 1, -1, 1)
    real = real & (reach >= 0) & (reach < nz)
    act, bend = silu_parts(columns(got_two, 0))
    near_rim[1] = column_window(jnp.where(real, act + rim[:32], 0.0))
    near_rim[2] = column_window(jnp.where(real, (columns(got_two, 1) + rim[32:]) * bend, 0.0))
    rim_sums[0] = rim_of(ws[2], near_rim[1])
    rim_sums[1] = rim_of(ws[3], near_rim[2])
    dz_edges[...] = jnp.zeros_like(dz_edges)

    def join(r, carry):
        x, y = r // 6, r % 6
        at_x, at_y = gx * 4 + x - 1, gy * 4 + y - 1
        real = (at_x >= 0) & (at_x < nx * 4) & (at_y >= 0) & (at_y < ny * 4)
        keep = jnp.where(real, 1.0, 0.0)
        up = grown[(x + 3) // 4, (y + 3) // 4]
        both = two[x, y].astype(f32)
        act, bend = silu_parts(both[:32])
        joined = (act + up[:32]) * keep
        dz = (both[32:] + up[32:]) * bend * keep
        jd[x, y] = jnp.concatenate([joined, dz]).astype(bf16)
        here = jnp.where((x >= 1) & (x <= 4) & (y >= 1) & (y <= 4), r, -1)
        turned = pltpu.roll(dz, (2 * r + 1) % 128, 1)
        dz_edges[...] = jnp.where(lanes_of(32) // 2 == here, turned, dz_edges[...])
        return carry

    lax.fori_loop(0, 36, join, 0)
    ends = pltpu.roll(pack_one[...].astype(f32), 64, 1)
    ends = jnp.where(lanes_of(32) < 64, ends, 0.0)
    sums[0] = dot_over(near_rim[1], thrice_rim(ends), (1, 1))
    sums[1] = dot_over(near_rim[0], thrice_rim(dz_edges[...]), (1, 1))

    def last(x, carry):
        joined = near(jd, x, slice(0, 32))
        rows = settle(dot(ws[2], joined), rim_sums[0], x)
        for y in range(4):
            tmp[0, pl.ds(y, 32, stride=4), :] = rows[y]
        out[:, x] = tmp[0].reshape(32, 4, 128).astype(bf16)
        given = [one[x + 1, y + 1, 32:64, :] for y in range(4)]
        sums[0] += dot_over(joined, thrice(jnp.concatenate(given, axis=1)), (1, 1))
        rows = settle(dot(ws[3], near(jd, x, slice(32, 64))), rim_sums[1], x)
        for y in range(4):
            tmp[1, pl.ds(y, 32, stride=4), :] = rows[y]
        g_input[:, x] = tmp[1].reshape(32, 4, 128).astype(bf16)
        given = [jd[x + 1, y + 1, 32:64, :] for y in range(4)]
        sums[1] += dot_over(
            near(one, x, slice(0, 32)), thrice(jnp.concatenate(given, axis=1)), (1, 1)
        )
        return carry

    lax.fori_loop(0, 4, last, 0)
    ci, co = 32 // nx, 32 // (ny * nz)
    for f in range(2):
        value = sums[f].reshape(9, nx, ci, 96)
        for i in range(nx):
            turned = value[:, i].reshape(9 * ci, 96).T
            block = jnp.concatenate([turned[:32], turned[32:64], turned[64:]], axis=1)
            for j in range(ny * nz):
                parts[i * ny * nz + j, f * co : f * co + co, :] = block[
                    j * co : j * co + co
                ].astype(bf16)
    each_peer(lambda k: sum_copy(k).start())
    own = pltpu.make_async_copy(parts.at[me], landed.at[me], sum_local)
    own.start()

    taken = []
    for ab in range(9):
        grad = dot(thirds[0], window(pad_smid, ab)) * scale
        share = grad.shape[1] // 3
        for c in range(3):
            g_mid[3 * ab + c] = grad[:, c * share : c * share + share]
        taken.append(dot(thirds[1], window(pad_sin, ab)) * scale)
    chosen = spread(jnp.concatenate(taken, axis=1), chooser_of(ci, 3 * ci, ci))
    for i in range(ci):
        g_in[i] = chosen[:, i * 128 : i * 128 + 27]
    chooser = chooser_of(ci, ci, 9 * ci)
    own.wait()
    each_peer(lambda k: sum_copy(k).wait())
    chosen = spread(landed[...].astype(f32).sum(0) * scale, chooser)
    for i in range(ci):
        g_fine_out[i] = chosen[:co, i * 128 : i * 128 + 27]
        g_fine_in[i] = chosen[co:, i * 128 : i * 128 + 27]


def hand_over(*refs):
    *refs, sems = refs
    half = len(refs) // 2
    copies = [
        pltpu.make_async_copy(source, target, sems.at[n])
        for n, (source, target) in enumerate(zip(refs[:half], refs[half:]))
    ]
    for copy in copies:
        copy.start()
    for copy in copies:
        copy.wait()


def shards(features, cotangent, w_fine_in, w_coarse_in, w_coarse_mid, w_lift, w_fine_out):
    counts = tuple(lax.axis_size(axis) for axis in AXES)
    nx, ny, nz = counts
    total = nx * ny * nz
    chans, depth, height, length = features.shape
    wide = w_lift.shape[0]
    scale = 1.0 / math.sqrt(total * depth * height * length)
    f32, bf16 = jnp.float32, jnp.bfloat16
    shape = jax.ShapeDtypeStruct
    co, cw = wide // (ny * nz), wide // nx
    ci, fo = chans // nx, chans // (ny * nz)
    pads = [3 * chans, 3 * wide, 3 * cw, 3 * ci]
    block = (2 * fo, 27 * ci)
    rows = pltpu.VMEM((6, 6, 2 * chans, 128), bf16)
    got = pltpu.VMEM((18, chans, 128), bf16)
    packed = pltpu.VMEM((chans, 128), bf16)
    swaps = pltpu.SemaphoreType.DMA((len(SIDES),))
    one, many = pltpu.SemaphoreType.DMA, pltpu.SemaphoreType.DMA((total,))
    anywhere = pl.BlockSpec(memory_space=pl.ANY)
    results = pl.pallas_call(
        lambda *refs: whole_kernel(counts, scale, *refs),
        out_shape=(
            shape(features.shape, bf16),
            shape(features.shape, bf16),
            shape((ci, fo, 27), f32),
            shape((ci, co, 27), f32),
            shape((27, co, cw), f32),
            shape((fo, cw), f32),
            shape((ci, fo, 27), f32),
        ),
        in_specs=[pl.BlockSpec(memory_space=pltpu.HBM)] * 7,
        out_specs=vmem(7),
        scratch_shapes=[
            rows, rows, got, got, packed, packed, swaps, swaps, swaps, swaps,
            pltpu.VMEM((2, 128, 128), f32),
            pltpu.VMEM((4, 3 * chans, 9 * chans), bf16),
            pltpu.VMEM((3, 9 * chans, 128), bf16),
            pltpu.VMEM((2, chans, 128), f32),
            pltpu.VMEM((2 * chans, 128), f32),
            pltpu.VMEM((16, 128), bf16),
            pltpu.VMEM((total, 16, 128), bf16),
            pltpu.VMEM((9, 3 * wide, wide), bf16),
            pltpu.VMEM((9, 3 * wide, chans), bf16),
            pltpu.SemaphoreType.DMA((7,)),
            pltpu.VMEM((9, 3 * chans, wide), bf16),
            pltpu.VMEM((9, 3 * wide, wide), bf16),
            one, many, many,
            pltpu.VMEM((3, 3, 2 * chans, 128), f32),
            pltpu.VMEM((2 * chans, 128), f32),
        ]
        + [pltpu.VMEM((nx + 2, ny + 2, 128, k), bf16) for k in pads]
        + [
            pltpu.VMEM((nx, ny, 128, 2 * chans), bf16),
            pltpu.VMEM((2, co, nx * ny * 128), bf16),
            rows,
            pltpu.VMEM((chans, 128), f32),
            pltpu.VMEM((2, 9 * chans, 3 * chans), f32),
            pltpu.VMEM((total,) + block, bf16),
            pltpu.VMEM((total,) + block, bf16),
            one, many, many,
            pltpu.VMEM(features.shape, bf16),
            pltpu.VMEM(features.shape, bf16),
            pltpu.VMEM(w_fine_in.shape, bf16),
            pltpu.VMEM(w_fine_in.shape, bf16),
            pltpu.VMEM((chans, wide), bf16),
            pltpu.SemaphoreType.REGULAR,
        ],
        compiler_params=pltpu.CompilerParams(
            collective_id=0, has_side_effects=True, vmem_limit_bytes=ROOMY
        ),
        name="whole",
    )(
        *[
            pltpu.with_memory_space_constraint(value, pltpu.HBM)
            for value in (
                features, cotangent, w_fine_in, w_fine_out,
                w_coarse_in.reshape(9, 3 * chans, wide),
                w_coarse_mid.reshape(9, 3 * wide, wide), w_lift.T,
            )
        ]
    )
    output, grad_input, g_fine_in, g_in, g_mid, g_lift, g_fine_out = pl.pallas_call(
        hand_over,
        out_shape=[shape(value.shape, value.dtype) for value in results],
        in_specs=vmem(7),
        out_specs=[anywhere] * 7,
        scratch_shapes=[pltpu.SemaphoreType.DMA((7,))],
        compiler_params=pltpu.CompilerParams(vmem_limit_bytes=HANDED),
        name="hand_over",
    )(*results)
    return (
        output,
        grad_input,
        g_fine_in.transpose(2, 0, 1),
        g_in.transpose(2, 0, 1),
        g_mid.transpose(0, 2, 1),
        g_lift.T,
        g_fine_out.transpose(2, 0, 1),
    )


def choose(features, *rest):
    nx, ny, nz = (lax.axis_size(axis) for axis in AXES)
    total = nx * ny * nz
    wide = rest[4].shape[0]
    fits = features.shape == (32, 4, 4, 128) and nz == 4 and total <= DIRECT
    fits = fits and 32 % (ny * nz) == 0 and 32 % nx == 0 and 32 // nx == 8 and wide == 128
    return (shards if fits else shards_layered)(features, *rest)


def solution(mesh):
    whole = P(None, "gx", "gy", "gz")
    split = P(None, "gx", ("gy", "gz"))
    return jax.shard_map(
        choose,
        mesh=mesh,
        in_specs=(whole, whole, P(), P(), P(), P(), P()),
        out_specs=(whole, whole, split, split, split, P("gx", ("gy", "gz")), split),
        check_vma=False,
    )
```

```python
import math

import jax
import jax.numpy as jnp
from jax import lax
from jax.experimental import pallas as pl
from jax.experimental.pallas import tpu as pltpu
from jax.sharding import PartitionSpec as P

AXES = ("gx", "gy", "gz")
MESH = pl.DeviceIdType.MESH
DIRECT = 64


def place(flat, counts):
    nx, ny, nz = counts
    return (flat // (ny * nz), (flat // nz) % ny, flat % nz)


def extended(cells, sides, width):
    for axis, dim in sides:
        count = lax.axis_size(axis)
        ends = count - 1
        head = lax.slice_in_dim(cells, 0, width, axis=dim)
        tail = lax.slice_in_dim(cells, cells.shape[dim] - width, cells.shape[dim], axis=dim)
        cells = jnp.concatenate(
            [
                lax.ppermute(tail, axis, [(i, (i + 1) % count) for i in range(ends)]),
                cells,
                lax.ppermute(head, axis, [((i + 1) % count, i) for i in range(ends)]),
            ],
            axis=dim,
        )
    return cells


def silu_slope(values):
    sigma = jax.nn.sigmoid(values)
    return sigma * (1.0 + values * (1.0 - sigma))


def conv_valid(padded, weight, form="NCDHW"):
    kernel = weight.reshape(3, 3, 3, weight.shape[1], weight.shape[2])
    result = lax.conv_general_dilated(
        padded[None],
        kernel,
        (1, 1, 1),
        "VALID",
        dimension_numbers=(form, "DHWIO", form),
        preferred_element_type=jnp.float32,
    )
    return result[0]


def flipped(weight):
    return jnp.flip(weight, 0).transpose(0, 2, 1)


def pool_blocks(field):
    chans, depth, height, length = field.shape
    grouped = field.astype(jnp.float32).reshape(
        chans, depth // 4, 4, height // 4, 4, length // 4, 4
    )
    return grouped.sum(axis=(2, 4, 6))


def spread_up(field):
    chans, depth, height, length = field.shape
    grown = jnp.broadcast_to(
        field[:, :, None, :, None, :, None], (chans, depth, 4, height, 4, length, 4)
    )
    return grown.reshape(chans, depth * 4, height * 4, length * 4)


def tap_grad_direct(padded, grad):
    depth = padded.shape[1] - 2
    height = padded.shape[2] - 2
    length = padded.shape[3] - 2
    flat_grad = grad.reshape(grad.shape[0], -1)
    blocks = []
    for tap in range(27):
        shift_x, shift_y, shift_z = (tap // 9, tap // 3 % 3, tap % 3)
        window = padded[
            :, shift_x : shift_x + depth, shift_y : shift_y + height, shift_z : shift_z + length
        ].reshape(padded.shape[0], -1)
        blocks.append(
            lax.dot_general(
                window, flat_grad, (((1,), (1,)), ((), ())), preferred_element_type=jnp.float32
            )
        )
    return jnp.stack(blocks)


def fine_rim(field):
    return extended(field, (("gx", 1), ("gy", 2), ("gz", 3)), 1)


def coarse_rim(field):
    return extended(field, (("gx", 1), ("gy", 2), ("gz", 3)), 1)


def reduce_grad(partial_value):
    first = lax.psum_scatter(partial_value, "gx", scatter_dimension=1, tiled=True)
    return lax.psum_scatter(first, ("gy", "gz"), scatter_dimension=2, tiled=True)


def input_share(field):
    parts = lax.all_to_all(field[None], "gx", split_axis=1, concat_axis=0, tiled=True)
    moved = jnp.moveaxis(parts, 0, 1)
    moved = moved.reshape(moved.shape[0], -1, moved.shape[3], moved.shape[4])
    moved = lax.all_gather(moved, "gy", axis=2, tiled=True)
    return lax.all_gather(moved, "gz", axis=3, tiled=True)


def output_share(field):
    parts = lax.all_to_all(field[None], ("gy", "gz"), split_axis=1, concat_axis=0, tiled=True)
    count_y = lax.axis_size("gy")
    count_z = lax.axis_size("gz")
    chans = parts.shape[1]
    depth, height, length = (parts.shape[2], parts.shape[3], parts.shape[4])
    grid = parts.reshape(count_y, count_z, chans, depth, height, length).transpose(2, 3, 0, 4, 1, 5)
    grid = grid.reshape(chans, depth, count_y * height, count_z * length)
    return lax.all_gather(grid, "gx", axis=1, tiled=True)


def shards_layered(features, cotangent, w_fine_in, w_coarse_in, w_coarse_mid, w_lift, w_fine_out):
    depth, height, length = (features.shape[1], features.shape[2], features.shape[3])
    whole_cells = (
        depth * lax.axis_size("gx") * height * lax.axis_size("gy") * length * lax.axis_size("gz")
    )
    scale = 1.0 / math.sqrt(whole_cells)
    padded_in = fine_rim(features)
    z_first = conv_valid(padded_in, w_fine_in)
    act_first = jax.nn.silu(z_first).astype(jnp.bfloat16)
    pooled = (pool_blocks(act_first) / 64.0).astype(jnp.bfloat16)
    pooled_pad = coarse_rim(pooled)
    z_second = conv_valid(pooled_pad, w_coarse_in)
    act_second = jax.nn.silu(z_second).astype(jnp.bfloat16)
    second_pad = coarse_rim(act_second)
    z_third = conv_valid(second_pad, w_coarse_mid)
    act_third = jax.nn.silu(z_third).astype(jnp.bfloat16)
    lifted = lax.dot_general(
        w_lift, act_third, (((0,), (0,)), ((), ())), preferred_element_type=jnp.float32
    )
    joined = (act_first.astype(jnp.float32) + spread_up(lifted)).astype(jnp.bfloat16)
    padded_joined = fine_rim(joined)
    output = conv_valid(padded_joined, w_fine_out).astype(jnp.bfloat16)
    part_fine_out = tap_grad_direct(padded_joined, cotangent) * scale
    d_joined = conv_valid(fine_rim(cotangent), flipped(w_fine_out))
    d_lift = pool_blocks(d_joined)
    lift_partial = (
        lax.dot_general(
            act_third.astype(jnp.float32),
            d_lift,
            (((1, 2, 3), (1, 2, 3)), ((), ())),
            precision=lax.Precision.HIGHEST,
        )
        * scale
    )
    d_third = lax.dot_general(
        w_lift.astype(jnp.float32),
        d_lift,
        (((1,), (0,)), ((), ())),
        precision=lax.Precision.HIGHEST,
    )
    dz_third = (d_third * silu_slope(z_third)).astype(jnp.bfloat16)
    dz_third_pad = coarse_rim(dz_third)
    grad_coarse_mid = None
    sources = input_share(act_second)
    sources_pad = jnp.pad(sources, ((0, 0), (1, 1), (1, 1), (1, 1)))
    targets = output_share(dz_third)
    grad_coarse_mid = tap_grad_direct(sources_pad, targets) * scale
    dz_second = (conv_valid(dz_third_pad, flipped(w_coarse_mid)) * silu_slope(z_second)).astype(
        jnp.bfloat16
    )
    dz_second_pad = coarse_rim(dz_second)
    part_coarse_in = tap_grad_direct(pooled_pad, dz_second) * scale
    d_pool = conv_valid(dz_second_pad, flipped(w_coarse_in))
    dz_first = ((d_joined + spread_up(d_pool) / 64.0) * silu_slope(z_first)).astype(jnp.bfloat16)
    part_fine_in = tap_grad_direct(padded_in, dz_first) * scale
    grad_input = conv_valid(fine_rim(dz_first), flipped(w_fine_in)).astype(jnp.bfloat16)
    pending = [part_fine_out, lift_partial[None], part_coarse_in, part_fine_in]
    reduced = [reduce_grad(partial_value) for partial_value in pending]
    grad_fine_out = reduced[0]
    grad_lift = reduced[1][0]
    grad_coarse_in = reduced[2]
    grad_fine_in = reduced[3]
    return (
        output,
        grad_input,
        grad_fine_in,
        grad_coarse_in,
        grad_coarse_mid,
        grad_lift,
        grad_fine_out,
    )


SIDES = [(i, j, 0) for i in (-1, 0, 1) for j in (-1, 0, 1) if (i, j) != (0, 0)]
SIDES += [(i, j, k) for i in (-1, 0, 1) for j in (-1, 0, 1) for k in (-1, 1)]
ROOMY = 32 * 1024 * 1024
HANDED = 4 * 1024 * 1024


def vmem(count):
    return [pl.BlockSpec(memory_space=pltpu.VMEM)] * count


def slot(i, j, k):
    return ((i + 1) * 3 + j + 1) * 2 + (1 if k > 0 else 0)


def there(counts, side, sign):
    place_of = [lax.axis_index(axis) + sign * step for axis, step in zip(AXES, side)]
    real = True
    for at, count, step in zip(place_of, counts, side):
        if step != 0:
            real = real & (at >= 0) & (at < count)
    return tuple(place_of), real


def swap_copy(counts, n, rows, packed, got, sends, recvs):
    i, j, k = SIDES[n]
    take = {-1: pl.ds(1, 1), 0: pl.ds(1, 4), 1: pl.ds(4, 1)}
    land = {-1: pl.ds(5, 1), 0: pl.ds(1, 4), 1: pl.ds(0, 1)}
    if k == 0:
        source, target = rows.at[take[i], take[j]], rows.at[land[i], land[j]]
    else:
        source, target = packed, got.at[slot(-i, -j, -k)]
    return pltpu.make_async_remote_copy(
        src_ref=source,
        dst_ref=target,
        send_sem=sends.at[n],
        recv_sem=recvs.at[n],
        device_id=there(counts, SIDES[n], 1)[0],
        device_id_type=MESH,
    )


def swap_start(counts, *refs):
    for n in range(len(SIDES)):

        @pl.when(there(counts, SIDES[n], 1)[1])
        def _():
            swap_copy(counts, n, *refs).start()


def swap_finish(counts, *refs):
    for n in range(len(SIDES)):

        @pl.when(there(counts, SIDES[n], -1)[1])
        def _():
            swap_copy(counts, n, *refs).wait_recv()

        @pl.when(there(counts, SIDES[n], 1)[1])
        def _():
            swap_copy(counts, n, *refs).wait_send()


def spot(x, y):
    return (x + 1) * 6 + y + 1


def lanes_of(rows, width=128):
    return lax.broadcasted_iota(jnp.int32, (rows, width), 1)


def clear_rim(rows, got):
    rows[0] = jnp.zeros(rows.shape[1:], rows.dtype)
    rows[5] = jnp.zeros(rows.shape[1:], rows.dtype)
    for x in range(1, 5):
        rows[x, 0] = jnp.zeros(rows.shape[2:], rows.dtype)
        rows[x, 5] = jnp.zeros(rows.shape[2:], rows.dtype)
    got[...] = jnp.zeros_like(got)


def edges(values, x, y, group):
    lane = lanes_of(32)
    place_of = spot(x, y)
    for f, value in enumerate(values):
        turned = pltpu.roll(value, (2 * place_of + 1 + 64 * f) % 128, 1)
        group = jnp.where(lane // 2 == place_of + 32 * f, turned, group)
    return group


def columns(got, f):
    lane = lanes_of(32)
    low = lane % 2 == 1
    at_x, at_y = lane // 12, lane // 2 % 6
    result = jnp.zeros((32, 128), jnp.float32)
    for i in (-1, 0, 1):
        for j in (-1, 0, 1):
            mine = (lane < 72) & (at_x == 0 if i < 0 else at_x == 5 if i > 0 else (at_x > 0) & (at_x < 5))
            mine = mine & (at_y == 0 if j < 0 else at_y == 5 if j > 0 else (at_y > 0) & (at_y < 5))
            for k in (-1, 1):
                turn = (48 * i + 8 * j - 64 * f - k) % 128
                block = pltpu.roll(got[slot(i, j, k)].astype(jnp.float32), turn, 1)
                result = jnp.where(mine & (low if k < 0 else ~low), block, result)
    return result


def column_window(value):
    return jnp.concatenate(
        [
            pltpu.roll(value, (-12 * (a - 1) - 2 * (b - 1)) % 128, 1)
            for a in range(3)
            for b in range(3)
        ]
    ).astype(jnp.bfloat16)


def dot(a, b):
    return jnp.dot(a, b, preferred_element_type=jnp.float32)


def dot_over(a, b, dims, precision=None):
    return lax.dot_general(
        a, b, ((dims[:1], dims[1:]), ((), ())), precision=precision, preferred_element_type=jnp.float32
    )


def ahead(weight):
    size = weight.shape[1]
    taps = weight[...].reshape(9, 3, size, weight.shape[2])
    return jnp.concatenate([taps[:, c].reshape(9 * size, weight.shape[2]).T for c in range(3)])


def back(weight):
    return jnp.concatenate(
        [
            jnp.concatenate([weight[26 - 3 * ab - c] for ab in range(9)], axis=1)
            for c in range(3)
        ]
    )


def near(ref, x, chans):
    return jnp.concatenate(
        [
            jnp.concatenate([ref[x + a, y + b, chans, :] for y in range(4)], axis=1)
            for a in range(3)
            for b in range(3)
        ]
    )


def settle(taps, rim, x):
    lane = lanes_of(32)
    rows = []
    for y in range(4):
        part = taps[:, y * 128 : y * 128 + 128]
        edge = pltpu.roll(rim, (127 - 2 * spot(x, y)) % 128, 1)
        low = jnp.where(lane == 0, edge, pltpu.roll(part[:32], 1, 1))
        high = jnp.where(lane == 127, edge, pltpu.roll(part[64:], 127, 1))
        rows.append(low + part[32:64] + high)
    return rows


def rim_of(weight, window):
    taps = dot(weight, window)
    return jnp.where(lanes_of(32) % 2 == 1, taps[:32], taps[64:])


def thrice(value):
    lane = lax.broadcasted_iota(jnp.int32, value.shape, 1) % 128
    size = value.shape[1]
    value = value.astype(jnp.float32)
    parts = []
    for at in range(0, size, 128):
        part = value[:, at : at + 128]
        spare = lane[:, :128]
        parts.append(
            jnp.concatenate(
                [
                    jnp.where(spare == 127, 0.0, pltpu.roll(part, 127, 1)),
                    part,
                    jnp.where(spare == 0, 0.0, pltpu.roll(part, 1, 1)),
                ]
            )
        )
    return jnp.concatenate(parts, axis=1).astype(jnp.bfloat16)


def thrice_rim(edge):
    low = lanes_of(32) % 2 == 1
    return jnp.concatenate(
        [jnp.where(low, edge, 0.0), jnp.zeros_like(edge), jnp.where(low, 0.0, edge)]
    ).astype(jnp.bfloat16)


def silu_parts(z):
    sigma = jax.nn.sigmoid(z)
    act = (z * sigma).astype(jnp.bfloat16).astype(jnp.float32)
    return act, sigma * (1.0 + z * (1.0 - sigma))


def spread(value, chooser):
    high = value.astype(jnp.bfloat16)
    rest = value - high.astype(jnp.float32)
    middle = rest.astype(jnp.bfloat16)
    low = (rest - middle.astype(jnp.float32)).astype(jnp.bfloat16)
    count = value.shape[0]
    chosen = dot(jnp.concatenate([high, middle, low]), chooser)
    return chosen[:count] + chosen[count : 2 * count] + chosen[2 * count :]


def chooser_of(blocks, step, inner):
    row = lax.broadcasted_iota(jnp.int32, (27 * blocks, 128 * blocks), 0)
    lane = lax.broadcasted_iota(jnp.int32, (27 * blocks, 128 * blocks), 1)
    tap = lane % 128
    ab, c = tap // 3, tap % 3
    source = ab * step + c * inner + lane // 128
    return jnp.where((row == source) & (tap < 27), 1.0, 0.0).astype(jnp.bfloat16)


def whole_kernel(
    counts, scale, fea_far, cot_far, w_in_far, w_out_far, w_in9, w_mid9, w_lift_far,
    out, g_input, g_fine_in, g_in, g_mid, g_lift, g_fine_out,
    one, two, got_one, got_two, pack_one, pack_two, sends_one, recvs_one, sends_two, recvs_two,
    tmp, ws, near_rim, rim_sums, total_ref, mine, full, mid_back, in_back, weight_sems,
    w9, wm9, gather_local, gather_sems,
    grown, grown_rim, pad_in, pad_mid, pad_smid, pad_sin, table, thirds,
    jd, dz_edges, sums, parts, landed, sum_local, sum_sems,
    fea, cot, w_in, w_out, w_lift, ready,
    own_cells, share_a, share_b, land_a, land_b, share_locals, a_sems, b_sems,
):
    nx, ny, nz = counts
    total = nx * ny * nz
    gx, gy, gz = (lax.axis_index(axis) for axis in AXES)
    me = (gx * ny + gy) * nz + gz
    f32, bf16 = jnp.float32, jnp.bfloat16
    pairs = [(fea_far, fea), (cot_far, cot), (w_in_far, w_in), (w_out_far, w_out)]
    pairs += [(w_in9, w9), (w_mid9, wm9), (w_lift_far, w_lift)]
    fetches = [
        pltpu.make_async_copy(source, target, weight_sems.at[n])
        for n, (source, target) in enumerate(pairs)
    ]
    for fetch in fetches:
        fetch.start()
    clear_rim(one, got_one)
    clear_rim(two, got_two)
    barrier = pltpu.get_barrier_semaphore()

    def tell(semaphore):
        told = 0
        for side in SIDES:
            peer, real = there(counts, side, 1)
            told = told + jnp.where(real, 1, 0)

            @pl.when(real)
            def _():
                pl.semaphore_signal(semaphore, inc=1, device_id=peer, device_id_type=MESH)

        return told

    told = tell(barrier)
    fetches[0].wait()
    fetches[1].wait()
    group = jnp.zeros((32, 128), f32)
    for x in range(4):
        tmp[0] = fea[:, x].astype(f32).reshape(128, 128)
        tmp[1] = cot[:, x].astype(f32).reshape(128, 128)
        for y in range(4):
            values = [tmp[f, pl.ds(y, 32, stride=4), :] for f in range(2)]
            one[x + 1, y + 1] = jnp.concatenate(values).astype(bf16)
            group = edges(values, x, y, group)
    pack_one[...] = group.astype(bf16)
    fetches[2].wait()
    fetches[3].wait()
    ws[0], ws[1], ws[2], ws[3] = ahead(w_in), back(w_out), ahead(w_out), back(w_in)
    pl.semaphore_wait(barrier, told)
    first = (counts, one, pack_one, got_one, sends_one, recvs_one)
    swap_start(*first)
    swap_finish(*first)
    tell(ready)

    for f in range(2):
        window = column_window(columns(got_one, f))
        if f == 0:
            near_rim[0] = window
        rim_sums[f] = rim_of(ws[f], window)
    total_ref[...] = jnp.zeros_like(total_ref)
    pack_two[...] = jnp.zeros_like(pack_two)

    def fine(x, carry):
        z = settle(dot(ws[0], near(one, x, slice(0, 32))), rim_sums[0], x)
        d = settle(dot(ws[1], near(one, x, slice(32, 64))), rim_sums[1], x)
        group = pack_two[...].astype(f32)
        acts = jnp.zeros((32, 128), f32)
        for y in range(4):
            two[x + 1, y + 1] = jnp.concatenate([z[y], d[y]]).astype(bf16)
            group = edges([z[y], d[y]], x, y, group)
            acts = acts + silu_parts(z[y])[0]
        pack_two[...] = group.astype(bf16)
        total_ref[...] += jnp.concatenate([acts, d[0] + d[1] + d[2] + d[3]])
        return carry

    lax.fori_loop(0, 4, fine, 0)
    row = lax.broadcasted_iota(jnp.int32, (32, 128), 0)
    pick_cell = jnp.where(lanes_of(32) // 4 == row, 1.0, 0.0)
    means = dot_over(pick_cell, total_ref[...], (1, 1), lax.Precision.HIGHEST)
    both = jnp.concatenate([means[:, :32] * (1.0 / 64.0), means[:, 32:]], axis=1)
    mine[...] = jnp.concatenate([both[:16], both[16:]], axis=1).astype(bf16)

    lines = [
        [at] + [lax.rem(at + k, count) for k in range(1, count)]
        for at, count in zip((gx, gy, gz), counts)
    ]

    def send_all(source, target, sems):
        for x in reversed(range(nx)):
            for y in reversed(range(ny)):
                for z in reversed(range(nz)):
                    if x + y + z > 0:
                        peer = (lines[0][x], lines[1][y], lines[2][z])
                        pltpu.make_async_remote_copy(
                            src_ref=source(peer[0], peer[1] * nz + peer[2]),
                            dst_ref=target.at[me],
                            send_sem=sems.at[0],
                            recv_sem=sems.at[1],
                            device_id=peer,
                            device_id_type=MESH,
                        ).start()

    def wait_all(target, sems):
        everyone_else = target.at[pl.ds(0, total - 1)]
        for n in range(2):
            pltpu.make_async_copy(everyone_else, everyone_else, sems.at[n]).wait()

    pl.semaphore_wait(ready, told)
    send_all(lambda x, o: mine, full, gather_sems)
    own = pltpu.make_async_copy(mine, full.at[me], gather_local)
    own.start()
    second = (counts, two, pack_two, got_two, sends_two, recvs_two)
    swap_start(*second)

    for fetch in fetches[4:]:
        fetch.wait()
    wide, narrow = w9.shape[2], in_back.shape[2]

    def turn(ab, carry):
        for c in range(3):
            rows = slice(c * wide, c * wide + wide)
            mid_back[ab, rows, :] = wm9[8 - ab, (2 - c) * wide : (3 - c) * wide, :].T
            in_back[ab, rows, :] = w9[8 - ab, (2 - c) * narrow : (3 - c) * narrow, :].T
        return carry

    lax.fori_loop(0, 9, turn, 0)
    for pad in (pad_in, pad_mid, pad_smid, pad_sin):
        pad[...] = jnp.zeros_like(pad)
    own.wait()
    wait_all(full, gather_sems)

    span = 48
    cells = nx * ny * span

    def pick(size, pieces, index):
        each = size // pieces
        row = lax.broadcasted_iota(jnp.int32, (size, each), 0)
        column = lax.broadcasted_iota(jnp.int32, (size, each), 1)
        return jnp.where(row == index * each + column, 1.0, 0.0).astype(bf16)

    at_o = gy * nz + gz

    def fill(pad, value):
        rows, size = value.shape[0], pad.shape[2]
        at = lax.broadcasted_iota(jnp.int32, value.shape, 0) % size
        low = jnp.where(at == 0, 0.0, pltpu.roll(value, 1, 0))
        high = jnp.where(at == size - 1, 0.0, pltpu.roll(value, rows - 1, 0))
        wide = jnp.concatenate([low, value, high], axis=1).astype(bf16)
        pad[1 : nx + 1, 1 : ny + 1] = wide.reshape(nx, ny, size, wide.shape[1])

    def window(pad, ab):
        a, b = ab // 3, ab % 3
        return pad[a : a + nx, b : b + ny].reshape(nx * ny * pad.shape[2], pad.shape[3])

    def conv(pad, weight):
        result = dot(window(pad, 0), weight[0])
        for ab in range(1, 9):
            result = result + dot(window(pad, ab), weight[ab])
        return result

    def slope(v):
        sigma = jax.nn.sigmoid(v)
        return sigma * (1.0 + v * (1.0 - sigma))

    before, after = jnp.maximum(gz - 1, 0), jnp.minimum(gz + 1, nz - 1)
    pieces = []
    for k in range(nx * ny):
        here = full[k * nz + gz].astype(f32)
        pieces += [full[k * nz + before].astype(f32)[8:, 64:], here[:, :64], here[:, 64:]]
        pieces += [full[k * nz + after].astype(f32)[:8, :64]]
    at_z = lax.broadcasted_iota(jnp.int32, (cells, 128), 0) % span + gz * 32 - 8
    keep = jnp.where((at_z >= 0) & (at_z < nz * 32), 1.0, 0.0)
    both = jnp.concatenate(pieces) * keep[:, :64]
    fill(pad_in, both[:, :32])
    z_second = conv(pad_in, w9)
    act_second = jax.nn.silu(z_second) * keep
    fill(pad_mid, act_second)
    z_third = conv(pad_mid, wm9)
    act_third = jax.nn.silu(z_third)
    lifted = dot(act_third.astype(bf16), w_lift[...].T)
    dz_third = dot(both[:, 32:].astype(bf16), w_lift[...]) * slope(z_third) * keep
    fill(pad_mid, dz_third)
    dz_second = conv(pad_mid, mid_back) * slope(z_second) * keep
    fill(pad_mid, dz_second)
    d_pool = conv(pad_mid, in_back)
    table[...] = (
        jnp.concatenate([lifted, d_pool * (1.0 / 64.0)], axis=1)
        .astype(bf16)
        .reshape(nx, ny, span, 64)
    )
    for n, value in enumerate([act_second, act_third, dz_third, dz_second]):
        own_cells[:, :, n * 128 : n * 128 + 128] = value.reshape(nx * ny, span, 128)
    mine_now = own_cells[gx * ny + gy, 8:40, :]
    wx, wo = 128 // nx, 128 // (ny * nz)
    for i in range(nx):
        block = jnp.concatenate(
            [mine_now[:, n * 128 + i * wx : n * 128 + i * wx + wx] for n in (0, 1)], axis=1
        )
        share_a[i] = jnp.concatenate([block[:16], block[16:]], axis=1).astype(bf16)
    for i in range(ny * nz):
        block = jnp.concatenate(
            [mine_now[:, n * 128 + i * wo : n * 128 + i * wo + wo] for n in (2, 3)], axis=1
        )
        share_b[i] = jnp.concatenate(
            [block[8 * q : 8 * q + 8] for q in range(4)], axis=1
        ).astype(bf16)

    row = lax.broadcasted_iota(jnp.int32, (span, 128), 0)
    lane = lanes_of(span)
    grow = jnp.where(row == lane // 4 + 8, 1.0, 0.0).astype(bf16)
    past = 8 + jnp.where(lane % 2 == 1, -1, 32)
    at_x, at_y = lane // 12, lane // 2 % 6
    rim = jnp.zeros((64, 128), f32)
    for i in range(3):
        for j in range(3):
            x = jnp.clip(gx + i - 1, 0, nx - 1)
            y = jnp.clip(gy + j - 1, 0, ny - 1)
            grown[i, j] = dot_over(table[x, y], grow, (0, 0))
            mine_too = ((at_x + 3) // 4 == i) & ((at_y + 3) // 4 == j) & (lane < 72)
            far = jnp.where((row == past) & mine_too, 1.0, 0.0).astype(bf16)
            rim = rim + dot_over(table[x, y], far, (0, 0))
    send_all(lambda x, o: share_a.at[x], land_a, a_sems)
    send_all(lambda x, o: share_b.at[o], land_b, b_sems)
    owns = [
        pltpu.make_async_copy(share_a.at[gx], land_a.at[me], share_locals.at[0]),
        pltpu.make_async_copy(share_b.at[at_o], land_b.at[me], share_locals.at[1]),
    ]
    for copy in owns:
        copy.start()
    swap_finish(*second)

    lane = lanes_of(32)
    at_x, at_y = gx * 4 + lane // 12 - 1, gy * 4 + lane // 2 % 6 - 1
    real = (at_x >= 0) & (at_x < nx * 4) & (at_y >= 0) & (at_y < ny * 4) & (lane < 72)
    reach = gz + jnp.where(lane % 2 == 1, -1, 1)
    real = real & (reach >= 0) & (reach < nz)
    act, bend = silu_parts(columns(got_two, 0))
    near_rim[1] = column_window(jnp.where(real, act + rim[:32], 0.0))
    near_rim[2] = column_window(jnp.where(real, (columns(got_two, 1) + rim[32:]) * bend, 0.0))
    rim_sums[0] = rim_of(ws[2], near_rim[1])
    rim_sums[1] = rim_of(ws[3], near_rim[2])
    dz_edges[...] = jnp.zeros_like(dz_edges)

    def join(r, carry):
        x, y = r // 6, r % 6
        at_x, at_y = gx * 4 + x - 1, gy * 4 + y - 1
        real = (at_x >= 0) & (at_x < nx * 4) & (at_y >= 0) & (at_y < ny * 4)
        keep = jnp.where(real, 1.0, 0.0)
        up = grown[(x + 3) // 4, (y + 3) // 4]
        both = two[x, y].astype(f32)
        act, bend = silu_parts(both[:32])
        joined = (act + up[:32]) * keep
        dz = (both[32:] + up[32:]) * bend * keep
        jd[x, y] = jnp.concatenate([joined, dz]).astype(bf16)
        here = jnp.where((x >= 1) & (x <= 4) & (y >= 1) & (y <= 4), r, -1)
        turned = pltpu.roll(dz, (2 * r + 1) % 128, 1)
        dz_edges[...] = jnp.where(lanes_of(32) // 2 == here, turned, dz_edges[...])
        return carry

    lax.fori_loop(0, 36, join, 0)
    ends = pltpu.roll(pack_one[...].astype(f32), 64, 1)
    ends = jnp.where(lanes_of(32) < 64, ends, 0.0)
    sums[0] = dot_over(near_rim[1], thrice_rim(ends), (1, 1))
    sums[1] = dot_over(near_rim[0], thrice_rim(dz_edges[...]), (1, 1))

    def last(x, carry):
        joined = near(jd, x, slice(0, 32))
        rows = settle(dot(ws[2], joined), rim_sums[0], x)
        for y in range(4):
            tmp[0, pl.ds(y, 32, stride=4), :] = rows[y]
        out[:, x] = tmp[0].reshape(32, 4, 128).astype(bf16)
        given = [one[x + 1, y + 1, 32:64, :] for y in range(4)]
        sums[0] += dot_over(joined, thrice(jnp.concatenate(given, axis=1)), (1, 1))
        rows = settle(dot(ws[3], near(jd, x, slice(32, 64))), rim_sums[1], x)
        for y in range(4):
            tmp[1, pl.ds(y, 32, stride=4), :] = rows[y]
        g_input[:, x] = tmp[1].reshape(32, 4, 128).astype(bf16)
        given = [jd[x + 1, y + 1, 32:64, :] for y in range(4)]
        sums[1] += dot_over(
            near(one, x, slice(0, 32)), thrice(jnp.concatenate(given, axis=1)), (1, 1)
        )
        return carry

    lax.fori_loop(0, 4, last, 0)
    ci, co = 32 // nx, 32 // (ny * nz)
    for f in range(2):
        value = sums[f].reshape(9, nx, ci, 96)
        for i in range(nx):
            turned = value[:, i].reshape(9 * ci, 96).T
            block = jnp.concatenate([turned[:32], turned[32:64], turned[64:]], axis=1)
            for j in range(ny * nz):
                parts[i * ny * nz + j, f * co : f * co + co, :] = block[
                    j * co : j * co + co
                ].astype(bf16)
    send_all(lambda x, o: parts.at[x * (ny * nz) + o], landed, sum_sems)
    own = pltpu.make_async_copy(parts.at[me], landed.at[me], sum_local)
    own.start()

    for copy in owns:
        copy.wait()
    wait_all(land_a, a_sems)
    wait_all(land_b, b_sems)
    pieces, firsts, seconds = [], [], []
    for k in range(total):
        block = full[k]
        pieces += [block[:, :64], block[:, 64:]]
        block = land_a[k].astype(f32)
        firsts += [block[:, :64], block[:, 64:]]
        block = land_b[k].astype(f32)
        seconds += [block[:, 32 * q : 32 * q + 32] for q in range(4)]
    both = jnp.concatenate(pieces)
    pooled, d_lift = both[:, :32], both[:, 32:]
    acts = jnp.concatenate(firsts)
    fill(pad_smid, acts[:, :32])
    fill(pad_sin, dot(pooled, pick(32, nx, gx)))
    turned = jnp.concatenate(seconds).T.astype(bf16)
    thirds[0], thirds[1] = turned[:16], turned[16:]
    lift_o = dot(d_lift, pick(32, ny * nz, at_o)).T.astype(bf16)
    g_lift[...] = dot(lift_o, acts[:, 32:].astype(bf16)) * scale
    taken = []
    for ab in range(9):
        grad = dot(thirds[0], window(pad_smid, ab)) * scale
        share = grad.shape[1] // 3
        for c in range(3):
            g_mid[3 * ab + c] = grad[:, c * share : c * share + share]
        taken.append(dot(thirds[1], window(pad_sin, ab)) * scale)
    chosen = spread(jnp.concatenate(taken, axis=1), chooser_of(ci, 3 * ci, ci))
    for i in range(ci):
        g_in[i] = chosen[:, i * 128 : i * 128 + 27]
    chooser = chooser_of(ci, ci, 9 * ci)
    own.wait()
    wait_all(landed, sum_sems)
    chosen = spread(landed[...].astype(f32).sum(0) * scale, chooser)
    for i in range(ci):
        g_fine_out[i] = chosen[:co, i * 128 : i * 128 + 27]
        g_fine_in[i] = chosen[co:, i * 128 : i * 128 + 27]


def hand_over(*refs):
    *refs, sems = refs
    half = len(refs) // 2
    copies = [
        pltpu.make_async_copy(source, target, sems.at[n])
        for n, (source, target) in enumerate(zip(refs[:half], refs[half:]))
    ]
    for copy in copies:
        copy.start()
    for copy in copies:
        copy.wait()


def shards(features, cotangent, w_fine_in, w_coarse_in, w_coarse_mid, w_lift, w_fine_out):
    counts = tuple(lax.axis_size(axis) for axis in AXES)
    nx, ny, nz = counts
    total = nx * ny * nz
    chans, depth, height, length = features.shape
    wide = w_lift.shape[0]
    scale = 1.0 / math.sqrt(total * depth * height * length)
    f32, bf16 = jnp.float32, jnp.bfloat16
    shape = jax.ShapeDtypeStruct
    co, cw = wide // (ny * nz), wide // nx
    ci, fo = chans // nx, chans // (ny * nz)
    pads = [3 * chans, 3 * wide, 3 * cw, 3 * ci]
    block = (2 * fo, 27 * ci)
    rows = pltpu.VMEM((6, 6, 2 * chans, 128), bf16)
    got = pltpu.VMEM((18, chans, 128), bf16)
    packed = pltpu.VMEM((chans, 128), bf16)
    swaps = pltpu.SemaphoreType.DMA((len(SIDES),))
    one, both_ways = pltpu.SemaphoreType.DMA, pltpu.SemaphoreType.DMA((2,))
    anywhere = pl.BlockSpec(memory_space=pl.ANY)
    results = pl.pallas_call(
        lambda *refs: whole_kernel(counts, scale, *refs),
        out_shape=(
            shape(features.shape, bf16),
            shape(features.shape, bf16),
            shape((ci, fo, 27), f32),
            shape((ci, co, 27), f32),
            shape((27, co, cw), f32),
            shape((fo, cw), f32),
            shape((ci, fo, 27), f32),
        ),
        in_specs=[pl.BlockSpec(memory_space=pltpu.HBM)] * 7,
        out_specs=vmem(7),
        scratch_shapes=[
            rows, rows, got, got, packed, packed, swaps, swaps, swaps, swaps,
            pltpu.VMEM((2, 128, 128), f32),
            pltpu.VMEM((4, 3 * chans, 9 * chans), bf16),
            pltpu.VMEM((3, 9 * chans, 128), bf16),
            pltpu.VMEM((2, chans, 128), f32),
            pltpu.VMEM((2 * chans, 128), f32),
            pltpu.VMEM((16, 128), bf16),
            pltpu.VMEM((total, 16, 128), bf16),
            pltpu.VMEM((9, 3 * wide, wide), bf16),
            pltpu.VMEM((9, 3 * wide, chans), bf16),
            pltpu.SemaphoreType.DMA((7,)),
            pltpu.VMEM((9, 3 * chans, wide), bf16),
            pltpu.VMEM((9, 3 * wide, wide), bf16),
            one, both_ways,
            pltpu.VMEM((3, 3, 2 * chans, 128), f32),
            pltpu.VMEM((2 * chans, 128), f32),
        ]
        + [
            pltpu.VMEM((nx + 2, ny + 2, z, k), bf16)
            for z, k in zip((48, 48, 128, 128), pads)
        ]
        + [
            pltpu.VMEM((nx, ny, 48, 2 * chans), bf16),
            pltpu.VMEM((2, co, nx * ny * 128), bf16),
            rows,
            pltpu.VMEM((chans, 128), f32),
            pltpu.VMEM((2, 9 * chans, 3 * chans), f32),
            pltpu.VMEM((total,) + block, bf16),
            pltpu.VMEM((total,) + block, bf16),
            one, both_ways,
            pltpu.VMEM(features.shape, bf16),
            pltpu.VMEM(features.shape, bf16),
            pltpu.VMEM(w_fine_in.shape, bf16),
            pltpu.VMEM(w_fine_in.shape, bf16),
            pltpu.VMEM((chans, wide), bf16),
            pltpu.SemaphoreType.REGULAR,
            pltpu.VMEM((nx * ny, 48, 4 * wide), f32),
            pltpu.VMEM((nx, 16, 128), bf16),
            pltpu.VMEM((ny * nz, 8, 128), bf16),
            pltpu.VMEM((total, 16, 128), bf16),
            pltpu.VMEM((total, 8, 128), bf16),
            pltpu.SemaphoreType.DMA((2,)),
            both_ways, both_ways,
        ],
        compiler_params=pltpu.CompilerParams(
            collective_id=0, has_side_effects=True, vmem_limit_bytes=ROOMY
        ),
        name="whole",
    )(
        *[
            pltpu.with_memory_space_constraint(value, pltpu.HBM)
            for value in (
                features, cotangent, w_fine_in, w_fine_out,
                w_coarse_in.reshape(9, 3 * chans, wide),
                w_coarse_mid.reshape(9, 3 * wide, wide), w_lift.T,
            )
        ]
    )
    output, grad_input, g_fine_in, g_in, g_mid, g_lift, g_fine_out = pl.pallas_call(
        hand_over,
        out_shape=[shape(value.shape, value.dtype) for value in results],
        in_specs=vmem(7),
        out_specs=[anywhere] * 7,
        scratch_shapes=[pltpu.SemaphoreType.DMA((7,))],
        compiler_params=pltpu.CompilerParams(vmem_limit_bytes=HANDED),
        name="hand_over",
    )(*results)
    return (
        output,
        grad_input,
        g_fine_in.transpose(2, 0, 1),
        g_in.transpose(2, 0, 1),
        g_mid.transpose(0, 2, 1),
        g_lift.T,
        g_fine_out.transpose(2, 0, 1),
    )


def choose(features, *rest):
    nx, ny, nz = (lax.axis_size(axis) for axis in AXES)
    total = nx * ny * nz
    wide = rest[4].shape[0]
    fits = features.shape == (32, 4, 4, 128) and nz == 4 and total <= DIRECT
    fits = fits and 32 % (ny * nz) == 0 and 32 % nx == 0 and 32 // nx == 8 and ny * nz == 8 and wide == 128
    return (shards if fits else shards_layered)(features, *rest)


def solution(mesh):
    whole = P(None, "gx", "gy", "gz")
    split = P(None, "gx", ("gy", "gz"))
    return jax.shard_map(
        choose,
        mesh=mesh,
        in_specs=(whole, whole, P(), P(), P(), P(), P()),
        out_specs=(whole, whole, split, split, split, P("gx", ("gy", "gz")), split),
        check_vma=False,
    )
```

```python
import math

import jax
import jax.numpy as jnp
from jax import lax
from jax.experimental import pallas as pl
from jax.experimental.pallas import tpu as pltpu
from jax.sharding import PartitionSpec as P

AXES = ("gx", "gy", "gz")
MESH = pl.DeviceIdType.MESH
DIRECT = 64


def place(flat, counts):
    nx, ny, nz = counts
    return (flat // (ny * nz), (flat // nz) % ny, flat % nz)


def extended(cells, sides, width):
    for axis, dim in sides:
        count = lax.axis_size(axis)
        ends = count - 1
        head = lax.slice_in_dim(cells, 0, width, axis=dim)
        tail = lax.slice_in_dim(cells, cells.shape[dim] - width, cells.shape[dim], axis=dim)
        cells = jnp.concatenate(
            [
                lax.ppermute(tail, axis, [(i, (i + 1) % count) for i in range(ends)]),
                cells,
                lax.ppermute(head, axis, [((i + 1) % count, i) for i in range(ends)]),
            ],
            axis=dim,
        )
    return cells


def silu_slope(values):
    sigma = jax.nn.sigmoid(values)
    return sigma * (1.0 + values * (1.0 - sigma))


def conv_valid(padded, weight, form="NCDHW"):
    kernel = weight.reshape(3, 3, 3, weight.shape[1], weight.shape[2])
    result = lax.conv_general_dilated(
        padded[None],
        kernel,
        (1, 1, 1),
        "VALID",
        dimension_numbers=(form, "DHWIO", form),
        preferred_element_type=jnp.float32,
    )
    return result[0]


def flipped(weight):
    return jnp.flip(weight, 0).transpose(0, 2, 1)


def pool_blocks(field):
    chans, depth, height, length = field.shape
    grouped = field.astype(jnp.float32).reshape(
        chans, depth // 4, 4, height // 4, 4, length // 4, 4
    )
    return grouped.sum(axis=(2, 4, 6))


def spread_up(field):
    chans, depth, height, length = field.shape
    grown = jnp.broadcast_to(
        field[:, :, None, :, None, :, None], (chans, depth, 4, height, 4, length, 4)
    )
    return grown.reshape(chans, depth * 4, height * 4, length * 4)


def tap_grad_direct(padded, grad):
    depth = padded.shape[1] - 2
    height = padded.shape[2] - 2
    length = padded.shape[3] - 2
    flat_grad = grad.reshape(grad.shape[0], -1)
    blocks = []
    for tap in range(27):
        shift_x, shift_y, shift_z = (tap // 9, tap // 3 % 3, tap % 3)
        window = padded[
            :, shift_x : shift_x + depth, shift_y : shift_y + height, shift_z : shift_z + length
        ].reshape(padded.shape[0], -1)
        blocks.append(
            lax.dot_general(
                window, flat_grad, (((1,), (1,)), ((), ())), preferred_element_type=jnp.float32
            )
        )
    return jnp.stack(blocks)


def fine_rim(field):
    return extended(field, (("gx", 1), ("gy", 2), ("gz", 3)), 1)


def coarse_rim(field):
    return extended(field, (("gx", 1), ("gy", 2), ("gz", 3)), 1)


def reduce_grad(partial_value):
    first = lax.psum_scatter(partial_value, "gx", scatter_dimension=1, tiled=True)
    return lax.psum_scatter(first, ("gy", "gz"), scatter_dimension=2, tiled=True)


def input_share(field):
    parts = lax.all_to_all(field[None], "gx", split_axis=1, concat_axis=0, tiled=True)
    moved = jnp.moveaxis(parts, 0, 1)
    moved = moved.reshape(moved.shape[0], -1, moved.shape[3], moved.shape[4])
    moved = lax.all_gather(moved, "gy", axis=2, tiled=True)
    return lax.all_gather(moved, "gz", axis=3, tiled=True)


def output_share(field):
    parts = lax.all_to_all(field[None], ("gy", "gz"), split_axis=1, concat_axis=0, tiled=True)
    count_y = lax.axis_size("gy")
    count_z = lax.axis_size("gz")
    chans = parts.shape[1]
    depth, height, length = (parts.shape[2], parts.shape[3], parts.shape[4])
    grid = parts.reshape(count_y, count_z, chans, depth, height, length).transpose(2, 3, 0, 4, 1, 5)
    grid = grid.reshape(chans, depth, count_y * height, count_z * length)
    return lax.all_gather(grid, "gx", axis=1, tiled=True)


def shards_layered(features, cotangent, w_fine_in, w_coarse_in, w_coarse_mid, w_lift, w_fine_out):
    depth, height, length = (features.shape[1], features.shape[2], features.shape[3])
    whole_cells = (
        depth * lax.axis_size("gx") * height * lax.axis_size("gy") * length * lax.axis_size("gz")
    )
    scale = 1.0 / math.sqrt(whole_cells)
    padded_in = fine_rim(features)
    z_first = conv_valid(padded_in, w_fine_in)
    act_first = jax.nn.silu(z_first).astype(jnp.bfloat16)
    pooled = (pool_blocks(act_first) / 64.0).astype(jnp.bfloat16)
    pooled_pad = coarse_rim(pooled)
    z_second = conv_valid(pooled_pad, w_coarse_in)
    act_second = jax.nn.silu(z_second).astype(jnp.bfloat16)
    second_pad = coarse_rim(act_second)
    z_third = conv_valid(second_pad, w_coarse_mid)
    act_third = jax.nn.silu(z_third).astype(jnp.bfloat16)
    lifted = lax.dot_general(
        w_lift, act_third, (((0,), (0,)), ((), ())), preferred_element_type=jnp.float32
    )
    joined = (act_first.astype(jnp.float32) + spread_up(lifted)).astype(jnp.bfloat16)
    padded_joined = fine_rim(joined)
    output = conv_valid(padded_joined, w_fine_out).astype(jnp.bfloat16)
    part_fine_out = tap_grad_direct(padded_joined, cotangent) * scale
    d_joined = conv_valid(fine_rim(cotangent), flipped(w_fine_out))
    d_lift = pool_blocks(d_joined)
    lift_partial = (
        lax.dot_general(
            act_third.astype(jnp.float32),
            d_lift,
            (((1, 2, 3), (1, 2, 3)), ((), ())),
            precision=lax.Precision.HIGHEST,
        )
        * scale
    )
    d_third = lax.dot_general(
        w_lift.astype(jnp.float32),
        d_lift,
        (((1,), (0,)), ((), ())),
        precision=lax.Precision.HIGHEST,
    )
    dz_third = (d_third * silu_slope(z_third)).astype(jnp.bfloat16)
    dz_third_pad = coarse_rim(dz_third)
    grad_coarse_mid = None
    sources = input_share(act_second)
    sources_pad = jnp.pad(sources, ((0, 0), (1, 1), (1, 1), (1, 1)))
    targets = output_share(dz_third)
    grad_coarse_mid = tap_grad_direct(sources_pad, targets) * scale
    dz_second = (conv_valid(dz_third_pad, flipped(w_coarse_mid)) * silu_slope(z_second)).astype(
        jnp.bfloat16
    )
    dz_second_pad = coarse_rim(dz_second)
    part_coarse_in = tap_grad_direct(pooled_pad, dz_second) * scale
    d_pool = conv_valid(dz_second_pad, flipped(w_coarse_in))
    dz_first = ((d_joined + spread_up(d_pool) / 64.0) * silu_slope(z_first)).astype(jnp.bfloat16)
    part_fine_in = tap_grad_direct(padded_in, dz_first) * scale
    grad_input = conv_valid(fine_rim(dz_first), flipped(w_fine_in)).astype(jnp.bfloat16)
    pending = [part_fine_out, lift_partial[None], part_coarse_in, part_fine_in]
    reduced = [reduce_grad(partial_value) for partial_value in pending]
    grad_fine_out = reduced[0]
    grad_lift = reduced[1][0]
    grad_coarse_in = reduced[2]
    grad_fine_in = reduced[3]
    return (
        output,
        grad_input,
        grad_fine_in,
        grad_coarse_in,
        grad_coarse_mid,
        grad_lift,
        grad_fine_out,
    )


SIDES = [(i, j, 0) for i in (-1, 0, 1) for j in (-1, 0, 1) if (i, j) != (0, 0)]
SIDES += [(i, j, k) for i in (-1, 0, 1) for j in (-1, 0, 1) for k in (-1, 1)]
ROOMY = 32 * 1024 * 1024
HANDED = 4 * 1024 * 1024


def vmem(count):
    return [pl.BlockSpec(memory_space=pltpu.VMEM)] * count


def slot(i, j, k):
    return ((i + 1) * 3 + j + 1) * 2 + (1 if k > 0 else 0)


def there(counts, side, sign):
    place_of = [lax.axis_index(axis) + sign * step for axis, step in zip(AXES, side)]
    real = True
    for at, count, step in zip(place_of, counts, side):
        if step != 0:
            real = real & (at >= 0) & (at < count)
    return tuple(place_of), real


def swap_copy(counts, n, rows, packed, got, sends, recvs):
    i, j, k = SIDES[n]
    take = {-1: pl.ds(1, 1), 0: pl.ds(1, 4), 1: pl.ds(4, 1)}
    land = {-1: pl.ds(5, 1), 0: pl.ds(1, 4), 1: pl.ds(0, 1)}
    if k == 0:
        source, target = rows.at[take[i], take[j]], rows.at[land[i], land[j]]
    else:
        source, target = packed, got.at[slot(-i, -j, -k)]
    return pltpu.make_async_remote_copy(
        src_ref=source,
        dst_ref=target,
        send_sem=sends.at[n],
        recv_sem=recvs.at[n],
        device_id=there(counts, SIDES[n], 1)[0],
        device_id_type=MESH,
    )


def swap_start(counts, *refs):
    for n in range(len(SIDES)):

        @pl.when(there(counts, SIDES[n], 1)[1])
        def _():
            swap_copy(counts, n, *refs).start()


def swap_finish(counts, *refs):
    for n in range(len(SIDES)):

        @pl.when(there(counts, SIDES[n], -1)[1])
        def _():
            swap_copy(counts, n, *refs).wait_recv()

        @pl.when(there(counts, SIDES[n], 1)[1])
        def _():
            swap_copy(counts, n, *refs).wait_send()


def spot(x, y):
    return (x + 1) * 6 + y + 1


def lanes_of(rows, width=128):
    return lax.broadcasted_iota(jnp.int32, (rows, width), 1)


def clear_rim(rows, got):
    rows[0] = jnp.zeros(rows.shape[1:], rows.dtype)
    rows[5] = jnp.zeros(rows.shape[1:], rows.dtype)
    for x in range(1, 5):
        rows[x, 0] = jnp.zeros(rows.shape[2:], rows.dtype)
        rows[x, 5] = jnp.zeros(rows.shape[2:], rows.dtype)
    got[...] = jnp.zeros_like(got)


def edges(values, x, y, group):
    lane = lanes_of(32)
    place_of = spot(x, y)
    for f, value in enumerate(values):
        turned = pltpu.roll(value, (2 * place_of + 1 + 64 * f) % 128, 1)
        group = jnp.where(lane // 2 == place_of + 32 * f, turned, group)
    return group


def columns(got, f):
    lane = lanes_of(32)
    low = lane % 2 == 1
    at_x, at_y = lane // 12, lane // 2 % 6
    result = jnp.zeros((32, 128), jnp.float32)
    for i in (-1, 0, 1):
        for j in (-1, 0, 1):
            mine = (lane < 72) & (at_x == 0 if i < 0 else at_x == 5 if i > 0 else (at_x > 0) & (at_x < 5))
            mine = mine & (at_y == 0 if j < 0 else at_y == 5 if j > 0 else (at_y > 0) & (at_y < 5))
            for k in (-1, 1):
                turn = (48 * i + 8 * j - 64 * f - k) % 128
                block = pltpu.roll(got[slot(i, j, k)].astype(jnp.float32), turn, 1)
                result = jnp.where(mine & (low if k < 0 else ~low), block, result)
    return result


def column_window(value):
    return jnp.concatenate(
        [
            pltpu.roll(value, (-12 * (a - 1) - 2 * (b - 1)) % 128, 1)
            for a in range(3)
            for b in range(3)
        ]
    ).astype(jnp.bfloat16)


def dot(a, b):
    return jnp.dot(a, b, preferred_element_type=jnp.float32)


def dot_over(a, b, dims, precision=None):
    return lax.dot_general(
        a, b, ((dims[:1], dims[1:]), ((), ())), precision=precision, preferred_element_type=jnp.float32
    )


def ahead(weight):
    size = weight.shape[1]
    taps = weight[...].reshape(9, 3, size, weight.shape[2])
    return jnp.concatenate([taps[:, c].reshape(9 * size, weight.shape[2]).T for c in range(3)])


def back(weight):
    return jnp.concatenate(
        [
            jnp.concatenate([weight[26 - 3 * ab - c] for ab in range(9)], axis=1)
            for c in range(3)
        ]
    )


def near(ref, x, chans):
    return jnp.concatenate(
        [
            jnp.concatenate([ref[x + a, y + b, chans, :] for y in range(4)], axis=1)
            for a in range(3)
            for b in range(3)
        ]
    )


def settle(taps, rim, x):
    lane = lanes_of(32)
    rows = []
    for y in range(4):
        part = taps[:, y * 128 : y * 128 + 128]
        edge = pltpu.roll(rim, (127 - 2 * spot(x, y)) % 128, 1)
        low = jnp.where(lane == 0, edge, pltpu.roll(part[:32], 1, 1))
        high = jnp.where(lane == 127, edge, pltpu.roll(part[64:], 127, 1))
        rows.append(low + part[32:64] + high)
    return rows


def rim_of(weight, window):
    taps = dot(weight, window)
    return jnp.where(lanes_of(32) % 2 == 1, taps[:32], taps[64:])


def thrice(value):
    lane = lax.broadcasted_iota(jnp.int32, value.shape, 1) % 128
    size = value.shape[1]
    value = value.astype(jnp.float32)
    parts = []
    for at in range(0, size, 128):
        part = value[:, at : at + 128]
        spare = lane[:, :128]
        parts.append(
            jnp.concatenate(
                [
                    jnp.where(spare == 127, 0.0, pltpu.roll(part, 127, 1)),
                    part,
                    jnp.where(spare == 0, 0.0, pltpu.roll(part, 1, 1)),
                ]
            )
        )
    return jnp.concatenate(parts, axis=1).astype(jnp.bfloat16)


def thrice_rim(edge):
    low = lanes_of(32) % 2 == 1
    return jnp.concatenate(
        [jnp.where(low, edge, 0.0), jnp.zeros_like(edge), jnp.where(low, 0.0, edge)]
    ).astype(jnp.bfloat16)


def silu_parts(z):
    sigma = jax.nn.sigmoid(z)
    act = (z * sigma).astype(jnp.bfloat16).astype(jnp.float32)
    return act, sigma * (1.0 + z * (1.0 - sigma))


def spread(value, chooser):
    high = value.astype(jnp.bfloat16)
    rest = value - high.astype(jnp.float32)
    middle = rest.astype(jnp.bfloat16)
    low = (rest - middle.astype(jnp.float32)).astype(jnp.bfloat16)
    count = value.shape[0]
    chosen = dot(jnp.concatenate([high, middle, low]), chooser)
    return chosen[:count] + chosen[count : 2 * count] + chosen[2 * count :]


def chooser_of(blocks, step, inner):
    row = lax.broadcasted_iota(jnp.int32, (27 * blocks, 128 * blocks), 0)
    lane = lax.broadcasted_iota(jnp.int32, (27 * blocks, 128 * blocks), 1)
    tap = lane % 128
    ab, c = tap // 3, tap % 3
    source = ab * step + c * inner + lane // 128
    return jnp.where((row == source) & (tap < 27), 1.0, 0.0).astype(jnp.bfloat16)


def whole_kernel(
    counts, scale, fea_far, cot_far, w_in_far, w_out_far, w_in9, w_mid9, w_lift_far,
    out, g_input, g_fine_in, g_in, g_mid, g_lift, g_fine_out,
    one, two, got_one, got_two, pack_one, pack_two, sends_one, recvs_one, sends_two, recvs_two,
    tmp, ws, near_rim, rim_sums, total_ref, mine, full, mid_back, in_back, weight_sems,
    w9, wm9, gather_local, gather_sems,
    grown, grown_rim, pad_in, pad_mid, pad_smid, pad_sin, table, thirds,
    jd, dz_edges, sums, parts, landed, sum_local, sum_sems,
    fea, cot, w_in, w_out, w_lift, ready,
    own_cells, share_a, share_b, land_a, land_b, share_locals, a_sems, b_sems,
):
    nx, ny, nz = counts
    total = nx * ny * nz
    gx, gy, gz = (lax.axis_index(axis) for axis in AXES)
    me = (gx * ny + gy) * nz + gz
    f32, bf16 = jnp.float32, jnp.bfloat16
    pairs = [(fea_far, fea), (cot_far, cot), (w_in_far, w_in), (w_out_far, w_out)]
    pairs += [(w_in9, w9), (w_mid9, wm9), (w_lift_far, w_lift)]
    fetches = [
        pltpu.make_async_copy(source, target, weight_sems.at[n])
        for n, (source, target) in enumerate(pairs)
    ]
    for fetch in fetches:
        fetch.start()
    clear_rim(one, got_one)
    barrier = pltpu.get_barrier_semaphore()

    def tell(semaphore):
        told = 0
        for side in SIDES:
            peer, real = there(counts, side, 1)
            told = told + jnp.where(real, 1, 0)

            @pl.when(real)
            def _():
                pl.semaphore_signal(semaphore, inc=1, device_id=peer, device_id_type=MESH)

        return told

    told = tell(barrier)
    clear_rim(two, got_two)
    fetches[0].wait()
    fetches[1].wait()
    group = jnp.zeros((32, 128), f32)
    for x in range(4):
        tmp[0] = fea[:, x].astype(f32).reshape(128, 128)
        tmp[1] = cot[:, x].astype(f32).reshape(128, 128)
        for y in range(4):
            values = [tmp[f, pl.ds(y, 32, stride=4), :] for f in range(2)]
            one[x + 1, y + 1] = jnp.concatenate(values).astype(bf16)
            group = edges(values, x, y, group)
    pack_one[...] = group.astype(bf16)
    fetches[2].wait()
    fetches[3].wait()
    ws[0], ws[1], ws[2], ws[3] = ahead(w_in), back(w_out), ahead(w_out), back(w_in)
    pl.semaphore_wait(barrier, told)
    first = (counts, one, pack_one, got_one, sends_one, recvs_one)
    swap_start(*first)
    swap_finish(*first)
    tell(ready)

    for f in range(2):
        window = column_window(columns(got_one, f))
        if f == 0:
            near_rim[0] = window
        rim_sums[f] = rim_of(ws[f], window)
    total_ref[...] = jnp.zeros_like(total_ref)
    pack_two[...] = jnp.zeros_like(pack_two)

    def fine(x, carry):
        z = settle(dot(ws[0], near(one, x, slice(0, 32))), rim_sums[0], x)
        d = settle(dot(ws[1], near(one, x, slice(32, 64))), rim_sums[1], x)
        group = pack_two[...].astype(f32)
        acts = jnp.zeros((32, 128), f32)
        for y in range(4):
            two[x + 1, y + 1] = jnp.concatenate([z[y], d[y]]).astype(bf16)
            group = edges([z[y], d[y]], x, y, group)
            acts = acts + silu_parts(z[y])[0]
        pack_two[...] = group.astype(bf16)
        total_ref[...] += jnp.concatenate([acts, d[0] + d[1] + d[2] + d[3]])
        return carry

    lax.fori_loop(0, 4, fine, 0)
    row = lax.broadcasted_iota(jnp.int32, (32, 128), 0)
    pick_cell = jnp.where(lanes_of(32) // 4 == row, 1.0, 0.0)
    means = dot_over(pick_cell, total_ref[...], (1, 1), lax.Precision.HIGHEST)
    both = jnp.concatenate([means[:, :32] * (1.0 / 64.0), means[:, 32:]], axis=1)
    mine[...] = jnp.concatenate([both[:16], both[16:]], axis=1).astype(bf16)

    lines = [
        [at] + [lax.rem(at + k, count) for k in range(1, count)]
        for at, count in zip((gx, gy, gz), counts)
    ]

    def send_all(source, target, sems):
        for x in reversed(range(nx)):
            for y in reversed(range(ny)):
                for z in reversed(range(nz)):
                    if x + y + z > 0:
                        peer = (lines[0][x], lines[1][y], lines[2][z])
                        pltpu.make_async_remote_copy(
                            src_ref=source(peer[0], peer[1] * nz + peer[2]),
                            dst_ref=target.at[me],
                            send_sem=sems.at[0],
                            recv_sem=sems.at[1],
                            device_id=peer,
                            device_id_type=MESH,
                        ).start()

    def wait_all(target, sems):
        everyone_else = target.at[pl.ds(0, total - 1)]
        for n in range(2):
            pltpu.make_async_copy(everyone_else, everyone_else, sems.at[n]).wait()

    pl.semaphore_wait(ready, told)
    send_all(lambda x, o: mine, full, gather_sems)
    own = pltpu.make_async_copy(mine, full.at[me], gather_local)
    own.start()
    second = (counts, two, pack_two, got_two, sends_two, recvs_two)
    swap_start(*second)

    for fetch in fetches[4:]:
        fetch.wait()
    wide, narrow = w9.shape[2], in_back.shape[2]

    def turn(ab, carry):
        for c in range(3):
            rows = slice(c * wide, c * wide + wide)
            mid_back[ab, rows, :] = wm9[8 - ab, (2 - c) * wide : (3 - c) * wide, :].T
            in_back[ab, rows, :] = w9[8 - ab, (2 - c) * narrow : (3 - c) * narrow, :].T
        return carry

    lax.fori_loop(0, 9, turn, 0)
    for pad in (pad_in, pad_mid, pad_smid, pad_sin):
        pad[...] = jnp.zeros_like(pad)
    own.wait()
    wait_all(full, gather_sems)

    span = 48
    cells = nx * ny * span

    def pick(size, pieces, index):
        each = size // pieces
        row = lax.broadcasted_iota(jnp.int32, (size, each), 0)
        column = lax.broadcasted_iota(jnp.int32, (size, each), 1)
        return jnp.where(row == index * each + column, 1.0, 0.0).astype(bf16)

    at_o = gy * nz + gz

    def fill(pad, value):
        rows, size = value.shape[0], pad.shape[2]
        at = lax.broadcasted_iota(jnp.int32, value.shape, 0) % size
        low = jnp.where(at == 0, 0.0, pltpu.roll(value, 1, 0))
        high = jnp.where(at == size - 1, 0.0, pltpu.roll(value, rows - 1, 0))
        wide = jnp.concatenate([low, value, high], axis=1).astype(bf16)
        pad[1 : nx + 1, 1 : ny + 1] = wide.reshape(nx, ny, size, wide.shape[1])

    def window(pad, ab):
        a, b = ab // 3, ab % 3
        return pad[a : a + nx, b : b + ny].reshape(nx * ny * pad.shape[2], pad.shape[3])

    def conv(pad, weight):
        result = dot(window(pad, 0), weight[0])
        for ab in range(1, 9):
            result = result + dot(window(pad, ab), weight[ab])
        return result

    def slope(v):
        sigma = jax.nn.sigmoid(v)
        return sigma * (1.0 + v * (1.0 - sigma))

    before, after = jnp.maximum(gz - 1, 0), jnp.minimum(gz + 1, nz - 1)
    pieces = []
    for k in range(nx * ny):
        here = full[k * nz + gz].astype(f32)
        pieces += [full[k * nz + before].astype(f32)[8:, 64:], here[:, :64], here[:, 64:]]
        pieces += [full[k * nz + after].astype(f32)[:8, :64]]
    at_z = lax.broadcasted_iota(jnp.int32, (cells, 128), 0) % span + gz * 32 - 8
    keep = jnp.where((at_z >= 0) & (at_z < nz * 32), 1.0, 0.0)
    both = jnp.concatenate(pieces) * keep[:, :64]
    fill(pad_in, both[:, :32])
    z_second = conv(pad_in, w9)
    act_second = jax.nn.silu(z_second) * keep
    fill(pad_mid, act_second)
    z_third = conv(pad_mid, wm9)
    act_third = jax.nn.silu(z_third)
    lifted = dot(act_third.astype(bf16), w_lift[...].T)
    dz_third = dot(both[:, 32:].astype(bf16), w_lift[...]) * slope(z_third) * keep
    fill(pad_mid, dz_third)
    dz_second = conv(pad_mid, mid_back) * slope(z_second) * keep
    fill(pad_mid, dz_second)
    d_pool = conv(pad_mid, in_back)
    table[...] = (
        jnp.concatenate([lifted, d_pool * (1.0 / 64.0)], axis=1)
        .astype(bf16)
        .reshape(nx, ny, span, 64)
    )
    for n, value in enumerate([act_second, act_third, dz_third, dz_second]):
        own_cells[:, :, n * 128 : n * 128 + 128] = value.reshape(nx * ny, span, 128)
    mine_now = own_cells[gx * ny + gy, 8:40, :]
    wx, wo = 128 // nx, 128 // (ny * nz)
    for i in range(nx):
        block = jnp.concatenate(
            [mine_now[:, n * 128 + i * wx : n * 128 + i * wx + wx] for n in (0, 1)], axis=1
        )
        share_a[i] = jnp.concatenate([block[:16], block[16:]], axis=1).astype(bf16)
    for i in range(ny * nz):
        block = jnp.concatenate(
            [mine_now[:, n * 128 + i * wo : n * 128 + i * wo + wo] for n in (2, 3)], axis=1
        )
        share_b[i] = jnp.concatenate(
            [block[8 * q : 8 * q + 8] for q in range(4)], axis=1
        ).astype(bf16)

    row = lax.broadcasted_iota(jnp.int32, (span, 128), 0)
    lane = lanes_of(span)
    grow = jnp.where(row == lane // 4 + 8, 1.0, 0.0).astype(bf16)
    past = 8 + jnp.where(lane % 2 == 1, -1, 32)
    at_x, at_y = lane // 12, lane // 2 % 6
    rim = jnp.zeros((64, 128), f32)
    for i in range(3):
        for j in range(3):
            x = jnp.clip(gx + i - 1, 0, nx - 1)
            y = jnp.clip(gy + j - 1, 0, ny - 1)
            grown[i, j] = dot_over(table[x, y], grow, (0, 0))
            mine_too = ((at_x + 3) // 4 == i) & ((at_y + 3) // 4 == j) & (lane < 72)
            far = jnp.where((row == past) & mine_too, 1.0, 0.0).astype(bf16)
            rim = rim + dot_over(table[x, y], far, (0, 0))
    send_all(lambda x, o: share_a.at[x], land_a, a_sems)
    send_all(lambda x, o: share_b.at[o], land_b, b_sems)
    owns = [
        pltpu.make_async_copy(share_a.at[gx], land_a.at[me], share_locals.at[0]),
        pltpu.make_async_copy(share_b.at[at_o], land_b.at[me], share_locals.at[1]),
    ]
    for copy in owns:
        copy.start()
    swap_finish(*second)

    lane = lanes_of(32)
    at_x, at_y = gx * 4 + lane // 12 - 1, gy * 4 + lane // 2 % 6 - 1
    real = (at_x >= 0) & (at_x < nx * 4) & (at_y >= 0) & (at_y < ny * 4) & (lane < 72)
    reach = gz + jnp.where(lane % 2 == 1, -1, 1)
    real = real & (reach >= 0) & (reach < nz)
    act, bend = silu_parts(columns(got_two, 0))
    near_rim[1] = column_window(jnp.where(real, act + rim[:32], 0.0))
    near_rim[2] = column_window(jnp.where(real, (columns(got_two, 1) + rim[32:]) * bend, 0.0))
    rim_sums[0] = rim_of(ws[2], near_rim[1])
    rim_sums[1] = rim_of(ws[3], near_rim[2])
    dz_edges[...] = jnp.zeros_like(dz_edges)

    def join(x, carry):
        group = dz_edges[...]
        for y in range(6):
            at_x, at_y = gx * 4 + x - 1, gy * 4 + y - 1
            real = (at_x >= 0) & (at_x < nx * 4) & (at_y >= 0) & (at_y < ny * 4)
            keep = jnp.where(real, 1.0, 0.0)
            up = grown[(x + 3) // 4, (y + 3) // 4]
            both = two[x, y].astype(f32)
            act, bend = silu_parts(both[:32])
            joined = (act + up[:32]) * keep
            dz = (both[32:] + up[32:]) * bend * keep
            jd[x, y] = jnp.concatenate([joined, dz]).astype(bf16)
            if 1 <= y <= 4:
                here = jnp.where((x >= 1) & (x <= 4), x * 6 + y, -1)
                turned = pltpu.roll(dz, (12 * x + 2 * y + 1) % 128, 1)
                group = jnp.where(lanes_of(32) // 2 == here, turned, group)
        dz_edges[...] = group
        return carry

    lax.fori_loop(0, 6, join, 0)
    ends = pltpu.roll(pack_one[...].astype(f32), 64, 1)
    ends = jnp.where(lanes_of(32) < 64, ends, 0.0)
    sums[0] = dot_over(near_rim[1], thrice_rim(ends), (1, 1))
    sums[1] = dot_over(near_rim[0], thrice_rim(dz_edges[...]), (1, 1))

    def last(x, carry):
        joined = near(jd, x, slice(0, 32))
        rows = settle(dot(ws[2], joined), rim_sums[0], x)
        for y in range(4):
            tmp[0, pl.ds(y, 32, stride=4), :] = rows[y]
        out[:, x] = tmp[0].reshape(32, 4, 128).astype(bf16)
        given = [one[x + 1, y + 1, 32:64, :] for y in range(4)]
        sums[0] += dot_over(joined, thrice(jnp.concatenate(given, axis=1)), (1, 1))
        rows = settle(dot(ws[3], near(jd, x, slice(32, 64))), rim_sums[1], x)
        for y in range(4):
            tmp[1, pl.ds(y, 32, stride=4), :] = rows[y]
        g_input[:, x] = tmp[1].reshape(32, 4, 128).astype(bf16)
        given = [jd[x + 1, y + 1, 32:64, :] for y in range(4)]
        sums[1] += dot_over(
            near(one, x, slice(0, 32)), thrice(jnp.concatenate(given, axis=1)), (1, 1)
        )
        return carry

    lax.fori_loop(0, 4, last, 0)
    ci, co = 32 // nx, 32 // (ny * nz)
    for f in range(2):
        value = sums[f].reshape(9, nx, ci, 96)
        for i in range(nx):
            turned = value[:, i].reshape(9 * ci, 96).T
            block = jnp.concatenate([turned[:32], turned[32:64], turned[64:]], axis=1)
            for j in range(ny * nz):
                parts[i * ny * nz + j, f * co : f * co + co, :] = block[
                    j * co : j * co + co
                ].astype(bf16)
    send_all(lambda x, o: parts.at[x * (ny * nz) + o], landed, sum_sems)
    own = pltpu.make_async_copy(parts.at[me], landed.at[me], sum_local)
    own.start()

    for copy in owns:
        copy.wait()
    wait_all(land_a, a_sems)
    wait_all(land_b, b_sems)
    pieces, firsts, seconds = [], [], []
    for k in range(total):
        block = full[k]
        pieces += [block[:, :64], block[:, 64:]]
        block = land_a[k].astype(f32)
        firsts += [block[:, :64], block[:, 64:]]
        block = land_b[k].astype(f32)
        seconds += [block[:, 32 * q : 32 * q + 32] for q in range(4)]
    both = jnp.concatenate(pieces)
    pooled, d_lift = both[:, :32], both[:, 32:]
    acts = jnp.concatenate(firsts)
    fill(pad_smid, acts[:, :32])
    fill(pad_sin, dot(pooled, pick(32, nx, gx)))
    turned = jnp.concatenate(seconds).T.astype(bf16)
    thirds[0], thirds[1] = turned[:16], turned[16:]
    lift_o = dot(d_lift, pick(32, ny * nz, at_o)).T.astype(bf16)
    g_lift[...] = dot(lift_o, acts[:, 32:].astype(bf16)) * scale
    taken = []
    for ab in range(9):
        grad = dot(thirds[0], window(pad_smid, ab)) * scale
        share = grad.shape[1] // 3
        for c in range(3):
            g_mid[3 * ab + c] = grad[:, c * share : c * share + share]
        taken.append(dot(thirds[1], window(pad_sin, ab)) * scale)
    chosen = spread(jnp.concatenate(taken, axis=1), chooser_of(ci, 3 * ci, ci))
    for i in range(ci):
        g_in[i] = chosen[:, i * 128 : i * 128 + 27]
    chooser = chooser_of(ci, ci, 9 * ci)
    own.wait()
    wait_all(landed, sum_sems)
    chosen = spread(landed[...].astype(f32).sum(0) * scale, chooser)
    for i in range(ci):
        g_fine_out[i] = chosen[:co, i * 128 : i * 128 + 27]
        g_fine_in[i] = chosen[co:, i * 128 : i * 128 + 27]


def hand_over(*refs):
    *refs, sems = refs
    half = len(refs) // 2
    copies = [
        pltpu.make_async_copy(source, target, sems.at[n])
        for n, (source, target) in enumerate(zip(refs[:half], refs[half:]))
    ]
    for copy in copies:
        copy.start()
    for copy in copies:
        copy.wait()


def shards(features, cotangent, w_fine_in, w_coarse_in, w_coarse_mid, w_lift, w_fine_out):
    counts = tuple(lax.axis_size(axis) for axis in AXES)
    nx, ny, nz = counts
    total = nx * ny * nz
    chans, depth, height, length = features.shape
    wide = w_lift.shape[0]
    scale = 1.0 / math.sqrt(total * depth * height * length)
    f32, bf16 = jnp.float32, jnp.bfloat16
    shape = jax.ShapeDtypeStruct
    co, cw = wide // (ny * nz), wide // nx
    ci, fo = chans // nx, chans // (ny * nz)
    pads = [3 * chans, 3 * wide, 3 * cw, 3 * ci]
    block = (2 * fo, 27 * ci)
    rows = pltpu.VMEM((6, 6, 2 * chans, 128), bf16)
    got = pltpu.VMEM((18, chans, 128), bf16)
    packed = pltpu.VMEM((chans, 128), bf16)
    swaps = pltpu.SemaphoreType.DMA((len(SIDES),))
    one, both_ways = pltpu.SemaphoreType.DMA, pltpu.SemaphoreType.DMA((2,))
    anywhere = pl.BlockSpec(memory_space=pl.ANY)
    results = pl.pallas_call(
        lambda *refs: whole_kernel(counts, scale, *refs),
        out_shape=(
            shape(features.shape, bf16),
            shape(features.shape, bf16),
            shape((ci, fo, 27), f32),
            shape((ci, co, 27), f32),
            shape((27, co, cw), f32),
            shape((fo, cw), f32),
            shape((ci, fo, 27), f32),
        ),
        in_specs=[pl.BlockSpec(memory_space=pltpu.HBM)] * 7,
        out_specs=vmem(7),
        scratch_shapes=[
            rows, rows, got, got, packed, packed, swaps, swaps, swaps, swaps,
            pltpu.VMEM((2, 128, 128), f32),
            pltpu.VMEM((4, 3 * chans, 9 * chans), bf16),
            pltpu.VMEM((3, 9 * chans, 128), bf16),
            pltpu.VMEM((2, chans, 128), f32),
            pltpu.VMEM((2 * chans, 128), f32),
            pltpu.VMEM((16, 128), bf16),
            pltpu.VMEM((total, 16, 128), bf16),
            pltpu.VMEM((9, 3 * wide, wide), bf16),
            pltpu.VMEM((9, 3 * wide, chans), bf16),
            pltpu.SemaphoreType.DMA((7,)),
            pltpu.VMEM((9, 3 * chans, wide), bf16),
            pltpu.VMEM((9, 3 * wide, wide), bf16),
            one, both_ways,
            pltpu.VMEM((3, 3, 2 * chans, 128), f32),
            pltpu.VMEM((2 * chans, 128), f32),
        ]
        + [
            pltpu.VMEM((nx + 2, ny + 2, z, k), bf16)
            for z, k in zip((48, 48, 128, 128), pads)
        ]
        + [
            pltpu.VMEM((nx, ny, 48, 2 * chans), bf16),
            pltpu.VMEM((2, co, nx * ny * 128), bf16),
            rows,
            pltpu.VMEM((chans, 128), f32),
            pltpu.VMEM((2, 9 * chans, 3 * chans), f32),
            pltpu.VMEM((total,) + block, bf16),
            pltpu.VMEM((total,) + block, bf16),
            one, both_ways,
            pltpu.VMEM(features.shape, bf16),
            pltpu.VMEM(features.shape, bf16),
            pltpu.VMEM(w_fine_in.shape, bf16),
            pltpu.VMEM(w_fine_in.shape, bf16),
            pltpu.VMEM((chans, wide), bf16),
            pltpu.SemaphoreType.REGULAR,
            pltpu.VMEM((nx * ny, 48, 4 * wide), f32),
            pltpu.VMEM((nx, 16, 128), bf16),
            pltpu.VMEM((ny * nz, 8, 128), bf16),
            pltpu.VMEM((total, 16, 128), bf16),
            pltpu.VMEM((total, 8, 128), bf16),
            pltpu.SemaphoreType.DMA((2,)),
            both_ways, both_ways,
        ],
        compiler_params=pltpu.CompilerParams(
            collective_id=0, has_side_effects=True, vmem_limit_bytes=ROOMY
        ),
        name="whole",
    )(
        *[
            pltpu.with_memory_space_constraint(value, pltpu.HBM)
            for value in (
                features, cotangent, w_fine_in, w_fine_out,
                w_coarse_in.reshape(9, 3 * chans, wide),
                w_coarse_mid.reshape(9, 3 * wide, wide), w_lift.T,
            )
        ]
    )
    output, grad_input, g_fine_in, g_in, g_mid, g_lift, g_fine_out = pl.pallas_call(
        hand_over,
        out_shape=[shape(value.shape, value.dtype) for value in results],
        in_specs=vmem(7),
        out_specs=[anywhere] * 7,
        scratch_shapes=[pltpu.SemaphoreType.DMA((7,))],
        compiler_params=pltpu.CompilerParams(vmem_limit_bytes=HANDED),
        name="hand_over",
    )(*results)
    return (
        output,
        grad_input,
        g_fine_in.transpose(2, 0, 1),
        g_in.transpose(2, 0, 1),
        g_mid.transpose(0, 2, 1),
        g_lift.T,
        g_fine_out.transpose(2, 0, 1),
    )


def choose(features, *rest):
    nx, ny, nz = (lax.axis_size(axis) for axis in AXES)
    total = nx * ny * nz
    wide = rest[4].shape[0]
    fits = features.shape == (32, 4, 4, 128) and nz == 4 and total <= DIRECT
    fits = fits and 32 % (ny * nz) == 0 and 32 % nx == 0 and 32 // nx == 8 and ny * nz == 8 and wide == 128
    return (shards if fits else shards_layered)(features, *rest)


def solution(mesh):
    whole = P(None, "gx", "gy", "gz")
    split = P(None, "gx", ("gy", "gz"))
    return jax.shard_map(
        choose,
        mesh=mesh,
        in_specs=(whole, whole, P(), P(), P(), P(), P()),
        out_specs=(whole, whole, split, split, split, P("gx", ("gy", "gz")), split),
        check_vma=False,
    )
```

```python
import math

import jax
import jax.numpy as jnp
from jax import lax
from jax.experimental import pallas as pl
from jax.experimental.pallas import tpu as pltpu
from jax.sharding import PartitionSpec as P

AXES = ("gx", "gy", "gz")
MESH = pl.DeviceIdType.MESH
DIRECT = 64


def place(flat, counts):
    nx, ny, nz = counts
    return (flat // (ny * nz), (flat // nz) % ny, flat % nz)


def extended(cells, sides, width):
    for axis, dim in sides:
        count = lax.axis_size(axis)
        ends = count - 1
        head = lax.slice_in_dim(cells, 0, width, axis=dim)
        tail = lax.slice_in_dim(cells, cells.shape[dim] - width, cells.shape[dim], axis=dim)
        cells = jnp.concatenate(
            [
                lax.ppermute(tail, axis, [(i, (i + 1) % count) for i in range(ends)]),
                cells,
                lax.ppermute(head, axis, [((i + 1) % count, i) for i in range(ends)]),
            ],
            axis=dim,
        )
    return cells


def silu_slope(values):
    sigma = jax.nn.sigmoid(values)
    return sigma * (1.0 + values * (1.0 - sigma))


def conv_valid(padded, weight, form="NCDHW"):
    kernel = weight.reshape(3, 3, 3, weight.shape[1], weight.shape[2])
    result = lax.conv_general_dilated(
        padded[None],
        kernel,
        (1, 1, 1),
        "VALID",
        dimension_numbers=(form, "DHWIO", form),
        preferred_element_type=jnp.float32,
    )
    return result[0]


def flipped(weight):
    return jnp.flip(weight, 0).transpose(0, 2, 1)


def pool_blocks(field):
    chans, depth, height, length = field.shape
    grouped = field.astype(jnp.float32).reshape(
        chans, depth // 4, 4, height // 4, 4, length // 4, 4
    )
    return grouped.sum(axis=(2, 4, 6))


def spread_up(field):
    chans, depth, height, length = field.shape
    grown = jnp.broadcast_to(
        field[:, :, None, :, None, :, None], (chans, depth, 4, height, 4, length, 4)
    )
    return grown.reshape(chans, depth * 4, height * 4, length * 4)


def tap_grad_direct(padded, grad):
    depth = padded.shape[1] - 2
    height = padded.shape[2] - 2
    length = padded.shape[3] - 2
    flat_grad = grad.reshape(grad.shape[0], -1)
    blocks = []
    for tap in range(27):
        shift_x, shift_y, shift_z = (tap // 9, tap // 3 % 3, tap % 3)
        window = padded[
            :, shift_x : shift_x + depth, shift_y : shift_y + height, shift_z : shift_z + length
        ].reshape(padded.shape[0], -1)
        blocks.append(
            lax.dot_general(
                window, flat_grad, (((1,), (1,)), ((), ())), preferred_element_type=jnp.float32
            )
        )
    return jnp.stack(blocks)


def fine_rim(field):
    return extended(field, (("gx", 1), ("gy", 2), ("gz", 3)), 1)


def coarse_rim(field):
    return extended(field, (("gx", 1), ("gy", 2), ("gz", 3)), 1)


def reduce_grad(partial_value):
    first = lax.psum_scatter(partial_value, "gx", scatter_dimension=1, tiled=True)
    return lax.psum_scatter(first, ("gy", "gz"), scatter_dimension=2, tiled=True)


def input_share(field):
    parts = lax.all_to_all(field[None], "gx", split_axis=1, concat_axis=0, tiled=True)
    moved = jnp.moveaxis(parts, 0, 1)
    moved = moved.reshape(moved.shape[0], -1, moved.shape[3], moved.shape[4])
    moved = lax.all_gather(moved, "gy", axis=2, tiled=True)
    return lax.all_gather(moved, "gz", axis=3, tiled=True)


def output_share(field):
    parts = lax.all_to_all(field[None], ("gy", "gz"), split_axis=1, concat_axis=0, tiled=True)
    count_y = lax.axis_size("gy")
    count_z = lax.axis_size("gz")
    chans = parts.shape[1]
    depth, height, length = (parts.shape[2], parts.shape[3], parts.shape[4])
    grid = parts.reshape(count_y, count_z, chans, depth, height, length).transpose(2, 3, 0, 4, 1, 5)
    grid = grid.reshape(chans, depth, count_y * height, count_z * length)
    return lax.all_gather(grid, "gx", axis=1, tiled=True)


def shards_layered(features, cotangent, w_fine_in, w_coarse_in, w_coarse_mid, w_lift, w_fine_out):
    depth, height, length = (features.shape[1], features.shape[2], features.shape[3])
    whole_cells = (
        depth * lax.axis_size("gx") * height * lax.axis_size("gy") * length * lax.axis_size("gz")
    )
    scale = 1.0 / math.sqrt(whole_cells)
    padded_in = fine_rim(features)
    z_first = conv_valid(padded_in, w_fine_in)
    act_first = jax.nn.silu(z_first).astype(jnp.bfloat16)
    pooled = (pool_blocks(act_first) / 64.0).astype(jnp.bfloat16)
    pooled_pad = coarse_rim(pooled)
    z_second = conv_valid(pooled_pad, w_coarse_in)
    act_second = jax.nn.silu(z_second).astype(jnp.bfloat16)
    second_pad = coarse_rim(act_second)
    z_third = conv_valid(second_pad, w_coarse_mid)
    act_third = jax.nn.silu(z_third).astype(jnp.bfloat16)
    lifted = lax.dot_general(
        w_lift, act_third, (((0,), (0,)), ((), ())), preferred_element_type=jnp.float32
    )
    joined = (act_first.astype(jnp.float32) + spread_up(lifted)).astype(jnp.bfloat16)
    padded_joined = fine_rim(joined)
    output = conv_valid(padded_joined, w_fine_out).astype(jnp.bfloat16)
    part_fine_out = tap_grad_direct(padded_joined, cotangent) * scale
    d_joined = conv_valid(fine_rim(cotangent), flipped(w_fine_out))
    d_lift = pool_blocks(d_joined)
    lift_partial = (
        lax.dot_general(
            act_third.astype(jnp.float32),
            d_lift,
            (((1, 2, 3), (1, 2, 3)), ((), ())),
            precision=lax.Precision.HIGHEST,
        )
        * scale
    )
    d_third = lax.dot_general(
        w_lift.astype(jnp.float32),
        d_lift,
        (((1,), (0,)), ((), ())),
        precision=lax.Precision.HIGHEST,
    )
    dz_third = (d_third * silu_slope(z_third)).astype(jnp.bfloat16)
    dz_third_pad = coarse_rim(dz_third)
    grad_coarse_mid = None
    sources = input_share(act_second)
    sources_pad = jnp.pad(sources, ((0, 0), (1, 1), (1, 1), (1, 1)))
    targets = output_share(dz_third)
    grad_coarse_mid = tap_grad_direct(sources_pad, targets) * scale
    dz_second = (conv_valid(dz_third_pad, flipped(w_coarse_mid)) * silu_slope(z_second)).astype(
        jnp.bfloat16
    )
    dz_second_pad = coarse_rim(dz_second)
    part_coarse_in = tap_grad_direct(pooled_pad, dz_second) * scale
    d_pool = conv_valid(dz_second_pad, flipped(w_coarse_in))
    dz_first = ((d_joined + spread_up(d_pool) / 64.0) * silu_slope(z_first)).astype(jnp.bfloat16)
    part_fine_in = tap_grad_direct(padded_in, dz_first) * scale
    grad_input = conv_valid(fine_rim(dz_first), flipped(w_fine_in)).astype(jnp.bfloat16)
    pending = [part_fine_out, lift_partial[None], part_coarse_in, part_fine_in]
    reduced = [reduce_grad(partial_value) for partial_value in pending]
    grad_fine_out = reduced[0]
    grad_lift = reduced[1][0]
    grad_coarse_in = reduced[2]
    grad_fine_in = reduced[3]
    return (
        output,
        grad_input,
        grad_fine_in,
        grad_coarse_in,
        grad_coarse_mid,
        grad_lift,
        grad_fine_out,
    )


SIDES = [(i, j, 0) for i in (-1, 0, 1) for j in (-1, 0, 1) if (i, j) != (0, 0)]
SIDES += [(i, j, k) for i in (-1, 0, 1) for j in (-1, 0, 1) for k in (-1, 1)]
ROOMY = 32 * 1024 * 1024
HANDED = 4 * 1024 * 1024


def vmem(count):
    return [pl.BlockSpec(memory_space=pltpu.VMEM)] * count


def slot(i, j, k):
    return ((i + 1) * 3 + j + 1) * 2 + (1 if k > 0 else 0)


def there(counts, side, sign):
    place_of = [lax.axis_index(axis) + sign * step for axis, step in zip(AXES, side)]
    real = True
    for at, count, step in zip(place_of, counts, side):
        if step != 0:
            real = real & (at >= 0) & (at < count)
    return tuple(place_of), real


def swap_copy(counts, n, rows, packed, got, sends, recvs):
    i, j, k = SIDES[n]
    take = {-1: pl.ds(1, 1), 0: pl.ds(1, 4), 1: pl.ds(4, 1)}
    land = {-1: pl.ds(5, 1), 0: pl.ds(1, 4), 1: pl.ds(0, 1)}
    if k == 0:
        source, target = rows.at[take[i], take[j]], rows.at[land[i], land[j]]
    else:
        source, target = packed, got.at[slot(-i, -j, -k)]
    return pltpu.make_async_remote_copy(
        src_ref=source,
        dst_ref=target,
        send_sem=sends.at[n],
        recv_sem=recvs.at[n],
        device_id=there(counts, SIDES[n], 1)[0],
        device_id_type=MESH,
    )


def swap_start(counts, *refs):
    for n in range(len(SIDES)):

        @pl.when(there(counts, SIDES[n], 1)[1])
        def _():
            swap_copy(counts, n, *refs).start()


def swap_finish(counts, *refs):
    for n in range(len(SIDES)):

        @pl.when(there(counts, SIDES[n], -1)[1])
        def _():
            swap_copy(counts, n, *refs).wait_recv()

        @pl.when(there(counts, SIDES[n], 1)[1])
        def _():
            swap_copy(counts, n, *refs).wait_send()


def spot(x, y):
    return (x + 1) * 6 + y + 1


def lanes_of(rows, width=128):
    return lax.broadcasted_iota(jnp.int32, (rows, width), 1)


def clear_rim(rows, got):
    rows[0] = jnp.zeros(rows.shape[1:], rows.dtype)
    rows[5] = jnp.zeros(rows.shape[1:], rows.dtype)
    for x in range(1, 5):
        rows[x, 0] = jnp.zeros(rows.shape[2:], rows.dtype)
        rows[x, 5] = jnp.zeros(rows.shape[2:], rows.dtype)
    got[...] = jnp.zeros_like(got)


def edges(values, x, y, group):
    lane = lanes_of(32)
    place_of = spot(x, y)
    for f, value in enumerate(values):
        turned = pltpu.roll(value, (2 * place_of + 1 + 64 * f) % 128, 1)
        group = jnp.where(lane // 2 == place_of + 32 * f, turned, group)
    return group


def columns(got, f):
    lane = lanes_of(32)
    low = lane % 2 == 1
    at_x, at_y = lane // 12, lane // 2 % 6
    result = jnp.zeros((32, 128), jnp.float32)
    for i in (-1, 0, 1):
        for j in (-1, 0, 1):
            mine = (lane < 72) & (at_x == 0 if i < 0 else at_x == 5 if i > 0 else (at_x > 0) & (at_x < 5))
            mine = mine & (at_y == 0 if j < 0 else at_y == 5 if j > 0 else (at_y > 0) & (at_y < 5))
            for k in (-1, 1):
                turn = (48 * i + 8 * j - 64 * f - k) % 128
                block = pltpu.roll(got[slot(i, j, k)].astype(jnp.float32), turn, 1)
                result = jnp.where(mine & (low if k < 0 else ~low), block, result)
    return result


def column_window(value):
    return jnp.concatenate(
        [
            pltpu.roll(value, (-12 * (a - 1) - 2 * (b - 1)) % 128, 1)
            for a in range(3)
            for b in range(3)
        ]
    ).astype(jnp.bfloat16)


def dot(a, b):
    return jnp.dot(a, b, preferred_element_type=jnp.float32)


def dot_over(a, b, dims, precision=None):
    return lax.dot_general(
        a, b, ((dims[:1], dims[1:]), ((), ())), precision=precision, preferred_element_type=jnp.float32
    )


def ahead(weight):
    size = weight.shape[1]
    taps = weight[...].reshape(9, 3, size, weight.shape[2])
    return jnp.concatenate([taps[:, c].reshape(9 * size, weight.shape[2]).T for c in range(3)])


def back(weight):
    return jnp.concatenate(
        [
            jnp.concatenate([weight[26 - 3 * ab - c] for ab in range(9)], axis=1)
            for c in range(3)
        ]
    )


def near(ref, x, chans):
    return jnp.concatenate(
        [
            jnp.concatenate([ref[x + a, y + b, chans, :] for y in range(4)], axis=1)
            for a in range(3)
            for b in range(3)
        ]
    )


def settle(taps, rim, x):
    lane = lanes_of(32)
    rows = []
    for y in range(4):
        part = taps[:, y * 128 : y * 128 + 128]
        edge = pltpu.roll(rim, (127 - 2 * spot(x, y)) % 128, 1)
        low = jnp.where(lane == 0, edge, pltpu.roll(part[:32], 1, 1))
        high = jnp.where(lane == 127, edge, pltpu.roll(part[64:], 127, 1))
        rows.append(low + part[32:64] + high)
    return rows


def rim_of(weight, window):
    taps = dot(weight, window)
    return jnp.where(lanes_of(32) % 2 == 1, taps[:32], taps[64:])


def thrice(value):
    lane = lax.broadcasted_iota(jnp.int32, value.shape, 1) % 128
    size = value.shape[1]
    value = value.astype(jnp.float32)
    parts = []
    for at in range(0, size, 128):
        part = value[:, at : at + 128]
        spare = lane[:, :128]
        parts.append(
            jnp.concatenate(
                [
                    jnp.where(spare == 127, 0.0, pltpu.roll(part, 127, 1)),
                    part,
                    jnp.where(spare == 0, 0.0, pltpu.roll(part, 1, 1)),
                ]
            )
        )
    return jnp.concatenate(parts, axis=1).astype(jnp.bfloat16)


def thrice_rim(edge):
    low = lanes_of(32) % 2 == 1
    return jnp.concatenate(
        [jnp.where(low, edge, 0.0), jnp.zeros_like(edge), jnp.where(low, 0.0, edge)]
    ).astype(jnp.bfloat16)


def silu_parts(z):
    sigma = jax.nn.sigmoid(z)
    act = (z * sigma).astype(jnp.bfloat16).astype(jnp.float32)
    return act, sigma * (1.0 + z * (1.0 - sigma))


def spread(value, chooser):
    high = value.astype(jnp.bfloat16)
    rest = value - high.astype(jnp.float32)
    middle = rest.astype(jnp.bfloat16)
    low = (rest - middle.astype(jnp.float32)).astype(jnp.bfloat16)
    count = value.shape[0]
    chosen = dot(jnp.concatenate([high, middle, low]), chooser)
    return chosen[:count] + chosen[count : 2 * count] + chosen[2 * count :]


def chooser_of(blocks, step, inner):
    row = lax.broadcasted_iota(jnp.int32, (27 * blocks, 128 * blocks), 0)
    lane = lax.broadcasted_iota(jnp.int32, (27 * blocks, 128 * blocks), 1)
    tap = lane % 128
    ab, c = tap // 3, tap % 3
    source = ab * step + c * inner + lane // 128
    return jnp.where((row == source) & (tap < 27), 1.0, 0.0).astype(jnp.bfloat16)


def whole_kernel(
    counts, scale, fea_far, cot_far, w_in_far, w_out_far, w_in9, w_mid9, w_lift_far,
    out, g_input, g_fine_in, g_in, g_mid, g_lift, g_fine_out,
    one, two, got_one, got_two, pack_one, pack_two, sends_one, recvs_one, sends_two, recvs_two,
    tmp, ws, near_rim, rim_sums, total_ref, mine, full, mid_back, in_back, weight_sems,
    w9, wm9, gather_local, gather_sems,
    grown, grown_rim, pad_in, pad_mid, pad_smid, pad_sin, table, thirds,
    jd, dz_edges, sums, parts, landed, sum_local, sum_sems,
    fea, cot, w_in, w_out, w_lift, ready,
    own_cells, share_a, share_b, land_a, land_b, share_locals, a_sems, b_sems,
):
    nx, ny, nz = counts
    total = nx * ny * nz
    gx, gy, gz = (lax.axis_index(axis) for axis in AXES)
    me = (gx * ny + gy) * nz + gz
    f32, bf16 = jnp.float32, jnp.bfloat16
    pairs = [(fea_far, fea), (cot_far, cot), (w_in_far, w_in), (w_out_far, w_out)]
    pairs += [(w_in9, w9), (w_mid9, wm9), (w_lift_far, w_lift)]
    fetches = [
        pltpu.make_async_copy(source, target, weight_sems.at[n])
        for n, (source, target) in enumerate(pairs)
    ]
    for fetch in fetches:
        fetch.start()
    clear_rim(one, got_one)
    barrier = pltpu.get_barrier_semaphore()

    def tell(semaphore):
        told = 0
        for side in SIDES:
            peer, real = there(counts, side, 1)
            told = told + jnp.where(real, 1, 0)

            @pl.when(real)
            def _():
                pl.semaphore_signal(semaphore, inc=1, device_id=peer, device_id_type=MESH)

        return told

    told = tell(barrier)
    clear_rim(two, got_two)
    fetches[0].wait()
    fetches[1].wait()
    group = jnp.zeros((32, 128), f32)
    for x in range(4):
        tmp[0] = fea[:, x].astype(f32).reshape(128, 128)
        tmp[1] = cot[:, x].astype(f32).reshape(128, 128)
        for y in range(4):
            values = [tmp[f, pl.ds(y, 32, stride=4), :] for f in range(2)]
            one[x + 1, y + 1] = jnp.concatenate(values).astype(bf16)
            group = edges(values, x, y, group)
    pack_one[...] = group.astype(bf16)
    fetches[2].wait()
    fetches[3].wait()
    ws[0], ws[1], ws[2], ws[3] = ahead(w_in), back(w_out), ahead(w_out), back(w_in)
    pl.semaphore_wait(barrier, told)
    first = (counts, one, pack_one, got_one, sends_one, recvs_one)
    swap_start(*first)
    swap_finish(*first)
    tell(ready)

    for f in range(2):
        window = column_window(columns(got_one, f))
        if f == 0:
            near_rim[0] = window
        rim_sums[f] = rim_of(ws[f], window)
    total_ref[...] = jnp.zeros_like(total_ref)
    pack_two[...] = jnp.zeros_like(pack_two)

    def fine(x, carry):
        z = settle(dot(ws[0], near(one, x, slice(0, 32))), rim_sums[0], x)
        d = settle(dot(ws[1], near(one, x, slice(32, 64))), rim_sums[1], x)
        group = pack_two[...].astype(f32)
        acts = jnp.zeros((32, 128), f32)
        for y in range(4):
            two[x + 1, y + 1] = jnp.concatenate([z[y], d[y]]).astype(bf16)
            group = edges([z[y], d[y]], x, y, group)
            acts = acts + silu_parts(z[y])[0]
        pack_two[...] = group.astype(bf16)
        total_ref[...] += jnp.concatenate([acts, d[0] + d[1] + d[2] + d[3]])
        return carry

    for x in range(4):
        fine(x, 0)
    row = lax.broadcasted_iota(jnp.int32, (32, 128), 0)
    pick_cell = jnp.where(lanes_of(32) // 4 == row, 1.0, 0.0)
    means = dot_over(pick_cell, total_ref[...], (1, 1), lax.Precision.HIGHEST)
    both = jnp.concatenate([means[:, :32] * (1.0 / 64.0), means[:, 32:]], axis=1)
    mine[...] = jnp.concatenate([both[:16], both[16:]], axis=1).astype(bf16)

    lines = [
        [at] + [lax.rem(at + k, count) for k in range(1, count)]
        for at, count in zip((gx, gy, gz), counts)
    ]

    def send_all(source, target, sems):
        for x in reversed(range(nx)):
            for y in reversed(range(ny)):
                for z in reversed(range(nz)):
                    if x + y + z > 0:
                        peer = (lines[0][x], lines[1][y], lines[2][z])
                        pltpu.make_async_remote_copy(
                            src_ref=source(peer[0], peer[1] * nz + peer[2]),
                            dst_ref=target.at[me],
                            send_sem=sems.at[0],
                            recv_sem=sems.at[1],
                            device_id=peer,
                            device_id_type=MESH,
                        ).start()

    def wait_all(target, sems):
        everyone_else = target.at[pl.ds(0, total - 1)]
        for n in range(2):
            pltpu.make_async_copy(everyone_else, everyone_else, sems.at[n]).wait()

    pl.semaphore_wait(ready, told)
    send_all(lambda x, o: mine, full, gather_sems)
    own = pltpu.make_async_copy(mine, full.at[me], gather_local)
    own.start()
    second = (counts, two, pack_two, got_two, sends_two, recvs_two)
    swap_start(*second)

    for fetch in fetches[4:]:
        fetch.wait()
    wide, narrow = w9.shape[2], in_back.shape[2]

    def turn(ab, carry):
        for c in range(3):
            rows = slice(c * wide, c * wide + wide)
            mid_back[ab, rows, :] = wm9[8 - ab, (2 - c) * wide : (3 - c) * wide, :].T
            in_back[ab, rows, :] = w9[8 - ab, (2 - c) * narrow : (3 - c) * narrow, :].T
        return carry

    lax.fori_loop(0, 9, turn, 0)
    for pad in (pad_in, pad_mid, pad_smid, pad_sin):
        pad[...] = jnp.zeros_like(pad)
    own.wait()
    wait_all(full, gather_sems)

    span = 48
    cells = nx * ny * span

    def pick(size, pieces, index):
        each = size // pieces
        row = lax.broadcasted_iota(jnp.int32, (size, each), 0)
        column = lax.broadcasted_iota(jnp.int32, (size, each), 1)
        return jnp.where(row == index * each + column, 1.0, 0.0).astype(bf16)

    at_o = gy * nz + gz

    def fill(pad, value):
        rows, size = value.shape[0], pad.shape[2]
        at = lax.broadcasted_iota(jnp.int32, value.shape, 0) % size
        low = jnp.where(at == 0, 0.0, pltpu.roll(value, 1, 0))
        high = jnp.where(at == size - 1, 0.0, pltpu.roll(value, rows - 1, 0))
        wide = jnp.concatenate([low, value, high], axis=1).astype(bf16)
        pad[1 : nx + 1, 1 : ny + 1] = wide.reshape(nx, ny, size, wide.shape[1])

    def window(pad, ab):
        a, b = ab // 3, ab % 3
        return pad[a : a + nx, b : b + ny].reshape(nx * ny * pad.shape[2], pad.shape[3])

    def conv(pad, weight):
        result = dot(window(pad, 0), weight[0])
        for ab in range(1, 9):
            result = result + dot(window(pad, ab), weight[ab])
        return result

    def slope(v):
        sigma = jax.nn.sigmoid(v)
        return sigma * (1.0 + v * (1.0 - sigma))

    before, after = jnp.maximum(gz - 1, 0), jnp.minimum(gz + 1, nz - 1)
    pieces = []
    for k in range(nx * ny):
        here = full[k * nz + gz].astype(f32)
        pieces += [full[k * nz + before].astype(f32)[8:, 64:], here[:, :64], here[:, 64:]]
        pieces += [full[k * nz + after].astype(f32)[:8, :64]]
    at_z = lax.broadcasted_iota(jnp.int32, (cells, 128), 0) % span + gz * 32 - 8
    keep = jnp.where((at_z >= 0) & (at_z < nz * 32), 1.0, 0.0)
    both = jnp.concatenate(pieces) * keep[:, :64]
    fill(pad_in, both[:, :32])
    z_second = conv(pad_in, w9)
    act_second = jax.nn.silu(z_second) * keep
    fill(pad_mid, act_second)
    z_third = conv(pad_mid, wm9)
    act_third = jax.nn.silu(z_third)
    lifted = dot(act_third.astype(bf16), w_lift[...].T)
    dz_third = dot(both[:, 32:].astype(bf16), w_lift[...]) * slope(z_third) * keep
    fill(pad_mid, dz_third)
    dz_second = conv(pad_mid, mid_back) * slope(z_second) * keep
    fill(pad_mid, dz_second)
    d_pool = conv(pad_mid, in_back)
    table[...] = (
        jnp.concatenate([lifted, d_pool * (1.0 / 64.0)], axis=1)
        .astype(bf16)
        .reshape(nx, ny, span, 64)
    )
    for n, value in enumerate([act_second, act_third, dz_third, dz_second]):
        own_cells[:, :, n * 128 : n * 128 + 128] = value.reshape(nx * ny, span, 128)
    mine_now = own_cells[gx * ny + gy, 8:40, :]
    wx, wo = 128 // nx, 128 // (ny * nz)
    for i in range(nx):
        block = jnp.concatenate(
            [mine_now[:, n * 128 + i * wx : n * 128 + i * wx + wx] for n in (0, 1)], axis=1
        )
        share_a[i] = jnp.concatenate([block[:16], block[16:]], axis=1).astype(bf16)
    for i in range(ny * nz):
        block = jnp.concatenate(
            [mine_now[:, n * 128 + i * wo : n * 128 + i * wo + wo] for n in (2, 3)], axis=1
        )
        share_b[i] = jnp.concatenate(
            [block[8 * q : 8 * q + 8] for q in range(4)], axis=1
        ).astype(bf16)

    row = lax.broadcasted_iota(jnp.int32, (span, 128), 0)
    lane = lanes_of(span)
    grow = jnp.where(row == lane // 4 + 8, 1.0, 0.0).astype(bf16)
    past = 8 + jnp.where(lane % 2 == 1, -1, 32)
    at_x, at_y = lane // 12, lane // 2 % 6
    rim = jnp.zeros((64, 128), f32)
    for i in range(3):
        for j in range(3):
            x = jnp.clip(gx + i - 1, 0, nx - 1)
            y = jnp.clip(gy + j - 1, 0, ny - 1)
            grown[i, j] = dot_over(table[x, y], grow, (0, 0))
            mine_too = ((at_x + 3) // 4 == i) & ((at_y + 3) // 4 == j) & (lane < 72)
            far = jnp.where((row == past) & mine_too, 1.0, 0.0).astype(bf16)
            rim = rim + dot_over(table[x, y], far, (0, 0))
    send_all(lambda x, o: share_a.at[x], land_a, a_sems)
    send_all(lambda x, o: share_b.at[o], land_b, b_sems)
    owns = [
        pltpu.make_async_copy(share_a.at[gx], land_a.at[me], share_locals.at[0]),
        pltpu.make_async_copy(share_b.at[at_o], land_b.at[me], share_locals.at[1]),
    ]
    for copy in owns:
        copy.start()
    swap_finish(*second)

    lane = lanes_of(32)
    at_x, at_y = gx * 4 + lane // 12 - 1, gy * 4 + lane // 2 % 6 - 1
    real = (at_x >= 0) & (at_x < nx * 4) & (at_y >= 0) & (at_y < ny * 4) & (lane < 72)
    reach = gz + jnp.where(lane % 2 == 1, -1, 1)
    real = real & (reach >= 0) & (reach < nz)
    act, bend = silu_parts(columns(got_two, 0))
    near_rim[1] = column_window(jnp.where(real, act + rim[:32], 0.0))
    near_rim[2] = column_window(jnp.where(real, (columns(got_two, 1) + rim[32:]) * bend, 0.0))
    rim_sums[0] = rim_of(ws[2], near_rim[1])
    rim_sums[1] = rim_of(ws[3], near_rim[2])
    dz_edges[...] = jnp.zeros_like(dz_edges)

    def join(x, carry):
        group = dz_edges[...]
        for y in range(6):
            at_x, at_y = gx * 4 + x - 1, gy * 4 + y - 1
            real = (at_x >= 0) & (at_x < nx * 4) & (at_y >= 0) & (at_y < ny * 4)
            keep = jnp.where(real, 1.0, 0.0)
            up = grown[(x + 3) // 4, (y + 3) // 4]
            both = two[x, y].astype(f32)
            act, bend = silu_parts(both[:32])
            joined = (act + up[:32]) * keep
            dz = (both[32:] + up[32:]) * bend * keep
            jd[x, y] = jnp.concatenate([joined, dz]).astype(bf16)
            if 1 <= y <= 4:
                here = jnp.where((x >= 1) & (x <= 4), x * 6 + y, -1)
                turned = pltpu.roll(dz, (12 * x + 2 * y + 1) % 128, 1)
                group = jnp.where(lanes_of(32) // 2 == here, turned, group)
        dz_edges[...] = group
        return carry

    for x in range(6):
        join(x, 0)
    ends = pltpu.roll(pack_one[...].astype(f32), 64, 1)
    ends = jnp.where(lanes_of(32) < 64, ends, 0.0)
    sums[0] = dot_over(near_rim[1], thrice_rim(ends), (1, 1))
    sums[1] = dot_over(near_rim[0], thrice_rim(dz_edges[...]), (1, 1))

    def last(x, carry):
        joined = near(jd, x, slice(0, 32))
        rows = settle(dot(ws[2], joined), rim_sums[0], x)
        for y in range(4):
            tmp[0, pl.ds(y, 32, stride=4), :] = rows[y]
        out[:, x] = tmp[0].reshape(32, 4, 128).astype(bf16)
        given = [one[x + 1, y + 1, 32:64, :] for y in range(4)]
        sums[0] += dot_over(joined, thrice(jnp.concatenate(given, axis=1)), (1, 1))
        rows = settle(dot(ws[3], near(jd, x, slice(32, 64))), rim_sums[1], x)
        for y in range(4):
            tmp[1, pl.ds(y, 32, stride=4), :] = rows[y]
        g_input[:, x] = tmp[1].reshape(32, 4, 128).astype(bf16)
        given = [jd[x + 1, y + 1, 32:64, :] for y in range(4)]
        sums[1] += dot_over(
            near(one, x, slice(0, 32)), thrice(jnp.concatenate(given, axis=1)), (1, 1)
        )
        return carry

    lax.fori_loop(0, 4, last, 0)
    ci, co = 32 // nx, 32 // (ny * nz)
    for f in range(2):
        value = sums[f].reshape(9, nx, ci, 96)
        for i in range(nx):
            turned = value[:, i].reshape(9 * ci, 96).T
            block = jnp.concatenate([turned[:32], turned[32:64], turned[64:]], axis=1)
            for j in range(ny * nz):
                parts[i * ny * nz + j, f * co : f * co + co, :] = block[
                    j * co : j * co + co
                ].astype(bf16)
    send_all(lambda x, o: parts.at[x * (ny * nz) + o], landed, sum_sems)
    own = pltpu.make_async_copy(parts.at[me], landed.at[me], sum_local)
    own.start()

    for copy in owns:
        copy.wait()
    wait_all(land_a, a_sems)
    wait_all(land_b, b_sems)
    pieces, firsts, seconds = [], [], []
    for k in range(total):
        block = full[k]
        pieces += [block[:, :64], block[:, 64:]]
        block = land_a[k].astype(f32)
        firsts += [block[:, :64], block[:, 64:]]
        block = land_b[k].astype(f32)
        seconds += [block[:, 32 * q : 32 * q + 32] for q in range(4)]
    both = jnp.concatenate(pieces)
    pooled, d_lift = both[:, :32], both[:, 32:]
    acts = jnp.concatenate(firsts)
    fill(pad_smid, acts[:, :32])
    fill(pad_sin, dot(pooled, pick(32, nx, gx)))
    turned = jnp.concatenate(seconds).T.astype(bf16)
    thirds[0], thirds[1] = turned[:16], turned[16:]
    lift_o = dot(d_lift, pick(32, ny * nz, at_o)).T.astype(bf16)
    g_lift[...] = dot(lift_o, acts[:, 32:].astype(bf16)) * scale
    taken = []
    for ab in range(9):
        grad = dot(thirds[0], window(pad_smid, ab)) * scale
        share = grad.shape[1] // 3
        for c in range(3):
            g_mid[3 * ab + c] = grad[:, c * share : c * share + share]
        taken.append(dot(thirds[1], window(pad_sin, ab)) * scale)
    chosen = spread(jnp.concatenate(taken, axis=1), chooser_of(ci, 3 * ci, ci))
    for i in range(ci):
        g_in[i] = chosen[:, i * 128 : i * 128 + 27]
    chooser = chooser_of(ci, ci, 9 * ci)
    own.wait()
    wait_all(landed, sum_sems)
    chosen = spread(landed[...].astype(f32).sum(0) * scale, chooser)
    for i in range(ci):
        g_fine_out[i] = chosen[:co, i * 128 : i * 128 + 27]
        g_fine_in[i] = chosen[co:, i * 128 : i * 128 + 27]


def hand_over(*refs):
    *refs, sems = refs
    half = len(refs) // 2
    copies = [
        pltpu.make_async_copy(source, target, sems.at[n])
        for n, (source, target) in enumerate(zip(refs[:half], refs[half:]))
    ]
    for copy in copies:
        copy.start()
    for copy in copies:
        copy.wait()


def shards(features, cotangent, w_fine_in, w_coarse_in, w_coarse_mid, w_lift, w_fine_out):
    counts = tuple(lax.axis_size(axis) for axis in AXES)
    nx, ny, nz = counts
    total = nx * ny * nz
    chans, depth, height, length = features.shape
    wide = w_lift.shape[0]
    scale = 1.0 / math.sqrt(total * depth * height * length)
    f32, bf16 = jnp.float32, jnp.bfloat16
    shape = jax.ShapeDtypeStruct
    co, cw = wide // (ny * nz), wide // nx
    ci, fo = chans // nx, chans // (ny * nz)
    pads = [3 * chans, 3 * wide, 3 * cw, 3 * ci]
    block = (2 * fo, 27 * ci)
    rows = pltpu.VMEM((6, 6, 2 * chans, 128), bf16)
    got = pltpu.VMEM((18, chans, 128), bf16)
    packed = pltpu.VMEM((chans, 128), bf16)
    swaps = pltpu.SemaphoreType.DMA((len(SIDES),))
    one, both_ways = pltpu.SemaphoreType.DMA, pltpu.SemaphoreType.DMA((2,))
    anywhere = pl.BlockSpec(memory_space=pl.ANY)
    results = pl.pallas_call(
        lambda *refs: whole_kernel(counts, scale, *refs),
        out_shape=(
            shape(features.shape, bf16),
            shape(features.shape, bf16),
            shape((ci, fo, 27), f32),
            shape((ci, co, 27), f32),
            shape((27, co, cw), f32),
            shape((fo, cw), f32),
            shape((ci, fo, 27), f32),
        ),
        in_specs=[pl.BlockSpec(memory_space=pltpu.HBM)] * 7,
        out_specs=vmem(7),
        scratch_shapes=[
            rows, rows, got, got, packed, packed, swaps, swaps, swaps, swaps,
            pltpu.VMEM((2, 128, 128), f32),
            pltpu.VMEM((4, 3 * chans, 9 * chans), bf16),
            pltpu.VMEM((3, 9 * chans, 128), bf16),
            pltpu.VMEM((2, chans, 128), f32),
            pltpu.VMEM((2 * chans, 128), f32),
            pltpu.VMEM((16, 128), bf16),
            pltpu.VMEM((total, 16, 128), bf16),
            pltpu.VMEM((9, 3 * wide, wide), bf16),
            pltpu.VMEM((9, 3 * wide, chans), bf16),
            pltpu.SemaphoreType.DMA((7,)),
            pltpu.VMEM((9, 3 * chans, wide), bf16),
            pltpu.VMEM((9, 3 * wide, wide), bf16),
            one, both_ways,
            pltpu.VMEM((3, 3, 2 * chans, 128), f32),
            pltpu.VMEM((2 * chans, 128), f32),
        ]
        + [
            pltpu.VMEM((nx + 2, ny + 2, z, k), bf16)
            for z, k in zip((48, 48, 128, 128), pads)
        ]
        + [
            pltpu.VMEM((nx, ny, 48, 2 * chans), bf16),
            pltpu.VMEM((2, co, nx * ny * 128), bf16),
            rows,
            pltpu.VMEM((chans, 128), f32),
            pltpu.VMEM((2, 9 * chans, 3 * chans), f32),
            pltpu.VMEM((total,) + block, bf16),
            pltpu.VMEM((total,) + block, bf16),
            one, both_ways,
            pltpu.VMEM(features.shape, bf16),
            pltpu.VMEM(features.shape, bf16),
            pltpu.VMEM(w_fine_in.shape, bf16),
            pltpu.VMEM(w_fine_in.shape, bf16),
            pltpu.VMEM((chans, wide), bf16),
            pltpu.SemaphoreType.REGULAR,
            pltpu.VMEM((nx * ny, 48, 4 * wide), f32),
            pltpu.VMEM((nx, 16, 128), bf16),
            pltpu.VMEM((ny * nz, 8, 128), bf16),
            pltpu.VMEM((total, 16, 128), bf16),
            pltpu.VMEM((total, 8, 128), bf16),
            pltpu.SemaphoreType.DMA((2,)),
            both_ways, both_ways,
        ],
        compiler_params=pltpu.CompilerParams(
            collective_id=0, has_side_effects=True, vmem_limit_bytes=ROOMY
        ),
        name="whole",
    )(
        *[
            pltpu.with_memory_space_constraint(value, pltpu.HBM)
            for value in (
                features, cotangent, w_fine_in, w_fine_out,
                w_coarse_in.reshape(9, 3 * chans, wide),
                w_coarse_mid.reshape(9, 3 * wide, wide), w_lift.T,
            )
        ]
    )
    output, grad_input, g_fine_in, g_in, g_mid, g_lift, g_fine_out = pl.pallas_call(
        hand_over,
        out_shape=[shape(value.shape, value.dtype) for value in results],
        in_specs=vmem(7),
        out_specs=[anywhere] * 7,
        scratch_shapes=[pltpu.SemaphoreType.DMA((7,))],
        compiler_params=pltpu.CompilerParams(vmem_limit_bytes=HANDED),
        name="hand_over",
    )(*results)
    return (
        output,
        grad_input,
        g_fine_in.transpose(2, 0, 1),
        g_in.transpose(2, 0, 1),
        g_mid.transpose(0, 2, 1),
        g_lift.T,
        g_fine_out.transpose(2, 0, 1),
    )


def choose(features, *rest):
    nx, ny, nz = (lax.axis_size(axis) for axis in AXES)
    total = nx * ny * nz
    wide = rest[4].shape[0]
    fits = features.shape == (32, 4, 4, 128) and nz == 4 and total <= DIRECT
    fits = fits and 32 % (ny * nz) == 0 and 32 % nx == 0 and 32 // nx == 8 and ny * nz == 8 and wide == 128
    return (shards if fits else shards_layered)(features, *rest)


def solution(mesh):
    whole = P(None, "gx", "gy", "gz")
    split = P(None, "gx", ("gy", "gz"))
    return jax.shard_map(
        choose,
        mesh=mesh,
        in_specs=(whole, whole, P(), P(), P(), P(), P()),
        out_specs=(whole, whole, split, split, split, P("gx", ("gy", "gz")), split),
        check_vma=False,
    )
```
